32 devices in a mesh: fsdp: 8 (over z, core), tp: 4 (over y, x).
Axes of the slice: x: 2, y: 2, z: 4, core: 2. Of those that a mesh axis runs over, the one named last changes fastest.
Arguments:
- block_input: bfloat16 [8, 1024, 2560], P('fsdp', 'tp'), may hold values from -6 to 6
- seq_lengths: int32 [8], replicated, may hold values from 128 to 1024, as said below
- dealt_order: int32 [8], replicated, may hold values from 0 to 7, as said below
- out_cotangent: bfloat16 [8, 1024, 2560], P('fsdp', 'tp'), may hold values from -6 to 6
- attn_gain: float32 [2560], P(('fsdp', 'tp')), may hold values from 0.1 to 1.9
- query_down: float32 [2560, 768], P(('fsdp', 'tp')), may hold values from -0.125 to 0.125
- query_gain: float32 [768], P(('fsdp', 'tp')), may hold values from 0.1 to 1.9
- latent_down: float32 [2560, 288], P(('fsdp', 'tp')), may hold values from -0.125 to 0.125
- latent_gain: float32 [256], P(('fsdp', 'tp')), may hold values from 0.1 to 1.9
- query_up: float32 [768, 3840], P('fsdp', 'tp'), may hold values from -0.21875 to 0.21875
- latent_up: float32 [256, 5120], P('fsdp', 'tp'), may hold values from -0.375 to 0.375
- output_matrix: float32 [2560, 2560], P('fsdp', 'tp'), may hold values from -6 to 6
- mlp_gain: float32 [2560], P(('fsdp', 'tp')), may hold values from 0.1 to 1.9
- gate_weight: float32 [2560, 6400], P('fsdp', 'tp'), may hold values from -0.125 to 0.125
- up_weight: float32 [2560, 6400], P('fsdp', 'tp'), may hold values from -0.125 to 0.125
- down_matrix: float32 [2560, 6400], P('fsdp', 'tp'), may hold values from -0.625 to 0.625
Outputs:
- block_output: bfloat16 [8, 1024, 2560], P('fsdp', 'tp')
- input_grad: bfloat16 [8, 1024, 2560], P('fsdp', 'tp')
- attn_gain_grad: float32 [2560], P(('fsdp', 'tp'))
- query_down_grad: float32 [2560, 768], P(('fsdp', 'tp'))
- query_gain_grad: float32 [768], P(('fsdp', 'tp'))
- latent_down_grad: float32 [2560, 288], P(('fsdp', 'tp'))
- latent_gain_grad: float32 [256], P(('fsdp', 'tp'))
- query_up_grad: float32 [768, 3840], P('fsdp', 'tp')
- latent_up_grad: float32 [256, 5120], P('fsdp', 'tp')
- out_weight_grad: float32 [2560, 2560], P('fsdp', 'tp')
- mlp_gain_grad: float32 [2560], P(('fsdp', 'tp'))
- gate_weight_grad: float32 [2560, 6400], P('fsdp', 'tp')
- up_weight_grad: float32 [2560, 6400], P('fsdp', 'tp')
- down_weight_grad: float32 [2560, 6400], P('fsdp', 'tp')
The draws below stay inside these ranges and needn't reach their ends.
Inputs may be any that keep to these rules, and one draw needn't show every extreme that they name: seq_lengths counts the valid leading tokens of each sequence; some sequence has exactly 1024 and some exactly 128. dealt_order is a permutation of the sequences; slot p belongs to index p // 1 of fsdp.
All inputs are finite; a program needn't handle non-finite values.
Results may differ from the reference program's by a relative error of at most 0.025.
Values may be sent and summed in bfloat16 or wider, within the bound.
A program may use at most 256 MiB of HBM per device.

```python
import math
import jax
import jax.numpy as jnp
from jax import lax

D = 2560
QR = 768
KR = 256
H = 40
NOPE = 64
ROPE = 32
VD = 64
FF = 6400
QKD = 96
LEN = 1024
SEQ_DEV = 1
SEQS = 8


def deal_sequences(key):
    count = SEQS
    groups = SEQS // SEQ_DEV
    lengths = jax.random.randint(jax.random.fold_in(key, 11), (count,), LEN // 8, LEN + 1, dtype=jnp.int32)
    chosen = jax.random.permutation(jax.random.fold_in(key, 12), count)
    lengths = lengths.at[chosen[0]].set(LEN).at[chosen[1]].set(LEN // 8)
    score = lengths * count + jnp.arange(count, dtype=jnp.int32)
    order = jnp.argsort(-score).astype(jnp.int32)
    rank = jnp.arange(count, dtype=jnp.int32)
    round_index = rank // groups
    within = rank % groups
    target = jnp.where(round_index % 2 == 0, within, groups - 1 - within)
    shuffle = jax.random.permutation(jax.random.fold_in(key, 13), groups).astype(jnp.int32)
    slot = jnp.take(shuffle, target) * SEQ_DEV + round_index
    placed = jnp.zeros((count,), jnp.int32).at[slot].set(order)
    return (lengths, placed)


def draw_seq_lengths(key, part):
    return deal_sequences(key)[0]


def draw_dealt_order(key, part):
    return deal_sequences(key)[1]


def shard_levels(stream_key, shape, split, least, top_value):
    loudness = 1.0
    for position, blocks in split:
        heights = jax.random.uniform(jax.random.fold_in(jax.random.fold_in(stream_key, 6), position), (blocks,), jnp.float32, least / len(split), top_value / len(split))
        loudness = loudness * jnp.repeat(jnp.exp(heights), shape[position] // blocks).reshape((-1,) + (1,) * (len(shape) - 1 - position))
    return loudness


def normal_values(own_key, dims, scale, bound, split=(), held_as=jnp.bfloat16):
    values = scale * jax.random.normal(own_key, dims, jnp.float32)
    if split:
        values = values * shard_levels(own_key, dims, split, -0.22, 0.18)
    return jnp.clip(values, -bound, bound).astype(held_as)


def setup_inputs(seed: int = 0) -> dict:
    splits = jax.random.split(jax.random.key(seed), 17)
    return {
        "block_input": normal_values(splits[0], (SEQS, LEN, D), 1.0, 6.0, ((0, 8), (1, 4))),
        "seq_lengths": draw_seq_lengths(jax.random.fold_in(splits[16], 71), 0),
        "dealt_order": draw_dealt_order(jax.random.fold_in(splits[16], 71), 0),
        "out_cotangent": normal_values(splits[3], (SEQS, LEN, D), 1.0, 6.0, ((0, 8), (1, 4))),
        "attn_gain": jnp.clip(1.0 + 0.18 * jax.random.normal(splits[4], (D,), jnp.float32), 0.1, 1.9),
        "query_down": normal_values(splits[5], (D, QR), D ** -0.5, 0.125, ((0, 32),), jnp.float32),
        "query_gain": jnp.clip(1.0 + 0.18 * jax.random.normal(splits[6], (QR,), jnp.float32), 0.1, 1.9),
        "latent_down": normal_values(splits[7], (D, KR + ROPE), D ** -0.5, 0.125, ((0, 32),), jnp.float32),
        "latent_gain": jnp.clip(1.0 + 0.18 * jax.random.normal(splits[8], (KR,), jnp.float32), 0.1, 1.9),
        "query_up": normal_values(splits[9], (QR, H * QKD), QR ** -0.5, 0.21875, ((0, 8), (1, 4)), jnp.float32),
        "latent_up": normal_values(splits[10], (KR, H * (NOPE + VD)), KR ** -0.5, 0.375, ((0, 8), (1, 4)), jnp.float32),
        "output_matrix": normal_values(splits[11], (D, H * VD), 1 ** -0.5, 6.0, ((0, 8), (1, 4)), jnp.float32),
        "mlp_gain": jnp.clip(1.0 + 0.18 * jax.random.normal(splits[12], (D,), jnp.float32), 0.1, 1.9),
        "gate_weight": normal_values(splits[13], (D, FF), D ** -0.5, 0.125, ((0, 8), (1, 4)), jnp.float32),
        "up_weight": normal_values(splits[14], (D, FF), D ** -0.5, 0.125, ((0, 8), (1, 4)), jnp.float32),
        "down_matrix": normal_values(splits[15], (D, FF), (FF // 64) ** -0.5, 0.625, ((0, 8), (1, 4)), jnp.float32),
    }


EPSILON = 1e-05
RESIDUAL_SCALE = 1.4 / math.sqrt(62.0)
ROTARY_BASE = 10000.0
MASKED = -1e+30
PRECISION_TOP = lax.Precision.HIGHEST

@jax.custom_vjp
def low(v):
    return lax.optimization_barrier(v.astype(jnp.bfloat16)).astype(jnp.float32)

@jax.custom_vjp
def lowered_backward(v):
    return v

def low_keep(v):
    return (low(v), None)

def low_pass(kept, grad):
    return (grad,)

def back_keep(v):
    return (v, None)

def back_low(kept, grad):
    return (low(grad),)
low.defvjp(low_keep, low_pass)
lowered_backward.defvjp(back_keep, back_low)

def normalize(values, gain):
    return values * lax.rsqrt(lax.optimization_barrier(jnp.mean(values * values, axis=-1, keepdims=True)) + EPSILON) * gain

def product(left, right):
    return jnp.dot(left, right, precision=PRECISION_TOP, preferred_element_type=jnp.float32)

def rotary_tables(positions):
    halfway = ROPE // 2
    spacing = jnp.arange(halfway, dtype=jnp.float32) * (2.0 / ROPE)
    freqs = jnp.power(jnp.float32(ROTARY_BASE), -spacing)
    angle = positions.astype(jnp.float32)[:, None] * freqs[None, :]
    cosine = jnp.concatenate([jnp.cos(angle), jnp.cos(angle)], axis=-1)
    sine = jnp.concatenate([jnp.sin(angle), jnp.sin(angle)], axis=-1)
    return (cosine, sine)

def rotate(values, cosine, sine):
    halfway = values.shape[-1] // 2
    turned = jnp.concatenate([-values[..., halfway:], values[..., :halfway]], axis=-1)
    return values * cosine + turned * sine

def attend(item):
    query_seq, keys, values, seq_len = item
    block = min(512, LEN)
    count = LEN // block

    def one_block(start):
        query_block = lax.dynamic_slice_in_dim(query_seq, start, block, 0)
        scores = lowered_backward(jnp.einsum('qhd,khd->hqk', query_block, keys, precision=PRECISION_TOP) * (1.0 / math.sqrt(QKD)))
        query_pos = start + jnp.arange(block, dtype=jnp.int32)
        key_pos = jnp.arange(LEN, dtype=jnp.int32)
        live = (key_pos[None, :] <= query_pos[:, None]) & (key_pos[None, :] < seq_len)
        scores = jnp.where(live[None, :, :], scores, MASKED)
        top = lax.optimization_barrier(jnp.max(scores, axis=-1, keepdims=True))
        expo = jnp.exp(scores - top)
        probs = expo / lax.optimization_barrier(jnp.sum(expo, axis=-1, keepdims=True))
        mixed_hidden = jnp.einsum('hqk,khd->qhd', low(probs), values, precision=PRECISION_TOP)
        return low(lowered_backward(mixed_hidden))
    starts = jnp.arange(count, dtype=jnp.int32) * block
    outs = lax.map(jax.checkpoint(one_block), starts)
    return outs.reshape(LEN, keys.shape[1], values.shape[-1])

def layer(block_vals, lens, weights):
    attn_gain, query_down, query_gain, latent_down, latent_gain, query_up, latent_up, output_matrix, mlp_gain, gate_weight, up_weight, down_matrix = [low(weight) for weight in weights]
    count = block_vals.shape[0]
    positions = jnp.arange(LEN, dtype=jnp.int32)
    cosine, sine = rotary_tables(positions)
    valid = (positions[None, :] < lens[:, None]).astype(jnp.float32)[:, :, None]
    normed = low(normalize(block_vals, attn_gain))
    query_latent = lowered_backward(product(normed, query_down))
    query_normed = low(normalize(query_latent, query_gain))
    joint = lowered_backward(product(normed, latent_down))
    compressed = low(normalize(joint[..., :KR], latent_gain))
    rotary_key = low(rotate(joint[..., KR:], cosine, sine))
    queries = lowered_backward(product(query_normed, query_up)).reshape(count, LEN, H, QKD)
    queries = low(jnp.concatenate([queries[..., :NOPE], rotate(queries[..., NOPE:], cosine[:, None, :], sine[:, None, :])], axis=-1))
    key_value = low(lowered_backward(product(compressed, latent_up))).reshape(count, LEN, H, NOPE + VD)
    keys = jnp.concatenate([key_value[..., :NOPE], jnp.broadcast_to(rotary_key[:, :, None, :], (count, LEN, H, ROPE))], axis=-1)
    values = key_value[..., NOPE:]
    mixed_hidden = lax.map(attend, (queries, keys, values, lens)).reshape(count, LEN, H * VD)
    attention_branch = lowered_backward(jnp.einsum('gno,ho->gnh', mixed_hidden, output_matrix, precision=PRECISION_TOP))
    after_attn = block_vals + RESIDUAL_SCALE * attention_branch
    mlp_normed = low(normalize(after_attn, mlp_gain))
    gate = lowered_backward(product(mlp_normed, gate_weight))
    up_vals = lowered_backward(product(mlp_normed, up_weight))
    activated_hidden = low(gate * jax.nn.sigmoid(gate) * up_vals)
    feedforward_branch = lowered_backward(jnp.einsum('cbt,pt->cbp', activated_hidden, down_matrix, precision=PRECISION_TOP))
    return valid * (after_attn + RESIDUAL_SCALE * feedforward_branch)

def reference(block_input, seq_lengths, dealt_order, out_cotangent, attn_gain, query_down, query_gain, latent_down, latent_gain, query_up, latent_up, output_matrix, mlp_gain, gate_weight, up_weight, down_matrix):
    weights = (attn_gain, query_down, query_gain, latent_down, latent_gain, query_up, latent_up, output_matrix, mlp_gain, gate_weight, up_weight, down_matrix)
    dealt = jnp.take(block_input, dealt_order, axis=0).astype(jnp.float32)
    lens = jnp.take(seq_lengths, dealt_order, axis=0)
    cotangent = out_cotangent.astype(jnp.float32)
    group_size = math.gcd(SEQS, max(1, 4096 // LEN))
    groups = SEQS // group_size
    dealt = dealt.reshape(groups, group_size, LEN, D)
    lens = lens.reshape(groups, group_size)
    cotangent = cotangent.reshape(groups, group_size, LEN, D)

    def one_group(totals, item):
        group_vals, group_lens, group_cot = item

        def forward(block_vals, *weight_list):
            return layer(block_vals, group_lens, weight_list)
        result, pull = jax.vjp(forward, group_vals, *weights)
        grads = pull(group_cot)
        totals = tuple((total + grad for total, grad in zip(totals, grads[1:])))
        return (totals, (result.astype(jnp.bfloat16), grads[0].astype(jnp.bfloat16)))
    start = tuple((jnp.zeros_like(weight, dtype=jnp.float32) for weight in weights))
    totals, (results, dealt_grads) = lax.scan(one_group, start, (dealt, lens, cotangent))
    block_output = results.reshape(SEQS, LEN, D)
    input_grad = jnp.zeros((SEQS, LEN, D), jnp.bfloat16).at[dealt_order].set(dealt_grads.reshape(SEQS, LEN, D))
    return (block_output, input_grad, totals[0], totals[1], totals[2], totals[3], totals[4], totals[5], totals[6], totals[7], totals[8], totals[9], totals[10], totals[11])
```

```python
import functools
import math

import jax
import jax.numpy as jnp
from jax import lax
from jax.experimental import pallas as pl
from jax.experimental.layout import Layout, with_layout_constraint
from jax.experimental.pallas import tpu as pltpu
from jax.sharding import PartitionSpec as P

KR = 256
NOPE = 64
ROPE = 32
VD = 64
QKD = 96
LANE = 128

EPSILON = 1e-05
RESIDUAL_SCALE = 1.4 / math.sqrt(62.0)
ROTARY_BASE = 10000.0
MASKED = -1e30
SCORE_SCALE = 1.0 / math.sqrt(QKD)

F32 = jnp.float32
LOW = jnp.bfloat16
NT = (((1,), (1,)), ((), ()))
TN = (((0,), (0,)), ((), ()))


def dot(left, right):
    return jnp.dot(left, right, preferred_element_type=F32)


def dot_nt(left, right):
    return lax.dot_general(left, right, NT, preferred_element_type=F32)


def dot_tn(left, right):
    return lax.dot_general(left, right, TN, preferred_element_type=F32)


def normalize(values, gain):
    factor = lax.rsqrt(jnp.mean(values * values, axis=-1, keepdims=True) + EPSILON)
    return (values * factor * gain, factor)


def norm_back(values, factor, gain, grad):
    weighted = grad * gain
    inner = jnp.mean(weighted * values, axis=-1, keepdims=True)
    dvalues = factor * weighted - values * (factor * factor * factor) * inner
    dgain = jnp.sum(grad * values * factor, axis=0)
    return (dvalues, dgain)


def rotary_tables(positions):
    halfway = ROPE // 2
    spacing = jnp.arange(halfway, dtype=F32) * (2.0 / ROPE)
    freqs = jnp.power(jnp.float32(ROTARY_BASE), -spacing)
    angle = positions.astype(F32)[:, None] * freqs[None, :]
    return (jnp.cos(angle), jnp.sin(angle))


def turn_half(values):
    halfway = values.shape[-1] // 2
    return jnp.concatenate([-values[..., halfway:], values[..., :halfway]], axis=-1)


def head_tables(cosine, sine):
    count = cosine.shape[0]
    one = jnp.ones((count, NOPE), F32)
    zero = jnp.zeros((count, NOPE), F32)
    half = jnp.zeros_like(sine)
    rest = jnp.zeros((count, LANE - NOPE - ROPE), F32)
    return (
        jnp.concatenate([one, cosine, cosine, rest], axis=1),
        jnp.concatenate([zero, half, sine, rest], axis=1),
        jnp.concatenate([zero, -sine, half, rest], axis=1),
    )


def attend_kernel(
    blocks, q_ref, kv_ref, rope_ref, bias_ref, cos_ref, lift_ref, drop_ref, rot_ref, mix_ref, lse_ref
):
    size = q_ref.shape[0] // blocks
    low = lax.broadcasted_iota(jnp.int32, (1, LANE), 1) < NOPE
    causal = lax.broadcasted_iota(jnp.int32, (size, size), 1) <= lax.broadcasted_iota(
        jnp.int32, (size, size), 0
    )
    half = ROPE // 2
    for i in range(blocks):
        rows = pl.ds(i * size, size)
        live = pl.ds(0, (i + 1) * size)
        outs = []
        for h in range(2):
            cols = pl.ds(h * LANE, LANE)
            query = q_ref[rows, cols].astype(F32)
            query = (
                query * cos_ref[rows, :]
                + pltpu.roll(query, half, 1) * lift_ref[rows, :]
                + pltpu.roll(query, LANE - half, 1) * drop_ref[rows, :]
            ).astype(LOW)
            rot_ref[rows, cols] = query
            pair = kv_ref[live, cols]
            key = jnp.where(low, pair, rope_ref[live, :])
            value = jnp.where(low, jnp.ones_like(pair), pair)
            scores = dot_nt(query, key) * SCORE_SCALE + bias_ref[:, live]
            edge = jnp.where(causal, scores[:, i * size :], MASKED)
            scores = edge if i == 0 else jnp.concatenate([scores[:, : i * size], edge], axis=1)
            top = jnp.max(scores, axis=1, keepdims=True)
            expo = jnp.exp(scores - top)
            out = dot(expo.astype(LOW), value)
            total = out[:, 0:1]
            lse_ref[rows, pl.ds(h * NOPE, NOPE)] = jnp.broadcast_to(top + jnp.log(total), (size, NOPE))
            outs.append(out / total)
        mix_ref[rows, :] = jnp.where(low, pltpu.roll(outs[0], NOPE, 1), outs[1]).astype(LOW)


def attend(query, pair, rope, bias, tables):
    count = query.shape[0]
    steps = query.shape[1] // (2 * LANE)
    blocks = 4

    def whole(shape):
        return pl.BlockSpec(shape, lambda i: (0, 0))

    wide = pl.BlockSpec((count, 2 * LANE), lambda i: (0, i))
    slim = pl.BlockSpec((count, LANE), lambda i: (0, i))
    table = whole((count, LANE))
    return pl.pallas_call(
        functools.partial(attend_kernel, blocks),
        grid=(steps,),
        in_specs=[wide, wide, table, whole((1, count)), table, table, table],
        out_specs=[wide, slim, slim],
        out_shape=[
            jax.ShapeDtypeStruct(query.shape, LOW),
            jax.ShapeDtypeStruct((count, steps * LANE), LOW),
            jax.ShapeDtypeStruct((count, steps * LANE), F32),
        ],
        cost_estimate=pl.CostEstimate(
            flops=steps * count * count * LANE * 5, bytes_accessed=count * steps * 2400, transcendentals=count * count * steps
        ),
        name="attend",
    )(query, pair, rope, bias, *tables)


def attend_back_kernel(
    blocks,
    q_ref,
    kv_ref,
    rope_ref,
    bias_ref,
    cos_ref,
    lift_ref,
    drop_ref,
    mix_ref,
    grad_ref,
    lse_ref,
    dq_ref,
    dkv_ref,
    drope_ref,
    dkey,
    dval,
):
    size = q_ref.shape[0] // blocks
    low = lax.broadcasted_iota(jnp.int32, (1, LANE), 1) < NOPE
    causal = lax.broadcasted_iota(jnp.int32, (size, size), 1) <= lax.broadcasted_iota(
        jnp.int32, (size, size), 0
    )
    half = ROPE // 2

    @pl.when(pl.program_id(0) == 0)
    def _():
        drope_ref[...] = jnp.zeros_like(drope_ref)

    for h in range(2):
        cols = pl.ds(h * LANE, LANE)
        for i in range(blocks):
            rows = pl.ds(i * size, size)
            past = i * size
            live = pl.ds(0, past + size)
            query = q_ref[rows, cols]
            pair = kv_ref[live, cols]
            key = jnp.where(low, pair, rope_ref[live, :])
            both = grad_ref[rows, :]
            turned = pltpu.roll(both.astype(F32), NOPE, 1).astype(LOW) if h == 0 else both
            grad = jnp.where(low, jnp.zeros_like(both), turned)
            product = both.astype(F32) * mix_ref[rows, :].astype(F32)
            mine = low if h == 0 else ~low
            inner = jnp.sum(jnp.where(mine, product, 0.0), axis=1, keepdims=True)
            scores = dot_nt(query, key) * SCORE_SCALE + bias_ref[:, live]
            probs = jnp.exp(scores - lse_ref[rows, pl.ds(h * NOPE, 1)])
            edge = jnp.where(causal, probs[:, past:], 0.0)
            probs = edge if i == 0 else jnp.concatenate([probs[:, :past], edge], axis=1)
            score_cot = (probs * (dot_nt(grad, pair) - inner)).astype(LOW)
            dquery = dot(score_cot, key) * SCORE_SCALE
            dq_ref[rows, cols] = (
                dquery * cos_ref[rows, :]
                - pltpu.roll(dquery, half, 1) * lift_ref[rows, :]
                - pltpu.roll(dquery, LANE - half, 1) * drop_ref[rows, :]
            ).astype(LOW)
            dk = dot_tn(score_cot, query) * SCORE_SCALE
            dv = dot_tn(probs.astype(LOW), grad)
            if i > 0:
                dkey[pl.ds(0, past), :] += dk[:past]
                dval[pl.ds(0, past), :] += dv[:past]
            dkey[rows, :] = dk[past:]
            dval[rows, :] = dv[past:]
        dkv_ref[:, cols] = jnp.where(low, dkey[...], dval[...]).astype(LOW)
        drope_ref[...] += dkey[...]


def attend_back(query, pair, rope, bias, tables, mixed, grad, lse):
    count = query.shape[0]
    steps = query.shape[1] // (2 * LANE)
    blocks = 4

    def whole(shape):
        return pl.BlockSpec(shape, lambda i: (0, 0))

    wide = pl.BlockSpec((count, 2 * LANE), lambda i: (0, i))
    slim = pl.BlockSpec((count, LANE), lambda i: (0, i))
    table = whole((count, LANE))
    return pl.pallas_call(
        functools.partial(attend_back_kernel, blocks),
        grid=(steps,),
        in_specs=[wide, wide, table, whole((1, count)), table, table, table, slim, slim, slim],
        out_specs=[wide, wide, table],
        out_shape=[
            jax.ShapeDtypeStruct(query.shape, LOW),
            jax.ShapeDtypeStruct(query.shape, LOW),
            jax.ShapeDtypeStruct((count, LANE), F32),
        ],
        scratch_shapes=[pltpu.VMEM((count, LANE), F32), pltpu.VMEM((count, LANE), F32)],
        cost_estimate=pl.CostEstimate(
            flops=steps * count * count * LANE * 12, bytes_accessed=count * steps * 3600, transcendentals=count * count * steps
        ),
        name="attend_back",
    )(query, pair, rope, bias, *tables, mixed, grad, lse)


LINE = 8
PLANE = 4


def special():
    return lax.axis_size("fsdp") == LINE and lax.axis_size("tp") == PLANE


def tie(*values):
    return lax.optimization_barrier(values)


def hop(values, pairs):
    moves = [(2 * a + core, 2 * b + core) for a, b in pairs for core in range(2)]
    return lax.ppermute(values, "fsdp", moves)


def swap_cores(values):
    return lax.ppermute(values, "fsdp", [(i, i ^ 1) for i in range(LINE)])


UP = [(0, 1), (1, 2), (2, 3)]
DOWN = [(1, 0), (2, 1), (3, 2)]


def line_index():
    return lax.axis_index("fsdp") // 2


def gather_one(values):
    return hop(values, UP), hop(values, DOWN)


def gather_two(above, below):
    return hop(above, UP[1:]) + hop(below, DOWN[:2])


def gather_three(far):
    return hop(far, [(1, 0), (2, 3)])


def assemble(own, above, below, far, last):
    z = line_index()
    whole = jnp.broadcast_to(own[None], (4,) + own.shape)
    put = lax.dynamic_update_index_in_dim
    whole = put(whole, far, (z + 2) % 4, 0)
    whole = put(whole, jnp.where(z == 0, last, above), (z + 3) % 4, 0)
    return put(whole, jnp.where(z == 3, last, below), (z + 1) % 4, 0)


def block_at(part, position):
    return lax.dynamic_index_in_dim(part, position, 0, keepdims=False)


def plus(left, right):
    return (left.astype(F32) + right.astype(F32)).astype(LOW)


def scatter_one(part):
    return hop(block_at(part, 3 - line_index()), [(0, 1), (3, 2)])


def scatter_two(part, first):
    z = line_index()
    up = hop(plus(block_at(part, jnp.minimum(z + 2, 3)), first), UP[:2])
    return up, hop(plus(block_at(part, jnp.maximum(z - 2, 0)), first), DOWN[1:])


def scatter_three(part, up, down):
    z = line_index()
    return hop(plus(block_at(part, jnp.minimum(z + 1, 3)), up), UP), hop(plus(block_at(part, jnp.maximum(z - 1, 0)), down), DOWN)


def scatter_end(part, up, down):
    return block_at(part, line_index()).astype(F32) + up.astype(F32) + down.astype(F32)


def rowwise(values):
    return with_layout_constraint(values, Layout(major_to_minor=tuple(range(values.ndim))))


def by_core(own, other):
    first = lax.axis_index("fsdp") % 2 == 0
    return jnp.where(first, own, other), jnp.where(first, other, own)


def to_line(values):
    block = values.shape[-1] // LINE
    parts = [values[..., i * block : (i + 1) * block] for i in range(LINE)]
    return jnp.concatenate(by_core(jnp.concatenate(parts[0::2], axis=-1), jnp.concatenate(parts[1::2], axis=-1)), axis=-1)


def from_line(values):
    block = values.shape[-1] // LINE
    half = values.shape[-1] // 2
    even, odd = by_core(values[..., :half], values[..., half:])
    parts = [p[..., i * block : (i + 1) * block] for i in range(LINE // 2) for p in (even, odd)]
    return jnp.concatenate(parts, axis=-1)


def deal_one(own):
    return hop(own, UP[:2]), hop(own, DOWN[1:])


def deal_two(up, down):
    return hop(jnp.where(line_index() == 1, up, down), [(1, 2), (2, 1)])


def deal_pick(position, own, up, down, far):
    away = position - line_index()
    near = jnp.where(away == 0, own, jnp.where(away == 1, down, up))
    return jnp.where(jnp.abs(away) < 2, near, far)


def deal_three(own, up, down, far, sources):
    z = line_index()
    core = lax.axis_index("fsdp") % 2
    end = jnp.where(z == 2, 6, 0)
    want, asked = jnp.take(sources, end + core), jnp.take(sources, end + 1 - core)
    theirs = swap_cores(deal_pick(asked // 2, own, up, down, far))
    relay = jnp.where(want % 2 == core, deal_pick(want // 2, own, up, down, far), theirs)
    return hop(relay, [(2, 3), (1, 0)])


def deal_end(own, up, down, far, last, sources):
    z = line_index()
    group = lax.axis_index("fsdp")
    edge = (z == 0) | (z == 3)
    want, asked = jnp.take(sources, group), jnp.take(sources, group + 1 - 2 * (group % 2))

    def pick(position):
        return jnp.where(edge, own, deal_pick(position, own, up, down, far))

    theirs = swap_cores(pick(asked // 2))
    local = jnp.where(want % 2 == group % 2, pick(want // 2), theirs)
    return jnp.where(edge & (want // 2 != z), last, local)


def deal_plain(values, sources):
    group = lax.axis_index("fsdp")
    return lax.dynamic_index_in_dim(lax.all_gather(values, "fsdp"), jnp.take(sources, group), 0, keepdims=False)


MESH = pl.DeviceIdType.MESH


def square():
    me = lax.axis_index("tp")
    y, x = me // 2, me % 2
    beside, across = 2 * y + (1 - x), 2 * (1 - y) + x
    return me, beside, across, 3 - me


def greet(beside, across):
    barrier = pltpu.get_barrier_semaphore()
    for peer in (beside, across):
        pl.semaphore_signal(barrier, inc=1, device_id={"tp": peer}, device_id_type=MESH)
    pl.semaphore_wait(barrier, 2)


def send(source, target, sems, slot, peer):
    copy = pltpu.make_async_remote_copy(
        src_ref=source,
        dst_ref=target,
        send_sem=sems[0].at[slot],
        recv_sem=sems[1].at[slot],
        device_id={"tp": peer},
        device_id_type=MESH,
    )
    copy.start()
    return copy


def rows_of(position, size):
    return pl.ds(pl.multiple_of(position * size, size), size)


def reduce_square(parts, got, kept, sems):
    size = got[0].shape[1]
    me, beside, across, corner = square()
    early = []
    for k, (first, second) in enumerate(((beside, across), (across, beside))):
        early.append(send(parts[k].at[rows_of(corner, size), :], got[k].at[0], sems, 3 * k, first))
    for k, (first, second) in enumerate(((beside, across), (across, beside))):
        early.append(send(parts[k].at[rows_of(first, size), :], got[k].at[1], sems, 3 * k + 1, first))
    for k, (first, second) in enumerate(((beside, across), (across, beside))):
        early[k].wait_recv()
        kept[k][...] = (
            parts[k][rows_of(second, size), :].astype(F32) + got[k][0].astype(F32)
        ).astype(LOW)
        early.append(send(kept[k], got[k].at[2], sems, 3 * k + 2, second))
    for copy in early[2:]:
        copy.wait_recv()
    return early


def spread_square(full, columns, sems, base):
    me, beside, across, corner = square()
    size = full.shape[0] // PLANE
    own = rows_of(me, size)

    def piece(position, k):
        return full.at[rows_of(position, size), columns[k]]

    def pass_on(position, k, slot, peer):
        return send(piece(position, k), piece(position, k), sems, base + slot, peer)

    one = pass_on(me, 0, 0, across)
    two = pass_on(me, 1, 1, beside)
    three = pass_on(me, 0, 2, beside)
    four = pass_on(me, 1, 3, across)
    one.wait_recv()
    five = pass_on(across, 0, 4, beside)
    two.wait_recv()
    six = pass_on(beside, 1, 5, across)
    for copy in (three, four, five, six):
        copy.wait_recv()
    return [one, two, three, four, five, six]


def gather_kernel(cut, own_ref, full_ref, send_sems, recv_sems):
    me, beside, across, _ = square()
    size, width = own_ref.shape
    full_ref[rows_of(me, size), :] = own_ref[...]
    greet(beside, across)
    for copy in spread_square(full_ref, (pl.ds(0, cut), pl.ds(cut, width - cut)), (send_sems, recv_sems), 0):
        copy.wait_send()


def gather_tp(values, name, ident):
    if not special():
        return lax.all_gather(values, "tp", axis=0, tiled=True)
    rows, columns = values.shape
    cut = columns // LANE // 2 * LANE
    return pl.pallas_call(
        functools.partial(gather_kernel, cut),
        in_specs=[pl.BlockSpec(memory_space=pltpu.VMEM)],
        out_specs=pl.BlockSpec(memory_space=pltpu.VMEM),
        out_shape=jax.ShapeDtypeStruct((PLANE * rows, columns), values.dtype),
        scratch_shapes=[pltpu.SemaphoreType.DMA((6,)), pltpu.SemaphoreType.DMA((6,))],
        compiler_params=pltpu.CompilerParams(collective_id=ident, has_side_effects=True),
        cost_estimate=pl.CostEstimate(flops=0, bytes_accessed=16 * rows * columns * 8, transcendentals=0),
        name=name,
    )(values)


def scatter_kernel(cut, all_ref, sum_ref, got0, got1, kept0, kept1, send_sems, recv_sems):
    me, beside, across, _ = square()
    width = all_ref.shape[1]
    size = sum_ref.shape[0]
    greet(beside, across)
    parts = (all_ref.at[:, pl.ds(0, cut)], all_ref.at[:, pl.ds(cut, width - cut)])
    copies = reduce_square(parts, (got0, got1), (kept0, kept1), (send_sems, recv_sems))
    for k, (part, got) in enumerate(zip(parts, (got0, got1))):
        total = part[rows_of(me, size), :].astype(F32) + got[1].astype(F32) + got[2].astype(F32)
        sum_ref[:, (pl.ds(0, cut), pl.ds(cut, width - cut))[k]] = total
    for copy in copies:
        copy.wait_send()


def scatter_tp(values, name, ident):
    if not special():
        return lax.psum_scatter(values, "tp", scatter_dimension=0, tiled=True).astype(F32)
    rows, columns = values.shape
    size = rows // PLANE
    cut = columns // LANE // 2 * LANE
    return pl.pallas_call(
        functools.partial(scatter_kernel, cut),
        in_specs=[pl.BlockSpec(memory_space=pltpu.VMEM)],
        out_specs=pl.BlockSpec(memory_space=pltpu.VMEM),
        out_shape=jax.ShapeDtypeStruct((size, columns), F32),
        scratch_shapes=[
            pltpu.VMEM((3, size, cut), LOW),
            pltpu.VMEM((3, size, columns - cut), LOW),
            pltpu.VMEM((size, cut), LOW),
            pltpu.VMEM((size, columns - cut), LOW),
            pltpu.SemaphoreType.DMA((6,)),
            pltpu.SemaphoreType.DMA((6,)),
        ],
        compiler_params=pltpu.CompilerParams(collective_id=ident, has_side_effects=True),
        cost_estimate=pl.CostEstimate(flops=0, bytes_accessed=16 * rows * columns * 2, transcendentals=0),
        name=name,
    )(values)


ROW_STEP = 32


def enter_kernel(p0_ref, p1_ref, x_ref, gain_ref, after_ref, low_ref, got0, got1, kept0, kept1, send_sems, recv_sems):
    me, beside, across, _ = square()
    size = after_ref.shape[0]
    greet(beside, across)
    parts, gots = (p0_ref, p1_ref), (got0, got1)
    copies = reduce_square(parts, gots, (kept0, kept1), (send_sems, recv_sems))

    def rows_step(step, carry):
        here = pl.ds(pl.multiple_of(step * ROW_STEP, ROW_STEP), ROW_STEP)
        mine = pl.ds(pl.multiple_of(me * size + step * ROW_STEP, ROW_STEP), ROW_STEP)
        total = jnp.concatenate(
            [
                part[mine, :].astype(F32) + got[1, here, :].astype(F32) + got[2, here, :].astype(F32)
                for part, got in zip(parts, gots)
            ],
            axis=1,
        )
        after = x_ref[here, :].astype(F32) + RESIDUAL_SCALE * total
        after_ref[here, :] = after
        factor = lax.rsqrt(jnp.mean(after * after, axis=-1, keepdims=True) + EPSILON)
        low_ref[here, :] = (after * factor * gain_ref[...]).astype(LOW)
        return carry

    lax.fori_loop(0, size // ROW_STEP, rows_step, 0)
    for copy in copies:
        copy.wait_send()


def leave_kernel(
    p0_ref, p1_ref, after_ref, cot_ref, gain_ref, grad_ref, dgain_ref, low_ref, got0, got1, kept0, kept1, send_sems, recv_sems
):
    me, beside, across, _ = square()
    size = after_ref.shape[0]
    greet(beside, across)
    parts, gots = (p0_ref, p1_ref), (got0, got1)
    copies = reduce_square(parts, gots, (kept0, kept1), (send_sems, recv_sems))
    dgain_ref[...] = jnp.zeros_like(dgain_ref)

    def rows_step(step, carry):
        here = pl.ds(pl.multiple_of(step * ROW_STEP, ROW_STEP), ROW_STEP)
        mine = pl.ds(pl.multiple_of(me * size + step * ROW_STEP, ROW_STEP), ROW_STEP)
        grad = jnp.concatenate(
            [
                part[mine, :].astype(F32) + got[1, here, :].astype(F32) + got[2, here, :].astype(F32)
                for part, got in zip(parts, gots)
            ],
            axis=1,
        )
        after = after_ref[here, :]
        factor = lax.rsqrt(jnp.mean(after * after, axis=-1, keepdims=True) + EPSILON)
        weighted = grad * gain_ref[...]
        inner = jnp.mean(weighted * after, axis=-1, keepdims=True)
        dgain_ref[...] += jnp.sum(grad * after * factor, axis=0, keepdims=True)
        total = cot_ref[here, :] + factor * weighted - after * (factor * factor * factor) * inner
        grad_ref[here, :] = total
        low_ref[here, :] = (RESIDUAL_SCALE * total).astype(LOW)
        return carry

    lax.fori_loop(0, size // ROW_STEP, rows_step, 0)
    for copy in copies:
        copy.wait_send()


def square_scratch(size, half):
    return [
        pltpu.VMEM((3, size, half), LOW),
        pltpu.VMEM((3, size, half), LOW),
        pltpu.VMEM((size, half), LOW),
        pltpu.VMEM((size, half), LOW),
        pltpu.SemaphoreType.DMA((6,)),
        pltpu.SemaphoreType.DMA((6,)),
    ]


def enter_mlp(pieces, x_low, gain):
    rows, half = pieces[0].shape[0], x_low.shape[1] // 2
    if not special():
        branch = lax.psum_scatter(pieces[0], "tp", scatter_dimension=0, tiled=True).astype(F32)
        after = x_low.astype(F32) + RESIDUAL_SCALE * branch
        normed, _ = normalize(after, gain)
        return after, normed.astype(LOW)
    size = x_low.shape[0]
    vmem = pl.BlockSpec(memory_space=pltpu.VMEM)
    return pl.pallas_call(
        enter_kernel,
        in_specs=[vmem] * 4,
        out_specs=[vmem] * 2,
        out_shape=[jax.ShapeDtypeStruct((size, 2 * half), F32), jax.ShapeDtypeStruct((size, 2 * half), LOW)],
        scratch_shapes=square_scratch(size, half),
        compiler_params=pltpu.CompilerParams(collective_id=2, has_side_effects=True, vmem_limit_bytes=48 << 20),
        cost_estimate=pl.CostEstimate(flops=0, bytes_accessed=160 << 20, transcendentals=0),
        name="enter_mlp",
    )(*pieces, x_low, gain[None])


def leave_mlp(pieces, after, grad_out, gain):
    rows, half = pieces[0].shape[0], after.shape[1] // 2
    if not special():
        grad = lax.psum_scatter(pieces[0], "tp", scatter_dimension=0, tiled=True).astype(F32)
        factor = lax.rsqrt(jnp.mean(after * after, axis=-1, keepdims=True) + EPSILON)
        extra, dgain = norm_back(after, factor, gain, grad)
        total = grad_out + extra
        return total, dgain, (RESIDUAL_SCALE * total).astype(LOW)
    size = after.shape[0]
    vmem = pl.BlockSpec(memory_space=pltpu.VMEM)
    total, dgain, full = pl.pallas_call(
        leave_kernel,
        in_specs=[vmem] * 5,
        out_specs=[vmem] * 3,
        out_shape=[
            jax.ShapeDtypeStruct((size, 2 * half), F32),
            jax.ShapeDtypeStruct((1, 2 * half), F32),
            jax.ShapeDtypeStruct((size, 2 * half), LOW),
        ],
        scratch_shapes=square_scratch(size, half),
        compiler_params=pltpu.CompilerParams(collective_id=3, has_side_effects=True, vmem_limit_bytes=48 << 20),
        cost_estimate=pl.CostEstimate(flops=0, bytes_accessed=160 << 20, transcendentals=0),
        name="leave_mlp",
    )(*pieces, after, grad_out, gain[None])
    return total, dgain[0], full


UNIT = 256
REST = 64
TOKEN_STEP = 512
FEATURE_STEP = 640


def units_kernel(unit, slabs, begun, x_ref, cot_ref, *refs):
    weights, rest = refs[:slabs], refs[slabs + begun :]
    act_ref, grads = rest[0], rest[1:]
    half = weights[0].shape[0]
    wide = 2 * unit

    def tokens(step, carry):
        rows = pl.ds(pl.multiple_of(step * TOKEN_STEP, TOKEN_STEP), TOKEN_STEP)
        both = 0.0
        grad = 0.0
        for k in range(slabs):
            part = pl.ds(k * half, half)
            both = both + dot(x_ref[rows, part], weights[k][:, 0:wide])
            grad = grad + dot(cot_ref[rows, part], weights[k][:, wide : wide + max(unit, LANE)])
        gate = both[:, : max(unit, LANE)]
        up = both[:, unit:] if unit >= LANE else pltpu.roll(both, unit, 1)
        sigma = 1.0 / (1.0 + jnp.exp(-gate))
        silu = gate * sigma
        activated = silu * up
        gate_cot = grad * up * (sigma * (1.0 + gate * (1.0 - sigma)))
        up_cot = grad * silu
        if unit >= LANE:
            act_ref[rows, 0:unit] = gate_cot.astype(LOW)
            act_ref[rows, unit:wide] = up_cot.astype(LOW)
            act_ref[rows, wide : wide + unit] = activated.astype(LOW)
        else:
            low = lax.broadcasted_iota(jnp.int32, (1, LANE), 1) < unit
            act_ref[rows, 0:LANE] = jnp.where(low, gate_cot, pltpu.roll(up_cot, unit, 1)).astype(LOW)
            act_ref[rows, LANE : 2 * LANE] = jnp.where(low, activated, 0.0).astype(LOW)
        return carry

    lax.fori_loop(0, x_ref.shape[0] // TOKEN_STEP, tokens, 0)
    columns = act_ref.shape[1]
    for k in range(slabs):

        def features(step, carry):
            rows = pl.ds(pl.multiple_of(step * FEATURE_STEP, FEATURE_STEP), FEATURE_STEP)
            part = pl.ds(pl.multiple_of(k * half + step * FEATURE_STEP, LANE), FEATURE_STEP)
            grads[k][rows, 0:wide] = dot_tn(x_ref[:, part], act_ref[:, 0:wide]).astype(LOW)
            grads[k][rows, wide:columns] = dot_tn(cot_ref[:, part], act_ref[:, wide:columns]).astype(LOW)
            return carry

        lax.fori_loop(0, half // FEATURE_STEP, features, 0)


def units_call(values, cot, slabs, unit, first, count, begun):
    rows, width = values.shape
    half, total = slabs[0].shape
    columns = 3 * unit if unit >= LANE else 2 * LANE
    whole = pl.BlockSpec((rows, width), lambda j: (0, 0), pipeline_mode=pl.Buffered(1))
    block = pl.BlockSpec((half, columns), lambda j: (0, j + first))
    shapes = [(rows, total)] + [(half, total)] * len(slabs)
    lead = 2 + len(slabs)
    return pl.pallas_call(
        functools.partial(units_kernel, unit, len(slabs), len(begun)),
        grid=(count,),
        in_specs=[whole, whole] + [block] * len(slabs) + [pl.BlockSpec(memory_space=pl.ANY)] * len(begun),
        out_specs=[pl.BlockSpec((rows, columns), lambda j: (0, j + first))] + [block] * len(slabs),
        out_shape=[jax.ShapeDtypeStruct(shape, LOW) for shape in shapes],
        input_output_aliases={lead + i: i for i in range(len(begun))},
        compiler_params=pltpu.CompilerParams(vmem_limit_bytes=60 << 20),
        cost_estimate=pl.CostEstimate(
            flops=count * 16 * rows * width * unit, bytes_accessed=count * 32 * width * unit, transcendentals=0
        ),
        name="units",
    )(values, cot, *slabs, *begun)


def units_tiles(values, cot, slabs):
    total = slabs[0].shape[1]
    full = total // (3 * UNIT)
    results = units_call(values, cot, slabs, UNIT, 0, full, [])
    if total % (3 * UNIT):
        results = units_call(values, cot, slabs, REST, full * 3, 1, results)
    return results[0], results[1:]


def close_kernel(counts, *refs):
    acts, weights = refs[: len(counts)], refs[len(counts) : 2 * len(counts)]
    back_ref, branch_ref = refs[2 * len(counts) :]

    def tokens(step, carry):
        rows = pl.ds(pl.multiple_of(step * TOKEN_STEP, TOKEN_STEP), TOKEN_STEP)
        back = 0.0
        branch = 0.0
        for (full, rest), act, weight in zip(counts, acts, weights):
            for j in range(full):
                a = 3 * UNIT * j
                b = a + 2 * UNIT
                back = back + dot_nt(act[rows, a:b], weight[:, a:b])
                branch = branch + dot_nt(act[rows, b : b + UNIT], weight[:, b : b + UNIT])
            if rest:
                a = 3 * UNIT * full
                b = a + LANE
                back = back + dot_nt(act[rows, a:b], weight[:, a:b])
                branch = branch + dot_nt(act[rows, b : b + LANE], weight[:, b : b + LANE])
        back_ref[rows, :] = back.astype(LOW)
        branch_ref[rows, :] = branch.astype(LOW)
        return carry

    lax.fori_loop(0, back_ref.shape[0] // TOKEN_STEP, tokens, 0)


def close_tiles(acts, slabs):
    rows = acts[0].shape[0]
    half = slabs[0].shape[0]
    counts = [(act.shape[1] // (3 * UNIT), act.shape[1] % (3 * UNIT)) for act in acts]
    total = sum(act.shape[1] for act in acts)
    return pl.pallas_call(
        functools.partial(close_kernel, counts),
        grid=(half // UNIT,),
        in_specs=[pl.BlockSpec(act.shape, lambda j: (0, 0), pipeline_mode=pl.Buffered(1)) for act in acts]
        + [pl.BlockSpec((UNIT, slab.shape[1]), lambda j: (j, 0)) for slab in slabs],
        out_specs=[pl.BlockSpec((rows, UNIT), lambda j: (0, j))] * 2,
        out_shape=[jax.ShapeDtypeStruct((rows, half), LOW)] * 2,
        compiler_params=pltpu.CompilerParams(vmem_limit_bytes=60 << 20),
        cost_estimate=pl.CostEstimate(flops=3 * rows * total * half, bytes_accessed=8 * rows * total, transcendentals=0),
        name="close",
    )(*acts, *slabs)


def per_device(
    block_input,
    seq_lengths,
    dealt_order,
    out_cotangent,
    attn_gain,
    query_down,
    query_gain,
    latent_down,
    latent_gain,
    query_up,
    latent_up,
    output_matrix,
    mlp_gain,
    gate_weight,
    up_weight,
    down_matrix,
):
    line = special()
    tp_count = lax.axis_size("tp")
    fsdp_count = lax.axis_size("fsdp")
    group = lax.axis_index("fsdp")
    column = lax.axis_index("tp")
    _, local_len, width = block_input.shape
    full_len = local_len * tp_count
    own_len = jnp.take(seq_lengths, group)
    local_pos = column * local_len + jnp.arange(local_len, dtype=jnp.int32)
    valid = (local_pos < own_len).astype(F32)[:, None]
    order = to_line if line else (lambda values: values)
    unorder = from_line if line else (lambda values: values)
    bounds = [(0, width // 2), (width // 2, width)] if line else [(0, width)]

    qr = query_down.shape[1]
    latent_rows = query_down.shape[0]
    small_q, small_l = query_gain.shape[0], latent_gain.shape[0]
    used = qr + KR + ROPE
    padded = -(-(used + 3) // LANE) * LANE
    small = jnp.concatenate([query_gain, latent_gain, jnp.zeros((latent_rows,), F32)])
    if small_q + small_l <= latent_rows:
        small = small[:latent_rows]
        extra = 0
    else:
        small = small[: 2 * latent_rows]
        extra = 1
    down_pack = jnp.concatenate(
        [
            query_down.astype(LOW),
            latent_down.astype(LOW),
            attn_gain.astype(LOW)[:, None],
            mlp_gain.astype(LOW)[:, None],
            small.astype(LOW).reshape(1 + extra, latent_rows).T,
            jnp.zeros((latent_rows, padded - used - 3 - extra), LOW),
        ],
        axis=1,
    )
    down_all = lax.all_gather(down_pack, ("fsdp", "tp"), axis=0, tiled=True)

    heads = query_up.shape[1] // QKD
    even = heads + heads % 2
    q_rows, l_rows = query_up.shape[0], latent_up.shape[0]
    o_rows = output_matrix.shape[0] // 2
    half_width = even * VD

    def pad_heads(values, size, to):
        rows = values.shape[0]
        values = values.reshape(rows, heads, size)
        return jnp.pad(values, ((0, 0), (0, even - heads), (0, to - size))).reshape(rows, even * to)

    out_low = pad_heads(output_matrix.astype(LOW), VD, VD)
    head_pack = jnp.concatenate(
        [
            pad_heads(query_up.astype(LOW), QKD, LANE),
            pad_heads(latent_up.astype(LOW), LANE, LANE),
            jnp.concatenate([out_low[:o_rows], out_low[o_rows:]], axis=1),
        ],
        axis=0,
    )
    units = gate_weight.shape[1]
    cut = 768 if units == 1600 else units // 2
    pieces = [(0, cut), (cut, units)]
    if line:
        tiles = []
        for a in range(0, units, UNIT):
            b = min(a + UNIT, units)
            tiles.append([weight[:, a:b].astype(LOW) for weight in (gate_weight, up_weight, down_matrix)])
        tiles[-1].append(jnp.zeros((gate_weight.shape[0], -3 * (units % UNIT) % LANE), LOW))
        mlp_packs = [jnp.concatenate(sum(part, []), axis=1) for part in (tiles[:3], tiles[3:])]
    else:
        mlp_packs = [
            jnp.concatenate(
                [gate_weight[:, a:b].astype(LOW), up_weight[:, a:b].astype(LOW), down_matrix[:, a:b].astype(LOW)], axis=1
            )
            for a, b in pieces
        ]
    cot_source = jnp.argsort(dealt_order).astype(jnp.int32)
    if line:
        head_low = head_pack
        cot_low = out_cotangent[0]
        head_steps = gather_one(head_low)
        cot_up, cot_down = deal_one(cot_low)
        head_steps += (gather_two(*head_steps),)
        cot_far = deal_two(cot_up, cot_down)
        head_steps += (gather_three(head_steps[2]),)
        cot_steps = (cot_low, cot_up, cot_down, cot_far)
        head_own = assemble(head_low, *head_steps)
        grad_out = deal_end(*cot_steps, deal_three(*cot_steps, cot_source), cot_source)
        down_all, head_own, grad_out, first_low = tie(down_all, head_own, grad_out, mlp_packs[0])
        first_steps = gather_one(first_low)
        head_other = swap_cores(head_own)
        head_slabs = [head_own, head_other]
        first, second = by_core(head_own, head_other)
        natural = jnp.stack([first[:, : q_rows + l_rows], second[:, : q_rows + l_rows]], axis=1)
        natural = natural.reshape(fsdp_count, q_rows + l_rows, -1)
    else:
        head_all = lax.all_gather(head_pack, "fsdp")
        natural = head_all[:, : q_rows + l_rows]
        head_slabs = [head_all]
        mlp_slabs = [[lax.all_gather(pack, "fsdp", axis=0, tiled=True)] for pack in mlp_packs]
        grad_out = deal_plain(out_cotangent[0], cot_source)
    w_qup = natural[:, :q_rows].reshape(-1, even * LANE)
    w_kvup = natural[:, q_rows:].reshape(-1, even * LANE)
    out_slabs = []
    for slab in head_slabs:
        slab = slab[:, q_rows + l_rows :]
        out_slabs.append(jnp.stack([slab[..., :half_width], slab[..., half_width:]], axis=1).reshape(-1, half_width))

    w_down = down_all[:, :used]
    gain_attn = down_all[:, used].astype(F32)
    gain_mlp = order(down_all[:, used + 1].astype(F32))
    smalls = down_all[:, used + 2 : used + 3 + extra].astype(F32).reshape(-1, latent_rows, 1 + extra)
    smalls = jnp.swapaxes(smalls, 1, 2).reshape(-1, latent_rows * (1 + extra))
    gain_query = smalls[:, :small_q].reshape(-1)
    gain_latent = smalls[:, small_q : small_q + small_l].reshape(-1)

    block_low = block_input[0]
    block_vals = block_low.astype(F32)
    normed, factor_in = normalize(block_vals, gain_attn)
    normed_low = normed.astype(LOW)
    latents = dot(normed_low, w_down)
    query_latent, kv_latent = latents[:, :qr], latents[:, qr : qr + KR]
    query_normed, factor_query = normalize(query_latent, gain_query)
    compressed, factor_kv = normalize(kv_latent, gain_latent)
    cos_local, sin_local = rotary_tables(local_pos)
    cos_local = jnp.concatenate([cos_local, cos_local], axis=1)
    sin_local = jnp.concatenate([sin_local, sin_local], axis=1)
    rope_raw = latents[:, qr + KR :]
    rotary_key = rope_raw * cos_local + turn_half(rope_raw) * sin_local
    rotary_key = jnp.pad(rotary_key, ((0, 0), (NOPE, LANE - NOPE - ROPE)))
    latent_low = jnp.concatenate([query_normed.astype(LOW), compressed.astype(LOW), rotary_key.astype(LOW)], axis=1)
    latent_all = gather_tp(latent_low, "gather_latents", 0)
    if line:
        latent_all, grad_out, *first_steps = tie(latent_all, grad_out, *first_steps)
        first_steps.append(gather_two(*first_steps))
    query_all = latent_all[:, :qr]
    comp_all = latent_all[:, qr : qr + KR]
    rope_all = latent_all[:, qr + KR :]

    tables = head_tables(*rotary_tables(jnp.arange(full_len, dtype=jnp.int32)))
    bias = jnp.where(jnp.arange(full_len, dtype=jnp.int32) < own_len, 0.0, MASKED).astype(F32)[None, :]
    query_proj = dot(query_all, w_qup).astype(LOW)
    key_value = dot(comp_all, w_kvup).astype(LOW)
    queries, mixed, lse = attend(query_proj, key_value, rope_all, bias, tables)
    attention_pieces = [dot_nt(mixed, slab).astype(LOW) for slab in out_slabs]
    if line:
        *attention_pieces, first_steps[2], second_low = tie(*attention_pieces, first_steps[2], mlp_packs[1])
        first_steps.append(gather_three(first_steps[2]))
        second_steps = gather_one(second_low)
    after_attn, mlp_in = enter_mlp(attention_pieces, order(block_low), gain_mlp)
    if line:
        mlp_in, first_steps[3], *second_steps = tie(mlp_in, first_steps[3], *second_steps)
        second_steps.append(gather_two(*second_steps))
        own = assemble(first_low, *first_steps)
        mlp_slabs = [[own.reshape(width // 2, -1), swap_cores(own).reshape(width // 2, -1)]]
    mlp_in = gather_tp(mlp_in, "gather_normed", 4)
    if line:
        mlp_in, second_steps[2], *mlp_slabs[0] = tie(mlp_in, second_steps[2], *mlp_slabs[0])
        second_steps.append(gather_three(second_steps[2]))

    grad_out = valid * order(grad_out).astype(F32)
    mlp_cot = lax.all_gather((RESIDUAL_SCALE * grad_out).astype(LOW), "tp", axis=0, tiled=True)

    def split(values):
        return values.reshape(4, -1, values.shape[-1])

    def branch_sum(parts):
        return jnp.concatenate(
            [lax.psum_scatter(piece, "tp", scatter_dimension=0, tiled=True).astype(F32) for piece in parts], axis=1
        )

    def finish(branch):
        return unorder((valid * (after_attn + RESIDUAL_SCALE * branch)).astype(LOW))

    if line:
        first_acts, first_grads = units_tiles(mlp_in, mlp_cot, mlp_slabs[0])
        own, other, second_steps[3] = tie(*first_grads, second_steps[3])
        slab = assemble(second_low, *second_steps)
        mlp_slabs.append([slab.reshape(width // 2, -1), swap_cores(slab).reshape(width // 2, -1)])
        first_part = split(plus(own, swap_cores(other)))
        first_sum = scatter_one(first_part)
        second_acts, second_grads = units_tiles(mlp_in, mlp_cot, mlp_slabs[1])
        second_acts, own, other, first_sum = tie(second_acts, *second_grads, first_sum)
        first_sums = scatter_two(first_part, first_sum)
        swapped = swap_cores(other)
        closed = [close_tiles([first_acts, second_acts], list(pair)) for pair in zip(*mlp_slabs)]
        back_low = [pair[0] for pair in closed]
        ff_low = [pair[1] for pair in closed]
        *back_low, first_up, first_down, swapped = tie(*back_low, *first_sums, swapped)
        first_sums = scatter_three(first_part, first_up, first_down)
        second_part = split(plus(own, swapped))
        second_sum = scatter_one(second_part)
    else:
        mlp_grads = []
        back, branch = 0.0, 0.0
        for (a, b), (slab,) in zip(pieces, mlp_slabs):
            size = b - a
            gate, up = dot(mlp_in, slab[:, :size]), dot(mlp_in, slab[:, size : 2 * size])
            sigma = jax.nn.sigmoid(gate)
            activated = (gate * sigma * up).astype(LOW)
            grad_act = dot(mlp_cot, slab[:, 2 * size :])
            gate_cot = (grad_act * up * sigma * (1.0 + gate * (1.0 - sigma))).astype(LOW)
            up_cot = (grad_act * gate * sigma).astype(LOW)
            back += dot_nt(gate_cot, slab[:, :size]) + dot_nt(up_cot, slab[:, size : 2 * size])
            branch += dot_nt(activated, slab[:, 2 * size :])
            grads = [dot_tn(mlp_in, gate_cot), dot_tn(mlp_in, up_cot), dot_tn(mlp_cot, activated)]
            mlp_grads.append(jnp.concatenate([grad.astype(LOW) for grad in grads], axis=1))
        back_low = [back.astype(LOW)]
        ff_low = [branch.astype(LOW)]
    grad_after, mlp_gain_grad, attn_cot = leave_mlp(back_low, after_attn, grad_out, gain_mlp)
    if line:
        attn_cot, first_up, first_down, second_sum = tie(attn_cot, *first_sums, second_sum)
        first_total = scatter_end(first_part, first_up, first_down)
        second_sums = scatter_two(second_part, second_sum)
    attn_cot = gather_tp(attn_cot, "gather_cot", 5)
    if line:
        attn_cot, second_up, second_down, *ff_low = tie(attn_cot, *second_sums, *ff_low)
        second_sums = scatter_three(second_part, second_up, second_down)
        own_output = finish(branch_sum(ff_low))
    else:
        mlp_sums = [lax.psum_scatter(grads, "fsdp", scatter_dimension=0, tiled=True).astype(F32) for grads in mlp_grads]
        block_output = deal_plain(finish(branch_sum(ff_low)), dealt_order)

    grad_mixed = 0.0
    for (a, b), slab in zip(bounds, out_slabs):
        grad_mixed += dot(attn_cot[:, a:b], slab)
    query_cot, kv_cot, grad_rope_all = attend_back(
        queries, key_value, rope_all, bias, tables, mixed, grad_mixed.astype(LOW), lse
    )
    out_grads = [rowwise(dot_tn(attn_cot[:, a:b], mixed).astype(LOW)) for a, b in bounds]
    if line:
        query_cot, kv_cot, second_up, second_down, own_output = tie(query_cot, kv_cot, *second_sums, own_output)
        second_total = scatter_end(second_part, second_up, second_down)
        deal_up, deal_down = deal_one(own_output)
        out_part = split(plus(out_grads[0], swap_cores(out_grads[1])))
        out_step = scatter_one(out_part)
    back_latents = jnp.concatenate([dot_nt(query_cot, w_qup), dot_nt(kv_cot, w_kvup), grad_rope_all], axis=1).astype(LOW)
    grad_latents = scatter_tp(back_latents, "scatter_latents", 1)
    qup_grad = rowwise(dot_tn(query_all, query_cot).astype(LOW)).reshape(fsdp_count, q_rows, even * LANE)
    kvup_grad = rowwise(dot_tn(comp_all, kv_cot).astype(LOW)).reshape(fsdp_count, l_rows, even * LANE)
    head_grads = jnp.concatenate([qup_grad, kvup_grad], axis=1)
    if line:
        grad_latents, deal_up, deal_down, out_step = tie(grad_latents, deal_up, deal_down, out_step)
        deal_steps = (own_output, deal_up, deal_down, deal_two(deal_up, deal_down))
        block_output = deal_end(*deal_steps, deal_three(*deal_steps, dealt_order), dealt_order)
        out_sum = scatter_end(out_part, *scatter_three(out_part, *scatter_two(out_part, out_step)))
        core = group % 2
        head_grads = head_grads.reshape(4, 2, q_rows + l_rows, even * LANE)
        keep = lax.dynamic_index_in_dim(head_grads, core, 1, keepdims=False)
        part = plus(keep, swap_cores(lax.dynamic_index_in_dim(head_grads, 1 - core, 1, keepdims=False)))
        head_sum = scatter_end(part, *scatter_three(part, *scatter_two(part, scatter_one(part))))
    else:
        head_sum = lax.psum_scatter(head_grads, "fsdp", scatter_dimension=0, tiled=False).astype(F32)
        out_sum = lax.psum_scatter(out_grads[0], "fsdp", scatter_dimension=0, tiled=True).astype(F32)

    def drop_heads(values, size, to):
        return values.reshape(values.shape[0], even, to)[:, :heads, :size].reshape(values.shape[0], heads * size)

    query_up_grad = drop_heads(head_sum[:q_rows], QKD, LANE)
    latent_up_grad = drop_heads(head_sum[q_rows:], LANE, LANE)
    out_weight_grad = drop_heads(out_sum, VD, VD)

    grad_query_latent, query_gain_grad = norm_back(query_latent, factor_query, gain_query, grad_latents[:, :qr])
    grad_kv_latent, latent_gain_grad = norm_back(kv_latent, factor_kv, gain_latent, grad_latents[:, qr : qr + KR])
    grad_rope = grad_latents[:, qr + KR + NOPE : qr + KR + NOPE + ROPE]
    grad_rope = grad_rope * cos_local - turn_half(grad_rope) * sin_local
    latent_cot = jnp.concatenate([grad_query_latent, grad_kv_latent, grad_rope], axis=1).astype(LOW)
    grad_normed = dot_nt(latent_cot, w_down)
    extra_input, attn_gain_grad = norm_back(block_vals, factor_in, gain_attn, grad_normed)
    input_grad = (unorder(grad_after) + extra_input).astype(LOW)

    def by_owner(values):
        return values.reshape(fsdp_count * tp_count, -1)

    gains = jnp.concatenate(
        [by_owner(values) for values in (attn_gain_grad, unorder(mlp_gain_grad), query_gain_grad, latent_gain_grad)], axis=1
    )
    extra_rows = 16
    gains = jnp.pad(gains, ((0, 0), (0, used - gains.shape[1])))
    if line:
        line_normed = order(normed_low)
        gains = gains.astype(LOW).reshape(4, 2, tp_count, 1, used)

        def rows_for(values, parity):
            values = values.reshape(4, tp_count, latent_rows, used)
            tops = lax.dynamic_index_in_dim(gains, parity, 1, keepdims=False)
            tops = jnp.pad(tops, ((0, 0), (0, 0), (0, extra_rows - 1), (0, 0)))
            return jnp.swapaxes(jnp.concatenate([values, tops], axis=2), 0, 1).reshape(-1, used)

        keep = rows_for(rowwise(dot_tn(line_normed[:, : width // 2], latent_cot).astype(LOW)), core)
        away = rows_for(rowwise(dot_tn(line_normed[:, width // 2 :], latent_cot).astype(LOW)), 1 - core)
        part = scatter_tp(plus(keep, swap_cores(away)), "scatter_down", 6).astype(LOW).reshape(4, -1, used)
        pack_sum = scatter_end(part, *scatter_three(part, *scatter_two(part, scatter_one(part))))
        down_sum, gain_sum = pack_sum[:latent_rows], pack_sum[latent_rows]
        first_cuts = [first_total[:, a : a + UNIT] for a in range(0, first_total.shape[1], UNIT)]
        full = second_total.shape[1] // (3 * UNIT) * 3 * UNIT
        second_cuts = [second_total[:, a : a + UNIT] for a in range(0, full, UNIT)]
        second_cuts += [second_total[:, full + i * REST : full + (i + 1) * REST] for i in range(3)]
        gate_grad, up_grad, down_grad = [
            jnp.concatenate(first_cuts[i::3] + second_cuts[i::3], axis=1) for i in range(3)
        ]
    else:
        down_sum = lax.psum_scatter(
            dot_tn(normed_low, latent_cot), ("fsdp", "tp"), scatter_dimension=0, tiled=True
        )
        gain_sum = lax.psum_scatter(gains, ("fsdp", "tp"), scatter_dimension=0, tiled=True)[0]
        sizes = [b - a for a, b in pieces]
        gate_grad, up_grad, down_grad = [
            jnp.concatenate([total[:, i * size : (i + 1) * size] for total, size in zip(mlp_sums, sizes)], axis=1)
            for i in range(3)
        ]
    at = [0, latent_rows, 2 * latent_rows, 2 * latent_rows + small_q, 2 * latent_rows + small_q + small_l]
    return (
        block_output[None],
        input_grad[None],
        gain_sum[at[0] : at[1]],
        down_sum[:, :qr],
        gain_sum[at[2] : at[3]],
        down_sum[:, qr:used],
        gain_sum[at[3] : at[4]],
        query_up_grad,
        latent_up_grad,
        out_weight_grad,
        gain_sum[at[1] : at[2]],
        gate_grad,
        up_grad,
        down_grad,
    )


def solution(mesh):
    both = P(("fsdp", "tp"))
    rows = P(("fsdp", "tp"), None)
    grid = P("fsdp", "tp")
    tokens = P("fsdp", "tp", None)
    return jax.shard_map(
        per_device,
        mesh=mesh,
        in_specs=(tokens, P(), P(), tokens, both, rows, both, rows, both, grid, grid, grid, both, grid, grid, grid),
        out_specs=(tokens, tokens, both, rows, both, rows, both, grid, grid, grid, both, grid, grid, grid),
        check_vma=False,
    )
```

```python
import functools
import math

import jax
import jax.numpy as jnp
from jax import lax
from jax.experimental import pallas as pl
from jax.experimental.layout import Layout, with_layout_constraint
from jax.experimental.pallas import tpu as pltpu
from jax.sharding import PartitionSpec as P

KR = 256
NOPE = 64
ROPE = 32
VD = 64
QKD = 96
LANE = 128

EPSILON = 1e-05
RESIDUAL_SCALE = 1.4 / math.sqrt(62.0)
ROTARY_BASE = 10000.0
MASKED = -1e30
SCORE_SCALE = 1.0 / math.sqrt(QKD)

F32 = jnp.float32
LOW = jnp.bfloat16
NT = (((1,), (1,)), ((), ()))
TN = (((0,), (0,)), ((), ()))


def dot(left, right):
    return jnp.dot(left, right, preferred_element_type=F32)


def dot_nt(left, right):
    return lax.dot_general(left, right, NT, preferred_element_type=F32)


def dot_tn(left, right):
    return lax.dot_general(left, right, TN, preferred_element_type=F32)


def normalize(values, gain):
    factor = lax.rsqrt(jnp.mean(values * values, axis=-1, keepdims=True) + EPSILON)
    return (values * factor * gain, factor)


def norm_back(values, factor, gain, grad):
    weighted = grad * gain
    inner = jnp.mean(weighted * values, axis=-1, keepdims=True)
    dvalues = factor * weighted - values * (factor * factor * factor) * inner
    dgain = jnp.sum(grad * values * factor, axis=0)
    return (dvalues, dgain)


def rotary_tables(positions):
    halfway = ROPE // 2
    spacing = jnp.arange(halfway, dtype=F32) * (2.0 / ROPE)
    freqs = jnp.power(jnp.float32(ROTARY_BASE), -spacing)
    angle = positions.astype(F32)[:, None] * freqs[None, :]
    return (jnp.cos(angle), jnp.sin(angle))


def turn_half(values):
    halfway = values.shape[-1] // 2
    return jnp.concatenate([-values[..., halfway:], values[..., :halfway]], axis=-1)


def head_tables(cosine, sine):
    count = cosine.shape[0]
    one = jnp.ones((count, NOPE), F32)
    zero = jnp.zeros((count, NOPE), F32)
    half = jnp.zeros_like(sine)
    rest = jnp.zeros((count, LANE - NOPE - ROPE), F32)
    return (
        jnp.concatenate([one, cosine, cosine, rest], axis=1),
        jnp.concatenate([zero, half, sine, rest], axis=1),
        jnp.concatenate([zero, -sine, half, rest], axis=1),
    )


def attend_kernel(
    blocks, q_rows, lat_ref, w_ref, bias_ref, cos_ref, lift_ref, drop_ref, rot_ref, kv_ref, mix_ref, lse_ref
):
    size = lat_ref.shape[0] // blocks
    low = lax.broadcasted_iota(jnp.int32, (1, LANE), 1) < NOPE
    causal = lax.broadcasted_iota(jnp.int32, (size, size), 1) <= lax.broadcasted_iota(
        jnp.int32, (size, size), 0
    )
    half = ROPE // 2
    groups, rows_all, columns = w_ref.shape
    qr = groups * q_rows
    kv = lat_ref.shape[1] - LANE
    w_query = w_ref[:, :q_rows].reshape(qr, columns)
    w_pair = w_ref[:, q_rows:].reshape(groups * (rows_all - q_rows), columns)
    kv_ref[...] = dot(lat_ref[:, qr:kv], w_pair).astype(LOW)
    rope_ref = lat_ref.at[:, pl.ds(kv, LANE)]
    for i in range(blocks):
        rows = pl.ds(i * size, size)
        live = pl.ds(0, (i + 1) * size)
        outs = []
        projected = dot(lat_ref[rows, :qr], w_query).astype(LOW).astype(F32)
        for h in range(2):
            cols = pl.ds(h * LANE, LANE)
            query = projected[:, h * LANE : (h + 1) * LANE]
            query = (
                query * cos_ref[rows, :]
                + pltpu.roll(query, half, 1) * lift_ref[rows, :]
                + pltpu.roll(query, LANE - half, 1) * drop_ref[rows, :]
            ).astype(LOW)
            rot_ref[rows, cols] = query
            pair = kv_ref[live, cols]
            key = jnp.where(low, pair, rope_ref[live, :])
            value = jnp.where(low, jnp.ones_like(pair), pair)
            scores = dot_nt(query, key) * SCORE_SCALE + bias_ref[:, live]
            edge = jnp.where(causal, scores[:, i * size :], MASKED)
            scores = edge if i == 0 else jnp.concatenate([scores[:, : i * size], edge], axis=1)
            top = jnp.max(scores, axis=1, keepdims=True)
            expo = jnp.exp(scores - top)
            out = dot(expo.astype(LOW), value)
            total = out[:, 0:1]
            lse_ref[rows, pl.ds(h * NOPE, NOPE)] = jnp.broadcast_to(top + jnp.log(total), (size, NOPE))
            outs.append(out / total)
        mix_ref[rows, :] = jnp.where(low, pltpu.roll(outs[0], NOPE, 1), outs[1]).astype(LOW)


def attend(latents, weights, q_rows, bias, tables):
    count = latents.shape[0]
    groups, rows_all, columns = weights.shape
    steps = columns // (2 * LANE)
    blocks = 4

    def whole(shape):
        return pl.BlockSpec(shape, lambda i: (0, 0))

    wide = pl.BlockSpec((count, 2 * LANE), lambda i: (0, i))
    slim = pl.BlockSpec((count, LANE), lambda i: (0, i))
    table = whole((count, LANE))
    return pl.pallas_call(
        functools.partial(attend_kernel, blocks, q_rows),
        grid=(steps,),
        in_specs=[
            whole(latents.shape),
            pl.BlockSpec((groups, rows_all, 2 * LANE), lambda i: (0, 0, i)),
            whole((1, count)),
            table,
            table,
            table,
        ],
        out_specs=[wide, wide, slim, slim],
        out_shape=[
            jax.ShapeDtypeStruct((count, columns), LOW),
            jax.ShapeDtypeStruct((count, columns), LOW),
            jax.ShapeDtypeStruct((count, steps * LANE), LOW),
            jax.ShapeDtypeStruct((count, steps * LANE), F32),
        ],
        cost_estimate=pl.CostEstimate(
            flops=steps * count * count * LANE * 8, bytes_accessed=count * steps * 4000, transcendentals=count * count * steps
        ),
        name="attend",
    )(latents, weights, bias, *tables)


def attend_back_kernel(
    blocks,
    q_ref,
    kv_ref,
    rope_ref,
    bias_ref,
    cos_ref,
    lift_ref,
    drop_ref,
    mix_ref,
    grad_ref,
    lse_ref,
    dq_ref,
    dkv_ref,
    drope_ref,
    dkey,
    dval,
    drope,
):
    size = q_ref.shape[0] // blocks
    low = lax.broadcasted_iota(jnp.int32, (1, LANE), 1) < NOPE
    causal = lax.broadcasted_iota(jnp.int32, (size, size), 1) <= lax.broadcasted_iota(
        jnp.int32, (size, size), 0
    )
    half = ROPE // 2

    @pl.when(pl.program_id(0) == 0)
    def _():
        drope[...] = jnp.zeros_like(drope)

    for h in range(2):
        cols = pl.ds(h * LANE, LANE)
        for i in range(blocks):
            rows = pl.ds(i * size, size)
            past = i * size
            live = pl.ds(0, past + size)
            query = q_ref[rows, cols]
            pair = kv_ref[live, cols]
            key = jnp.where(low, pair, rope_ref[live, :])
            both = grad_ref[rows, :]
            turned = pltpu.roll(both.astype(F32), NOPE, 1).astype(LOW) if h == 0 else both
            grad = jnp.where(low, jnp.zeros_like(both), turned)
            product = both.astype(F32) * mix_ref[rows, :].astype(F32)
            mine = low if h == 0 else ~low
            inner = jnp.sum(jnp.where(mine, product, 0.0), axis=1, keepdims=True)
            scores = dot_nt(query, key) * SCORE_SCALE + bias_ref[:, live]
            probs = jnp.exp(scores - lse_ref[rows, pl.ds(h * NOPE, 1)])
            edge = jnp.where(causal, probs[:, past:], 0.0)
            probs = edge if i == 0 else jnp.concatenate([probs[:, :past], edge], axis=1)
            score_cot = (probs * (dot_nt(grad, pair) - inner)).astype(LOW)
            dquery = dot(score_cot, key) * SCORE_SCALE
            dq_ref[rows, cols] = (
                dquery * cos_ref[rows, :]
                - pltpu.roll(dquery, half, 1) * lift_ref[rows, :]
                - pltpu.roll(dquery, LANE - half, 1) * drop_ref[rows, :]
            ).astype(LOW)
            dk = dot_tn(score_cot, query) * SCORE_SCALE
            dv = dot_tn(probs.astype(LOW), grad)
            if i > 0:
                dkey[pl.ds(0, past), :] += dk[:past]
                dval[pl.ds(0, past), :] += dv[:past]
            dkey[rows, :] = dk[past:]
            dval[rows, :] = dv[past:]
        dkv_ref[:, cols] = jnp.where(low, dkey[...], dval[...]).astype(LOW)
        drope[...] += dkey[...]
    drope_ref[...] = drope[...].astype(LOW)


def attend_back(query, pair, rope, bias, tables, mixed, grad, lse):
    count = query.shape[0]
    steps = query.shape[1] // (2 * LANE)
    blocks = 4

    def whole(shape):
        return pl.BlockSpec(shape, lambda i: (0, 0))

    wide = pl.BlockSpec((count, 2 * LANE), lambda i: (0, i))
    slim = pl.BlockSpec((count, LANE), lambda i: (0, i))
    table = whole((count, LANE))
    return pl.pallas_call(
        functools.partial(attend_back_kernel, blocks),
        grid=(steps,),
        in_specs=[wide, wide, table, whole((1, count)), table, table, table, slim, slim, slim],
        out_specs=[wide, wide, table],
        out_shape=[
            jax.ShapeDtypeStruct(query.shape, LOW),
            jax.ShapeDtypeStruct(query.shape, LOW),
            jax.ShapeDtypeStruct((count, LANE), LOW),
        ],
        scratch_shapes=[pltpu.VMEM((count, LANE), F32)] * 3,
        cost_estimate=pl.CostEstimate(
            flops=steps * count * count * LANE * 12, bytes_accessed=count * steps * 3600, transcendentals=count * count * steps
        ),
        name="attend_back",
    )(query, pair, rope, bias, *tables, mixed, grad, lse)


LINE = 8
PLANE = 4


def special():
    return lax.axis_size("fsdp") == LINE and lax.axis_size("tp") == PLANE


def tie(*values):
    return lax.optimization_barrier(values)


def hop(values, pairs):
    moves = [(2 * a + core, 2 * b + core) for a, b in pairs for core in range(2)]
    return lax.ppermute(values, "fsdp", moves)


def swap_cores(values):
    return lax.ppermute(values, "fsdp", [(i, i ^ 1) for i in range(LINE)])


UP = [(0, 1), (1, 2), (2, 3)]
DOWN = [(1, 0), (2, 1), (3, 2)]


def line_index():
    return lax.axis_index("fsdp") // 2


def gather_one(values):
    return hop(values, UP), hop(values, DOWN)


def gather_two(above, below):
    return hop(above, UP[1:]) + hop(below, DOWN[:2])


def gather_three(far):
    return hop(far, [(1, 0), (2, 3)])


def assemble(own, above, below, far, last):
    z = line_index()
    whole = jnp.broadcast_to(own[None], (4,) + own.shape)
    put = lax.dynamic_update_index_in_dim
    whole = put(whole, far, (z + 2) % 4, 0)
    whole = put(whole, jnp.where(z == 0, last, above), (z + 3) % 4, 0)
    return put(whole, jnp.where(z == 3, last, below), (z + 1) % 4, 0)


def block_at(part, position):
    return lax.dynamic_index_in_dim(part, position, 0, keepdims=False)


def plus(left, right):
    return (left.astype(F32) + right.astype(F32)).astype(LOW)


def scatter_one(part):
    return hop(block_at(part, 3 - line_index()), [(0, 1), (3, 2)])


def scatter_two(part, first):
    z = line_index()
    up = hop(plus(block_at(part, jnp.minimum(z + 2, 3)), first), UP[:2])
    return up, hop(plus(block_at(part, jnp.maximum(z - 2, 0)), first), DOWN[1:])


def scatter_three(part, up, down):
    z = line_index()
    return hop(plus(block_at(part, jnp.minimum(z + 1, 3)), up), UP), hop(plus(block_at(part, jnp.maximum(z - 1, 0)), down), DOWN)


def scatter_end(part, up, down):
    return block_at(part, line_index()).astype(F32) + up.astype(F32) + down.astype(F32)


def rowwise(values):
    return with_layout_constraint(values, Layout(major_to_minor=tuple(range(values.ndim))))


def by_core(own, other):
    first = lax.axis_index("fsdp") % 2 == 0
    return jnp.where(first, own, other), jnp.where(first, other, own)


def to_line(values):
    block = values.shape[-1] // LINE
    parts = [values[..., i * block : (i + 1) * block] for i in range(LINE)]
    return jnp.concatenate(by_core(jnp.concatenate(parts[0::2], axis=-1), jnp.concatenate(parts[1::2], axis=-1)), axis=-1)


def from_line(values):
    block = values.shape[-1] // LINE
    half = values.shape[-1] // 2
    even, odd = by_core(values[..., :half], values[..., half:])
    parts = [p[..., i * block : (i + 1) * block] for i in range(LINE // 2) for p in (even, odd)]
    return jnp.concatenate(parts, axis=-1)


def deal_plain(values, sources):
    group = lax.axis_index("fsdp")
    return lax.dynamic_index_in_dim(lax.all_gather(values, "fsdp"), jnp.take(sources, group), 0, keepdims=False)


MESH = pl.DeviceIdType.MESH


def square():
    me = lax.axis_index("tp")
    y, x = me // 2, me % 2
    beside, across = 2 * y + (1 - x), 2 * (1 - y) + x
    return me, beside, across, 3 - me


def greet(beside, across):
    barrier = pltpu.get_barrier_semaphore()
    for peer in (beside, across):
        pl.semaphore_signal(barrier, inc=1, device_id={"tp": peer}, device_id_type=MESH)
    pl.semaphore_wait(barrier, 2)


def send(source, target, sems, slot, peer):
    copy = pltpu.make_async_remote_copy(
        src_ref=source,
        dst_ref=target,
        send_sem=sems[0].at[slot],
        recv_sem=sems[1].at[slot],
        device_id={"tp": peer},
        device_id_type=MESH,
    )
    copy.start()
    return copy


def rows_of(position, size):
    return pl.ds(pl.multiple_of(position * size, size), size)


def reduce_square(parts, got, sems, prepare=lambda position: None, meanwhile=lambda: None):
    size = got[0].shape[1]
    me, beside, across, corner = square()
    peers = ((beside, across), (across, beside))
    prepare(corner)
    early = [
        send(parts[k].at[rows_of(corner, size), :], got[k].at[0], sems, 3 * k, first) for k, (first, _) in enumerate(peers)
    ]
    for k, (first, _) in enumerate(peers):
        prepare(first)
        early.append(send(parts[k].at[rows_of(first, size), :], got[k].at[1], sems, 3 * k + 1, first))
    for k, (_, second) in enumerate(peers):
        early[k].wait_recv()
        onward = rows_of(second, size)
        parts[k][onward, :] = (parts[k][onward, :].astype(F32) + got[k][0].astype(F32)).astype(LOW)
        early.append(send(parts[k].at[onward, :], got[k].at[2], sems, 3 * k + 2, second))
    prepare(me)
    meanwhile()
    for copy in early[2:]:
        copy.wait_recv()
    return early


def spread_square(full, columns, sems, base):
    me, beside, across, corner = square()
    size = full.shape[0] // PLANE
    own = rows_of(me, size)

    def piece(position, k):
        return full.at[rows_of(position, size), columns[k]]

    def pass_on(position, k, slot, peer):
        return send(piece(position, k), piece(position, k), sems, base + slot, peer)

    one = pass_on(me, 0, 0, across)
    two = pass_on(me, 1, 1, beside)
    three = pass_on(me, 0, 2, beside)
    four = pass_on(me, 1, 3, across)
    one.wait_recv()
    five = pass_on(across, 0, 4, beside)
    two.wait_recv()
    six = pass_on(beside, 1, 5, across)
    for copy in (three, four, five, six):
        copy.wait_recv()
    return [one, two, three, four, five, six]


def gather_kernel(cut, own_ref, full_ref, send_sems, recv_sems):
    me, beside, across, _ = square()
    size, width = own_ref.shape
    full_ref[rows_of(me, size), :] = own_ref[...]
    greet(beside, across)
    for copy in spread_square(full_ref, (pl.ds(0, cut), pl.ds(cut, width - cut)), (send_sems, recv_sems), 0):
        copy.wait_send()


def gather_tp(values, name, ident):
    if not special():
        return lax.all_gather(values, "tp", axis=0, tiled=True)
    rows, columns = values.shape
    cut = columns // LANE // 2 * LANE
    return pl.pallas_call(
        functools.partial(gather_kernel, cut),
        in_specs=[pl.BlockSpec(memory_space=pltpu.VMEM)],
        out_specs=pl.BlockSpec(memory_space=pltpu.VMEM),
        out_shape=jax.ShapeDtypeStruct((PLANE * rows, columns), values.dtype),
        scratch_shapes=[pltpu.SemaphoreType.DMA((6,)), pltpu.SemaphoreType.DMA((6,))],
        compiler_params=pltpu.CompilerParams(collective_id=ident, has_side_effects=True),
        cost_estimate=pl.CostEstimate(flops=0, bytes_accessed=16 * rows * columns * 8, transcendentals=0),
        name=name,
    )(values)


ROW_STEP = 32


def enter_kernel(
    mix_ref, w0_ref, w1_ref, x_ref, gain_ref, after_ref, low_ref, p0_ref, p1_ref, got0, got1, send_sems, recv_sems
):
    me, beside, across, _ = square()
    size = after_ref.shape[0]
    greet(beside, across)
    parts, gots = (p0_ref, p1_ref), (got0, got1)

    def prepare(position):
        here = rows_of(position, size)
        for part, weight in zip(parts, (w0_ref, w1_ref)):
            part[here, :] = dot_nt(mix_ref[here, :], weight[...]).astype(LOW)

    copies = reduce_square(parts, gots, (send_sems, recv_sems), prepare)

    def rows_step(step, carry):
        here = pl.ds(pl.multiple_of(step * ROW_STEP, ROW_STEP), ROW_STEP)
        mine = pl.ds(pl.multiple_of(me * size + step * ROW_STEP, ROW_STEP), ROW_STEP)
        total = jnp.concatenate(
            [
                part[mine, :].astype(F32) + got[1, here, :].astype(F32) + got[2, here, :].astype(F32)
                for part, got in zip(parts, gots)
            ],
            axis=1,
        )
        after = x_ref[here, :].astype(F32) + RESIDUAL_SCALE * total
        after_ref[here, :] = after
        factor = lax.rsqrt(jnp.mean(after * after, axis=-1, keepdims=True) + EPSILON)
        low_ref[here, :] = (after * factor * gain_ref[...]).astype(LOW)
        return carry

    lax.fori_loop(0, size // ROW_STEP, rows_step, 0)
    for copy in copies:
        copy.wait_send()


def leave_kernel(
    p0_ref, p1_ref, after_ref, cot_ref, gain_ref, grad_ref, dgain_ref, low_ref, got0, got1, send_sems, recv_sems
):
    me, beside, across, _ = square()
    size = after_ref.shape[0]
    greet(beside, across)
    parts, gots = (p0_ref, p1_ref), (got0, got1)
    copies = reduce_square(parts, gots, (send_sems, recv_sems))
    dgain_ref[...] = jnp.zeros_like(dgain_ref)

    def rows_step(step, carry):
        here = pl.ds(pl.multiple_of(step * ROW_STEP, ROW_STEP), ROW_STEP)
        mine = pl.ds(pl.multiple_of(me * size + step * ROW_STEP, ROW_STEP), ROW_STEP)
        grad = jnp.concatenate(
            [
                part[mine, :].astype(F32) + got[1, here, :].astype(F32) + got[2, here, :].astype(F32)
                for part, got in zip(parts, gots)
            ],
            axis=1,
        )
        after = after_ref[here, :]
        factor = lax.rsqrt(jnp.mean(after * after, axis=-1, keepdims=True) + EPSILON)
        weighted = grad * gain_ref[...]
        inner = jnp.mean(weighted * after, axis=-1, keepdims=True)
        dgain_ref[...] += jnp.sum(grad * after * factor, axis=0, keepdims=True)
        total = cot_ref[here, :].astype(F32) + factor * weighted - after * (factor * factor * factor) * inner
        grad_ref[here, :] = total
        low_ref[here, :] = (RESIDUAL_SCALE * total).astype(LOW)
        return carry

    lax.fori_loop(0, size // ROW_STEP, rows_step, 0)
    for copy in copies:
        copy.wait_send()


def square_scratch(size, half):
    return [
        pltpu.VMEM((3, size, half), LOW),
        pltpu.VMEM((3, size, half), LOW),
        pltpu.SemaphoreType.DMA((6,)),
        pltpu.SemaphoreType.DMA((6,)),
    ]


def enter_mlp(mixed, slabs, x_low, gain):
    rows, half = mixed.shape[0], x_low.shape[1] // 2
    if not special():
        piece = dot_nt(mixed, slabs[0]).astype(LOW)
        branch = lax.psum_scatter(piece, "tp", scatter_dimension=0, tiled=True).astype(F32)
        after = x_low.astype(F32) + RESIDUAL_SCALE * branch
        normed, _ = normalize(after, gain)
        return after, normed.astype(LOW)
    size = x_low.shape[0]
    vmem = pl.BlockSpec(memory_space=pltpu.VMEM)
    return pl.pallas_call(
        enter_kernel,
        in_specs=[vmem] * 5,
        out_specs=[vmem] * 2,
        out_shape=[jax.ShapeDtypeStruct((size, 2 * half), F32), jax.ShapeDtypeStruct((size, 2 * half), LOW)],
        scratch_shapes=[pltpu.VMEM((rows, half), LOW)] * 2 + square_scratch(size, half),
        compiler_params=pltpu.CompilerParams(collective_id=2, has_side_effects=True, vmem_limit_bytes=48 << 20),
        cost_estimate=pl.CostEstimate(flops=0, bytes_accessed=160 << 20, transcendentals=0),
        name="enter_mlp",
    )(mixed, *slabs, x_low, gain[None])


def leave_mlp(pieces, after, grad_out, gain):
    rows, half = pieces[0].shape[0], after.shape[1] // 2
    if not special():
        grad = lax.psum_scatter(pieces[0], "tp", scatter_dimension=0, tiled=True).astype(F32)
        factor = lax.rsqrt(jnp.mean(after * after, axis=-1, keepdims=True) + EPSILON)
        extra, dgain = norm_back(after, factor, gain, grad)
        total = grad_out + extra
        return total, dgain, (RESIDUAL_SCALE * total).astype(LOW)
    size = after.shape[0]
    vmem = pl.BlockSpec(memory_space=pltpu.VMEM)
    total, dgain, full = pl.pallas_call(
        leave_kernel,
        in_specs=[vmem] * 5,
        out_specs=[vmem] * 3,
        out_shape=[
            jax.ShapeDtypeStruct((size, 2 * half), F32),
            jax.ShapeDtypeStruct((1, 2 * half), F32),
            jax.ShapeDtypeStruct((size, 2 * half), LOW),
        ],
        scratch_shapes=square_scratch(size, half),
        compiler_params=pltpu.CompilerParams(collective_id=3, has_side_effects=True, vmem_limit_bytes=48 << 20),
        cost_estimate=pl.CostEstimate(flops=0, bytes_accessed=160 << 20, transcendentals=0),
        name="leave_mlp",
    )(*pieces, after, grad_out.astype(LOW), gain[None])
    return total, dgain[0], full


UNIT = 256
REST = 64
TOKEN_STEP = 512
FEATURE_STEP = 640


def units_kernel(unit, slabs, begun, x_ref, cot_ref, *refs):
    weights, rest = refs[:slabs], refs[slabs + begun :]
    act_ref, grads = rest[0], rest[1:]
    half = weights[0].shape[0]
    wide = 2 * unit

    def tokens(step, carry):
        rows = pl.ds(pl.multiple_of(step * TOKEN_STEP, TOKEN_STEP), TOKEN_STEP)
        both = 0.0
        grad = 0.0
        for k in range(slabs):
            part = pl.ds(k * half, half)
            both = both + dot(x_ref[rows, part], weights[k][:, 0:wide])
            grad = grad + dot(cot_ref[rows, part], weights[k][:, wide : wide + max(unit, LANE)])
        gate = both[:, : max(unit, LANE)]
        up = both[:, unit:] if unit >= LANE else pltpu.roll(both, unit, 1)
        sigma = 1.0 / (1.0 + jnp.exp(-gate))
        silu = gate * sigma
        activated = silu * up
        gate_cot = grad * up * (sigma * (1.0 + gate * (1.0 - sigma)))
        up_cot = grad * silu
        if unit >= LANE:
            act_ref[rows, 0:unit] = gate_cot.astype(LOW)
            act_ref[rows, unit:wide] = up_cot.astype(LOW)
            act_ref[rows, wide : wide + unit] = activated.astype(LOW)
        else:
            low = lax.broadcasted_iota(jnp.int32, (1, LANE), 1) < unit
            act_ref[rows, 0:LANE] = jnp.where(low, gate_cot, pltpu.roll(up_cot, unit, 1)).astype(LOW)
            act_ref[rows, LANE : 2 * LANE] = jnp.where(low, activated, 0.0).astype(LOW)
        return carry

    lax.fori_loop(0, x_ref.shape[0] // TOKEN_STEP, tokens, 0)
    columns = act_ref.shape[1]
    for k in range(slabs):

        def features(step, carry):
            rows = pl.ds(pl.multiple_of(step * FEATURE_STEP, FEATURE_STEP), FEATURE_STEP)
            part = pl.ds(pl.multiple_of(k * half + step * FEATURE_STEP, LANE), FEATURE_STEP)
            grads[k][rows, 0:wide] = dot_tn(x_ref[:, part], act_ref[:, 0:wide]).astype(LOW)
            grads[k][rows, wide:columns] = dot_tn(cot_ref[:, part], act_ref[:, wide:columns]).astype(LOW)
            return carry

        lax.fori_loop(0, half // FEATURE_STEP, features, 0)


def units_call(values, cot, slabs, unit, first, count, begun):
    rows, width = values.shape
    half, total = slabs[0].shape
    columns = 3 * unit if unit >= LANE else 2 * LANE
    whole = pl.BlockSpec((rows, width), lambda j: (0, 0), pipeline_mode=pl.Buffered(1))
    block = pl.BlockSpec((half, columns), lambda j: (0, j + first))
    shapes = [(rows, total)] + [(half, total)] * len(slabs)
    lead = 2 + len(slabs)
    return pl.pallas_call(
        functools.partial(units_kernel, unit, len(slabs), len(begun)),
        grid=(count,),
        in_specs=[whole, whole] + [block] * len(slabs) + [pl.BlockSpec(memory_space=pl.ANY)] * len(begun),
        out_specs=[pl.BlockSpec((rows, columns), lambda j: (0, j + first))] + [block] * len(slabs),
        out_shape=[jax.ShapeDtypeStruct(shape, LOW) for shape in shapes],
        input_output_aliases={lead + i: i for i in range(len(begun))},
        compiler_params=pltpu.CompilerParams(vmem_limit_bytes=60 << 20),
        cost_estimate=pl.CostEstimate(
            flops=count * 16 * rows * width * unit, bytes_accessed=count * 32 * width * unit, transcendentals=0
        ),
        name="units",
    )(values, cot, *slabs, *begun)


def units_tiles(values, cot, slabs):
    total = slabs[0].shape[1]
    full = total // (3 * UNIT)
    results = units_call(values, cot, slabs, UNIT, 0, full, [])
    if total % (3 * UNIT):
        results = units_call(values, cot, slabs, REST, full * 3, 1, results)
    return results[0], results[1:]


def close_kernel(counts, begun, *refs):
    acts, weights = refs[: len(counts)], refs[len(counts) : 2 * len(counts)]
    back_ref, branch_ref = refs[2 * len(counts) + begun :]

    def tokens(step, carry):
        rows = pl.ds(pl.multiple_of(step * TOKEN_STEP, TOKEN_STEP), TOKEN_STEP)
        back = 0.0
        branch = 0.0
        for (full, rest), act, weight in zip(counts, acts, weights):
            for j in range(full):
                a = 3 * UNIT * j
                b = a + 2 * UNIT
                back = back + dot_nt(act[rows, a:b], weight[:, a:b])
                branch = branch + dot_nt(act[rows, b : b + UNIT], weight[:, b : b + UNIT])
            if rest:
                a = 3 * UNIT * full
                b = a + LANE
                back = back + dot_nt(act[rows, a:b], weight[:, a:b])
                branch = branch + dot_nt(act[rows, b : b + LANE], weight[:, b : b + LANE])
        back_ref[rows, :] = back.astype(LOW)
        branch_ref[rows, :] = branch.astype(LOW)
        return carry

    lax.fori_loop(0, back_ref.shape[0] // TOKEN_STEP, tokens, 0)


def close_tiles(acts, slabs, first, begun):
    rows = acts[0].shape[0]
    half = slabs[0].shape[0]
    counts = [(act.shape[1] // (3 * UNIT), act.shape[1] % (3 * UNIT)) for act in acts]
    total = sum(act.shape[1] for act in acts)
    return pl.pallas_call(
        functools.partial(close_kernel, counts, len(begun)),
        grid=(half // UNIT,),
        in_specs=[pl.BlockSpec(act.shape, lambda j: (0, 0), pipeline_mode=pl.Buffered(1)) for act in acts]
        + [pl.BlockSpec((UNIT, slab.shape[1]), lambda j: (j, 0)) for slab in slabs]
        + [pl.BlockSpec(memory_space=pl.ANY)] * len(begun),
        out_specs=[
            pl.BlockSpec((rows, UNIT), lambda j: (0, j)),
            pl.BlockSpec((rows, UNIT), lambda j: (0, j + first)),
        ],
        out_shape=[jax.ShapeDtypeStruct((rows, half), LOW), jax.ShapeDtypeStruct((rows, 2 * half), LOW)],
        input_output_aliases={2 * len(acts): 1} if begun else {},
        compiler_params=pltpu.CompilerParams(vmem_limit_bytes=60 << 20),
        cost_estimate=pl.CostEstimate(flops=3 * rows * total * half, bytes_accessed=8 * rows * total, transcendentals=0),
        name="close",
    )(*acts, *slabs, *begun)


class Wires:
    def __init__(self, send_sems, recv_sems):
        self.send_sems, self.recv_sems = send_sems, recv_sems

    def _copy(self, source, target, number, peer):
        return pltpu.make_async_remote_copy(
            src_ref=source,
            dst_ref=target,
            send_sem=self.send_sems.at[number],
            recv_sem=self.recv_sems.at[number],
            device_id=peer,
            device_id_type=MESH,
        )

    def start(self, source, target, number, peer):
        self._copy(source, target, number, peer).start()

    def sent(self, source, number, peer):
        self._copy(source, source, number, peer).wait_send()

    def arrived(self, target, number, peer):
        self._copy(target, target, number, peer).wait_recv()


def line_peers():
    group = lax.axis_index("fsdp")
    z, core = group // 2, group % 2
    return z, core, {"fsdp": group + 1 - 2 * core}


def line_peer(z, core):
    return {"fsdp": 2 * z + core}


def greet_all(peers):
    barrier = pltpu.get_barrier_semaphore()
    for peer in peers:
        pl.semaphore_signal(barrier, inc=1, device_id=peer, device_id_type=MESH)
    pl.semaphore_wait(barrier, len(peers))


def gather_square(piece, sources, wires, base):
    me, beside, across, corner = square()
    beside_peer, across_peer = {"tp": beside}, {"tp": across}
    for number, (k, peer) in enumerate(((0, across_peer), (1, beside_peer), (0, beside_peer), (1, across_peer))):
        wires.start(sources[k], piece(me, k), base + number, peer)

    def relay():
        wires.arrived(piece(across, 0), base, across_peer)
        wires.start(piece(across, 0), piece(across, 0), base + 4, beside_peer)
        wires.arrived(piece(beside, 1), base + 1, beside_peer)
        wires.start(piece(beside, 1), piece(beside, 1), base + 5, across_peer)

    def neighbours():
        wires.arrived(piece(beside, 0), base + 2, beside_peer)
        wires.arrived(piece(across, 1), base + 3, across_peer)

    def finish():
        wires.arrived(piece(corner, 0), base + 4, beside_peer)
        wires.arrived(piece(corner, 1), base + 5, across_peer)

    def leave():
        for number, k in enumerate((0, 1, 0, 1, 0, 1)):
            wires.sent(piece(me, k), base + number, beside_peer)

    return relay, neighbours, finish, leave


def store_line(ref, rows, values, core):
    half = values.shape[1] // 2
    block = half // 4
    for i in range(4):
        even = values[:, 2 * i * block : (2 * i + 1) * block]
        odd = values[:, (2 * i + 1) * block : (2 * i + 2) * block]
        ref[rows, i * block : (i + 1) * block] = jnp.where(core == 0, even, odd).astype(ref.dtype)
        ref[rows, half + i * block : half + (i + 1) * block] = jnp.where(core == 0, odd, even).astype(ref.dtype)


def bring_kernel(
    sources_ref,
    length_ref,
    down_ref,
    qk_ref,
    out_ref,
    cot_ref,
    input_ref,
    spot_ref,
    cos_ref,
    lift_ref,
    drop_ref,
    part_ref,
    downs_ref,
    qks_ref,
    outs_ref,
    own_cot_ref,
    normed_ref,
    latents_ref,
    gains_ref,
    all_ref,
    cots_ref,
    above_ref,
    below_ref,
    x_ref,
    scaled,
    blocks,
    got,
    theirs,
    stage,
    send_sems,
    recv_sems,
    local_sems,
):
    z, core, sibling = line_peers()
    me, beside, across, corner = square()
    wires = Wires(send_sems, recv_sems)
    size, width = cot_ref.shape
    half = width // 2
    turns = [line_peer((z + r) % 4, core) for r in (1, 2, 3)]
    greet_all([sibling, {"tp": beside}, {"tp": across}] + turns)
    up, down = line_peer((z + 1) % 4, core), line_peer((z + 3) % 4, core)
    edge = (z == 0) | (z == 3)
    inner = (z == 1) | (z == 2)

    def when(condition, action):
        @pl.when(condition)
        def _():
            action()

    heads = ((qk_ref, lambda at, side: qks_ref.at[at, (core + side) % 2], 0), (out_ref, lambda at, side: outs_ref.at[side, at], 1))

    def head_hop(at, number, peer, own=False):
        for ref, slot, k in heads:
            wires.start(ref if own else slot(at, 0), slot(at, 0), number + k, peer)

    def head_in(at, number, peer):
        for _, slot, k in heads:
            wires.arrived(slot(at, 0), number + k, peer)

    def head_over(at, number):
        for ref, slot, k in heads:
            target = qks_ref.at[at, core] if k == 0 else outs_ref.at[1, at]
            wires.start(slot(at, 0), target, number + k, sibling)

    def head_back(at, number):
        for _, slot, k in heads:
            wires.arrived(slot(at, 1), number + k, sibling)

    blocks[pl.ds(z, 1)] = cot_ref[...][None]
    downs_ref[0, pl.ds(z, 1), pl.ds(me, 1)] = down_ref[...][None, None]
    keeps = [pltpu.make_async_copy(ref, slot(z, 0), local_sems.at[k]) for ref, slot, k in heads]
    for keep in keeps:
        keep.start()

    for r in (1, 2, 3):
        wires.start(down_ref, downs_ref.at[0, z, me], r, turns[r - 1])
    wires.start(down_ref, downs_ref.at[1, z, me], 4, sibling)
    when(z < 2, lambda: wires.start(cot_ref, blocks.at[z], 0, up))
    when(z > 1, lambda: wires.start(cot_ref, blocks.at[z], 5, down))
    when((z == 0) | (z == 2), lambda: head_hop(z, 6, up, True))
    when((z == 1) | (z == 3), lambda: head_hop(z, 8, down, True))
    when((z == 0) | (z == 2), lambda: wires.start(part_ref, above_ref, 48, up))
    when((z == 1) | (z == 3), lambda: wires.start(part_ref, below_ref, 49, down))
    for keep in keeps:
        keep.wait()
    head_over(z, 10)

    for r in (1, 2, 3):
        wires.arrived(downs_ref.at[0, (z + 4 - r) % 4, me], r, turns[r - 1])
    relay, neighbours, finish, leave_downs = gather_square(
        lambda position, k: downs_ref.at[0, pl.ds(2 * k, 2), position],
        [downs_ref.at[0, pl.ds(2 * k, 2), me] for k in range(2)],
        wires,
        12,
    )
    for r in (1, 2, 3):
        here = (z + r) % 4
        wires.start(downs_ref.at[0, here, me], downs_ref.at[1, here, me], 17 + r, sibling)

    @pl.when(inner)
    def _():
        wires.arrived(blocks.at[z - 1], 0, down)
        wires.arrived(blocks.at[z + 1], 5, up)

    @pl.when(z == 1)
    def _():
        wires.start(blocks.at[0], blocks.at[0], 21, up)
        head_hop(z, 6, up, True)
        head_in(0, 6, down)
        head_hop(0, 22, up)
        wires.start(part_ref, above_ref, 48, up)
        head_over(0, 24)

    @pl.when(z == 2)
    def _():
        wires.start(blocks.at[3], blocks.at[3], 21, down)
        head_hop(z, 8, down, True)
        head_in(3, 8, up)
        head_hop(3, 22, down)
        wires.start(part_ref, below_ref, 49, down)
        head_over(3, 24)

    relay()
    neighbours()
    wires.start(downs_ref.at[0, :, beside], downs_ref.at[1, :, beside], 26, sibling)
    wires.start(downs_ref.at[0, :, across], downs_ref.at[1, :, across], 27, sibling)
    finish()
    wires.start(downs_ref.at[0, :, corner], downs_ref.at[1, :, corner], 28, sibling)
    wires.arrived(downs_ref.at[1, z, me], 4, sibling)
    for r in (1, 2, 3):
        wires.arrived(downs_ref.at[1, (z + r) % 4, me], 17 + r, sibling)
    for number, position in ((26, beside), (27, across), (28, corner)):
        wires.arrived(downs_ref.at[1, :, position], number, sibling)

    kv = all_ref.shape[1] - LANE
    used = kv + ROPE
    tail = jnp.concatenate([downs_ref[k, :, :, :, kv:].reshape(half, LANE) for k in range(2)], axis=0).astype(F32).T
    gains_ref[...] = tail[ROPE : ROPE + 8]
    lead = tail[ROPE : ROPE + 8].astype(LOW)
    small = 0.0
    chunk = 4 * LANE
    for a in range(0, width, chunk):
        row = lax.broadcasted_iota(jnp.int32, (chunk, spot_ref.shape[1]), 0) + a
        here = jnp.where(row == spot_ref[...], 1.0, 0.0).astype(LOW)
        small = small + dot(lead[:, a : a + chunk], here)
    small = small[2:3]
    gain = tail[ROPE : ROPE + 1]

    def normed_step(step, carry):
        here = pl.ds(pl.multiple_of(step * ROW_STEP, ROW_STEP), ROW_STEP)
        store_line(x_ref, here, input_ref[here, :].astype(F32), core)
        value = x_ref[here, :].astype(F32)
        factor = lax.rsqrt(jnp.mean(value * value, axis=-1, keepdims=True) + EPSILON)
        normed_ref[here, :] = (value * factor * gain).astype(LOW)
        return carry

    lax.fori_loop(0, size // ROW_STEP, normed_step, 0)
    for a in range(0, kv + LANE, 3 * LANE):
        b = min(a + 3 * LANE, kv + LANE)
        total = 0.0
        for k in range(2):
            total = total + dot(normed_ref[:, k * half : (k + 1) * half], downs_ref[k, :, :, :, a:b].reshape(half, b - a))
        latents_ref[:, a:b] = total
    low = lax.broadcasted_iota(jnp.int32, (1, LANE), 1) < ROPE
    cuts = ((0, kv - KR), (kv - KR, kv))

    def latent_step(step, carry):
        here = pl.ds(pl.multiple_of(step * ROW_STEP, ROW_STEP), ROW_STEP)
        mine = pl.ds(pl.multiple_of(me * size + step * ROW_STEP, ROW_STEP), ROW_STEP)
        for a, b in cuts:
            value = latents_ref[here, a:b]
            factor = lax.rsqrt(jnp.mean(value * value, axis=-1, keepdims=True) + EPSILON)
            all_ref[mine, a:b] = (value * factor * small[:, a:b]).astype(LOW)
        rope = pltpu.roll(jnp.where(low, latents_ref[here, kv:], 0.0), NOPE, 1)
        rope = (
            rope * cos_ref[here, :]
            + pltpu.roll(rope, ROPE // 2, 1) * lift_ref[here, :]
            + pltpu.roll(rope, LANE - ROPE // 2, 1) * drop_ref[here, :]
        )
        all_ref[mine, kv:] = rope.astype(LOW)
        return carry

    lax.fori_loop(0, size // ROW_STEP, latent_step, 0)
    cut = (kv + LANE) // LANE // 2 * LANE
    columns = (pl.ds(0, cut), pl.ds(cut, kv + LANE - cut))
    relay, neighbours, finish, leave_latents = gather_square(
        lambda position, k: all_ref.at[rows_of(position, size), columns[k]],
        [all_ref.at[rows_of(me, size), columns[k]] for k in range(2)],
        wires,
        30,
    )

    when(z == 2, lambda: wires.arrived(blocks.at[0], 21, down))
    when(z == 1, lambda: wires.arrived(blocks.at[3], 21, up))
    end = jnp.where(z == 2, 6, 0)
    inner_want, inner_asked = sources_ref[end + core], sources_ref[end + 1 - core]
    want, asked = sources_ref[2 * z + core], sources_ref[2 * z + 1 - core]
    stage[0] = blocks[inner_asked // 2]
    wires.start(stage.at[0], theirs.at[0], 36, sibling)
    stage[1] = jnp.where(edge, cot_ref[...], blocks[asked // 2])
    wires.start(stage.at[1], theirs.at[1], 37, sibling)
    wires.arrived(theirs.at[0], 36, sibling)
    stage[2] = jnp.where(inner_want % 2 == core, blocks[inner_want // 2], theirs[0])
    when(z == 2, lambda: wires.start(stage.at[2], got, 38, up))
    when(z == 1, lambda: wires.start(stage.at[2], got, 38, down))
    relay()
    neighbours()
    finish()

    @pl.when(z == 1)
    def _():
        head_in(2, 8, up)
        head_hop(2, 40, down)
        head_over(2, 42)
        head_in(3, 22, up)
        head_hop(3, 44, down)
        head_over(3, 46)

    @pl.when(z == 2)
    def _():
        head_in(1, 6, down)
        head_hop(1, 40, up)
        head_over(1, 42)
        head_in(0, 22, down)
        head_hop(0, 44, up)
        head_over(0, 46)

    when(z == 0, lambda: wires.arrived(got, 38, up))
    when(z == 3, lambda: wires.arrived(got, 38, down))
    wires.arrived(theirs.at[1], 37, sibling)

    def rows_step(step, carry):
        here = pl.ds(pl.multiple_of(step * ROW_STEP, ROW_STEP), ROW_STEP)
        mine = jnp.where(edge, cot_ref[here, :], blocks[want // 2, here, :])
        local = jnp.where(want % 2 == core, mine, theirs[1, here, :])
        value = jnp.where(edge & (want // 2 != z), got[here, :], local).astype(F32)
        position = me * size + step * ROW_STEP + lax.broadcasted_iota(jnp.int32, (ROW_STEP, 1), 0)
        value = jnp.where(position < length_ref[0], value, 0.0)
        store_line(own_cot_ref, here, value, core)
        store_line(scaled, here, RESIDUAL_SCALE * value, core)
        return carry

    lax.fori_loop(0, size // ROW_STEP, rows_step, 0)

    keep_cot = pltpu.make_async_copy(scaled, cots_ref.at[rows_of(me, size), :], local_sems.at[2])
    keep_cot.start()
    halves = (pl.ds(0, half), pl.ds(half, half))
    relay, neighbours, finish, leave_cots = gather_square(
        lambda position, k: cots_ref.at[rows_of(position, size), halves[k]],
        [scaled.at[:, halves[k]] for k in range(2)],
        wires,
        50,
    )

    @pl.when(z == 0)
    def _():
        head_in(1, 8, up)
        head_over(1, 24)
        head_in(2, 40, up)
        head_over(2, 42)

    @pl.when(z == 3)
    def _():
        head_in(2, 6, down)
        head_over(2, 24)
        head_in(1, 40, down)
        head_over(1, 42)

    relay()

    @pl.when(z == 0)
    def _():
        head_in(3, 44, up)
        head_over(3, 46)

    @pl.when(z == 3)
    def _():
        head_in(0, 44, down)
        head_over(0, 46)


    head_back(z, 10)
    when(z == 1, lambda: [head_back(at, number) for at, number in ((0, 24), (2, 42), (3, 46))])
    when(z == 2, lambda: [head_back(at, number) for at, number in ((3, 24), (1, 42), (0, 46))])
    when(z == 0, lambda: [head_back(at, number) for at, number in ((1, 24), (2, 42), (3, 46))])
    when(z == 3, lambda: [head_back(at, number) for at, number in ((2, 24), (1, 42), (0, 46))])

    neighbours()
    finish()
    keep_cot.wait()
    when(z > 0, lambda: wires.arrived(above_ref, 48, down))
    when(z < 3, lambda: wires.arrived(below_ref, 49, up))

    leave_cots()
    when(z < 3, lambda: wires.sent(part_ref, 48, up))
    when(z > 0, lambda: wires.sent(part_ref, 49, down))
    for number in (1, 2, 3, 4, 18, 19, 20):
        wires.sent(down_ref, number, sibling)
    leave_downs()
    for number in (26, 27, 28):
        wires.sent(downs_ref.at[0, :, me], number, sibling)
    leave_latents()
    for number in (36, 37):
        wires.sent(stage.at[0], number, sibling)

    def head_sent(*numbers):
        for number in numbers:
            for ref, _, k in heads:
                wires.sent(ref, number + k, sibling)

    head_sent(10, 24, 42, 46)
    when(z < 2, lambda: wires.sent(cot_ref, 0, sibling))
    when(z > 1, lambda: wires.sent(cot_ref, 5, sibling))
    when(z < 3, lambda: head_sent(6))
    when(z > 0, lambda: head_sent(8))

    @pl.when(inner)
    def _():
        wires.sent(cot_ref, 21, sibling)
        wires.sent(cot_ref, 38, sibling)
        head_sent(22, 40, 44)


def bring(sources, length, down_pack, qk_pack, out_pack, cot, values, spot, tables, part):
    size, width = cot.shape
    columns = down_pack.shape[1]
    vmem, anywhere = pl.BlockSpec(memory_space=pltpu.VMEM), pl.BlockSpec(memory_space=pl.ANY)
    smem = pl.BlockSpec(memory_space=pltpu.SMEM)
    return pl.pallas_call(
        bring_kernel,
        in_specs=[smem, smem] + [vmem] * 9 + [anywhere],
        out_specs=[vmem, anywhere, anywhere] + [vmem] * 5 + [anywhere] * 3 + [vmem],
        out_shape=[
            jax.ShapeDtypeStruct((2, 4, PLANE) + down_pack.shape, LOW),
            jax.ShapeDtypeStruct((4, 2) + qk_pack.shape, LOW),
            jax.ShapeDtypeStruct((2, 4) + out_pack.shape, LOW),
            jax.ShapeDtypeStruct((size, width), LOW),
            jax.ShapeDtypeStruct((size, width), LOW),
            jax.ShapeDtypeStruct((size, columns), F32),
            jax.ShapeDtypeStruct((8, width), F32),
            jax.ShapeDtypeStruct((PLANE * size, columns), LOW),
            jax.ShapeDtypeStruct((PLANE * size, width), LOW),
            jax.ShapeDtypeStruct(part.shape, LOW),
            jax.ShapeDtypeStruct(part.shape, LOW),
            jax.ShapeDtypeStruct((size, width), LOW),
        ],
        scratch_shapes=[
            pltpu.VMEM((size, width), LOW),
            pltpu.VMEM((4, size, width), LOW),
            pltpu.VMEM((size, width), LOW),
            pltpu.VMEM((2, size, width), LOW),
            pltpu.VMEM((3, size, width), LOW),
            pltpu.SemaphoreType.DMA((56,)),
            pltpu.SemaphoreType.DMA((56,)),
            pltpu.SemaphoreType.DMA((3,)),
        ],
        compiler_params=pltpu.CompilerParams(collective_id=7, has_side_effects=True, vmem_limit_bytes=56 << 20),
        cost_estimate=pl.CostEstimate(flops=0, bytes_accessed=480 << 20, transcendentals=0),
        name="bring",
    )(sources, length, down_pack, qk_pack, out_pack, cot, values, spot, *tables, part)


def finish_kernel(
    sources_ref,
    qcot_ref,
    kvcot_ref,
    rope_ref,
    weight_ref,
    lat_ref,
    latents_ref,
    smalls_ref,
    cos_ref,
    lift_ref,
    drop_ref,
    x_ref,
    normed_ref,
    downs_ref,
    gain_ref,
    after_grad_ref,
    mlp_dgain_ref,
    own_ref,
    down_ref,
    head_ref,
    dealt_ref,
    input_ref,
    gains,
    query_ref,
    key_ref,
    part0,
    part1,
    got2,
    got3,
    cot_ref,
    gains_came,
    grad_block,
    keep,
    away,
    came,
    got0,
    got1,
    line,
    lines,
    head_came,
    head_part,
    head_lines,
    blocks,
    theirs,
    stage,
    send_sems,
    recv_sems,
    square_send,
    square_recv,
    local_sems,
):
    z, core, sibling = line_peers()
    me, beside, across, corner = square()
    wires = Wires(send_sems, recv_sems)
    turns = [line_peer((z + r) % 4, core) for r in (1, 2, 3)]
    greet_all([sibling, {"tp": beside}, {"tp": across}] + turns)
    up, down = line_peer((z + 1) % 4, core), line_peer((z + 3) % 4, core)
    edge = (z == 0) | (z == 3)
    half = normed_ref.shape[1] // 2
    used = cot_ref.shape[1]
    size = normed_ref.shape[0]
    groups, rows_all, columns = weight_ref.shape
    q_rows = query_ref.shape[2]
    qr = groups * q_rows
    kv = lat_ref.shape[1] - LANE
    slim = part0.shape[1]

    keep_own = pltpu.make_async_copy(own_ref, blocks.at[z], local_sems.at[0])
    keep_own.start()

    @pl.when(z < 2)
    def _():
        wires.start(own_ref, blocks.at[z], 0, up)

    @pl.when(z > 1)
    def _():
        wires.start(own_ref, blocks.at[z], 12, down)

    w_query = weight_ref[:, :q_rows].reshape(qr, columns)
    w_pair = weight_ref[:, q_rows:].reshape(groups * (rows_all - q_rows), columns)

    def prepare(position):
        here = rows_of(position, size)
        back = dot_nt(qcot_ref[here, :], w_query)
        part0[here, :] = back[:, :slim].astype(LOW)
        part1[here, 0 : qr - slim] = back[:, slim:].astype(LOW)
        part1[here, qr - slim : kv - slim] = dot_nt(kvcot_ref[here, :], w_pair).astype(LOW)
        part1[here, kv - slim :] = rope_ref[here, :]

    def head_gradients():
        for i in range(4):
            for c in range(2):
                g = 2 * i + c
                if g % 4 == 0:
                    grads = dot_tn(lat_ref[:, g * q_rows : (g + 4) * q_rows], qcot_ref[...]).astype(LOW)
                query_ref[i, c] = grads[(g % 4) * q_rows : (g % 4 + 1) * q_rows]
        pair_rows = rows_all - q_rows
        grads = dot_tn(lat_ref[:, qr:kv], kvcot_ref[...]).astype(LOW)
        for i in range(4):
            for c in range(2):
                g = 2 * i + c
                key_ref[i, c] = grads[g * pair_rows : (g + 1) * pair_rows]
        wires.start(query_ref.at[:, 1 - core], head_came.at[:, pl.ds(0, q_rows)], 1, sibling)
        wires.start(key_ref.at[:, 1 - core], head_came.at[:, pl.ds(q_rows, pair_rows)], 2, sibling)

    copies = reduce_square(
        (part0, part1),
        (got2, got3),
        (square_send.at[pl.ds(6, 6)], square_recv.at[pl.ds(6, 6)]),
        prepare,
        head_gradients,
    )
    gains[...] = jnp.zeros_like(gains)
    keep_own.wait()

    @pl.when((z == 1) | (z == 2))
    def _():
        wires.arrived(blocks.at[z - 1], 0, down)
        wires.arrived(blocks.at[z + 1], 12, up)

    @pl.when(z == 1)
    def _():
        wires.start(blocks.at[0], blocks.at[0], 19, up)

    @pl.when(z == 2)
    def _():
        wires.start(blocks.at[3], blocks.at[3], 19, down)

    end = jnp.where(z == 2, 6, 0)
    inner_want, inner_asked = sources_ref[end + core], sources_ref[end + 1 - core]
    want, asked = sources_ref[2 * z + core], sources_ref[2 * z + 1 - core]

    def last_hop():
        @pl.when(z == 2)
        def _():
            wires.arrived(blocks.at[0], 19, down)

        @pl.when(z == 1)
        def _():
            wires.arrived(blocks.at[3], 19, up)

        stage[0] = blocks[inner_asked // 2]
        wires.start(stage.at[0], theirs.at[0], 10, sibling)
        stage[1] = jnp.where(edge, blocks[z], blocks[asked // 2])
        wires.start(stage.at[1], theirs.at[1], 11, sibling)
        wires.arrived(theirs.at[0], 10, sibling)
        wires.sent(stage.at[0], 10, sibling)
        stage[0] = jnp.where(inner_want % 2 == core, blocks[inner_want // 2], theirs[0])

        @pl.when(z == 2)
        def _():
            wires.start(stage.at[0], dealt_ref, 20, up)

        @pl.when(z == 1)
        def _():
            wires.start(stage.at[0], dealt_ref, 20, down)

    def latent_step(step, carry):
        here = pl.ds(pl.multiple_of(step * ROW_STEP, ROW_STEP), ROW_STEP)
        mine = pl.ds(pl.multiple_of(me * size + step * ROW_STEP, ROW_STEP), ROW_STEP)
        total = jnp.concatenate(
            [
                part[mine, :].astype(F32) + come[1, here, :].astype(F32) + come[2, here, :].astype(F32)
                for part, come in ((part0, got2), (part1, got3))
            ],
            axis=1,
        )
        for a, b in ((0, qr), (qr, kv)):
            grad, value = total[:, a:b], latents_ref[here, a:b]
            factor = lax.rsqrt(jnp.mean(value * value, axis=-1, keepdims=True) + EPSILON)
            weighted = grad * smalls_ref[:, a:b]
            inside = jnp.mean(weighted * value, axis=-1, keepdims=True)
            gains[2:3, a:b] += jnp.sum(grad * value * factor, axis=0, keepdims=True)
            cot_ref[here, a:b] = (factor * weighted - value * (factor * factor * factor) * inside).astype(LOW)
        rope = total[:, kv:]
        rope = (
            rope * cos_ref[here, :]
            - pltpu.roll(rope, ROPE // 2, 1) * lift_ref[here, :]
            - pltpu.roll(rope, LANE - ROPE // 2, 1) * drop_ref[here, :]
        )
        cot_ref[here, kv:] = pltpu.roll(rope, NOPE, 1)[:, : used - kv].astype(LOW)
        return carry

    lax.fori_loop(0, size // ROW_STEP, latent_step, 0)
    rows = keep.shape[0] // 16
    block = half // 4

    def gradients(k, target):
        for pair in range(2):
            a = k * half + pair * 2 * block
            grads = dot_tn(normed_ref[:, a : a + 2 * block], cot_ref[...]).astype(LOW)
            for i in range(2):
                for t in range(PLANE):
                    row = (t * 4 + pair * 2 + i) * rows
                    target[row : row + rows, :] = grads[i * block + t * rows : i * block + (t + 1) * rows]

    gradients(1, away)
    wires.start(away, came, 3, sibling)
    gradients(0, keep)

    wires.arrived(head_came.at[:, pl.ds(0, q_rows)], 1, sibling)
    wires.arrived(head_came.at[:, pl.ds(q_rows, key_ref.shape[2])], 2, sibling)
    for i in range(4):
        for ref, a in ((query_ref, 0), (key_ref, q_rows)):
            b = a + ref.shape[2]
            head_part[i, a:b] = (ref[i, core].astype(F32) + head_came[i, a:b].astype(F32)).astype(LOW)
    for r in (1, 2, 3):
        wires.start(head_part.at[(z + r) % 4], head_lines.at[r - 1], 3 + r, turns[r - 1])
    wires.arrived(came, 3, sibling)

    def add_step(step, carry):
        here = pl.ds(pl.multiple_of(step * rows, 16), rows)
        keep[here, :] = (keep[here, :].astype(F32) + came[here, :].astype(F32)).astype(LOW)
        return carry

    lax.fori_loop(0, 16, add_step, 0)
    cut = got0.shape[2]
    parts = (keep.at[:, pl.ds(0, cut)], keep.at[:, pl.ds(cut, used - cut)])
    input_rows = grad_block.shape[0]

    def input_gradient():
        last_hop()

        def input_step(step, carry):
            here = pl.ds(pl.multiple_of(step * input_rows, input_rows), input_rows)
            bring_block = pltpu.make_async_copy(after_grad_ref.at[here, :], grad_block, local_sems.at[3])
            bring_block.start()
            cot = cot_ref[here, :]
            grad = jnp.concatenate([dot_nt(cot, downs_ref[k, :, :used]) for k in range(2)], axis=1)
            value = x_ref[here, :].astype(F32)
            factor = lax.rsqrt(jnp.mean(value * value, axis=-1, keepdims=True) + EPSILON)
            weighted = grad * gain_ref[...]
            inside = jnp.mean(weighted * value, axis=-1, keepdims=True)
            gains[0:1, :] += jnp.sum(grad * value * factor, axis=0, keepdims=True)
            total = factor * weighted - value * (factor * factor * factor) * inside
            bring_block.wait()
            total = total + grad_block[...]
            first, second = total[:, :half], total[:, half:]
            evens, odds = jnp.where(core == 0, first, second), jnp.where(core == 0, second, first)
            for i in range(4):
                piece = slice(i * block, (i + 1) * block)
                input_ref[here, 2 * i * block : (2 * i + 1) * block] = evens[:, piece].astype(LOW)
                input_ref[here, (2 * i + 1) * block : (2 * i + 2) * block] = odds[:, piece].astype(LOW)
            return carry

        lax.fori_loop(0, size // input_rows, input_step, 0)
        gains[1:2, :] = mlp_dgain_ref[...]
        for row in range(2):
            first, second = gains[row : row + 1, :half], gains[row : row + 1, half:]
            gains[row : row + 1, :half] = jnp.where(core == 0, first, second)
            gains[row : row + 1, half:] = jnp.where(core == 0, second, first)
        wires.start(gains, gains_came.at[0], 13, sibling)

    copies += reduce_square(
        parts,
        (got0, got1),
        (square_send.at[pl.ds(0, 6)], square_recv.at[pl.ds(0, 6)]),
        lambda position: None,
        input_gradient,
    )
    for k, (a, b) in enumerate(((0, cut), (cut, used))):
        got_k = (got0, got1)[k]
        total = keep[rows_of(me, 4 * rows), a:b].astype(F32) + got_k[1].astype(F32) + got_k[2].astype(F32)
        line[:, a:b] = total.astype(LOW)
    for r in (1, 2, 3):
        wires.start(line.at[rows_of((z + r) % 4, rows), :], lines.at[r - 1], 6 + r, turns[r - 1])

    for number, (slot, peer) in enumerate(((0, sibling), (1, {"tp": beside}), (2, {"tp": across}))):
        wires.arrived(gains_came.at[slot], 13 + number, peer)
        wires.sent(gains, 13 + number, peer)
        gains[...] += gains_came[slot]
        if number < 2:
            wires.start(gains, gains_came.at[slot + 1], 14 + number, ({"tp": beside}, {"tp": across})[number])
    for r in (1, 2, 3):
        wires.start(gains, gains_came.at[2 + r], 15 + r, turns[r - 1])
    for r in (1, 2, 3):
        wires.arrived(head_lines.at[r - 1], 3 + r, turns[r - 1])
    head_ref[...] = head_part[z].astype(F32) + (
        head_lines[0].astype(F32) + head_lines[1].astype(F32) + head_lines[2].astype(F32)
    )
    for r in (1, 2, 3):
        wires.arrived(lines.at[r - 1], 6 + r, turns[r - 1])
    down_ref[...] = line[rows_of(z, rows), :].astype(F32) + (
        lines[0].astype(F32) + lines[1].astype(F32) + lines[2].astype(F32)
    )
    for r in (1, 2, 3):
        wires.arrived(gains_came.at[2 + r], 15 + r, turns[r - 1])
    for r in (1, 2, 3):
        wires.sent(gains, 15 + r, turns[r - 1])
    gains[...] += gains_came[3] + (gains_came[4] + gains_came[5])
    wires.arrived(theirs.at[1], 11, sibling)

    @pl.when(z == 3)
    def _():
        wires.arrived(dealt_ref, 20, down)

    @pl.when(z == 0)
    def _():
        wires.arrived(dealt_ref, 20, up)

    mine = jnp.where(edge, blocks[z], blocks[want // 2])
    local = jnp.where(want % 2 == core, mine, theirs[1])
    dealt_ref[...] = jnp.where(edge & (want // 2 != z), dealt_ref[...], local)
    for copy in copies:
        copy.wait_send()
    wires.sent(query_ref.at[:, 0], 1, sibling)
    wires.sent(key_ref.at[:, 0], 2, sibling)
    wires.sent(away, 3, sibling)
    for r in (1, 2, 3):
        wires.sent(head_part.at[0], 3 + r, sibling)
        wires.sent(line.at[pl.ds(0, rows), :], 6 + r, sibling)
    wires.sent(stage.at[1], 11, sibling)

    @pl.when(z < 2)
    def _():
        wires.sent(own_ref, 0, sibling)

    @pl.when(z > 1)
    def _():
        wires.sent(own_ref, 12, sibling)

    @pl.when((z == 1) | (z == 2))
    def _():
        wires.sent(stage.at[0], 19, sibling)
        wires.sent(stage.at[0], 20, sibling)


def finish_all(sources, cots, rope, weights, q_rows, lat, latents, smalls, tables, values, normed, downs, gain, grad, dgain, own):
    size, width = normed.shape
    used = lat.shape[1] - LANE + ROPE
    rows = width // (LINE * PLANE)
    groups, head_rows, columns = weights.shape
    slim = lat.shape[1] // LANE // 2 * LANE + LANE
    cut = used // LANE // 2 * LANE
    vmem, smem = pl.BlockSpec(memory_space=pltpu.VMEM), pl.BlockSpec(memory_space=pltpu.SMEM)
    anywhere = pl.BlockSpec(memory_space=pl.ANY)
    mine, other = (4, 2, q_rows, columns), (4, 2, head_rows - q_rows, columns)
    return pl.pallas_call(
        finish_kernel,
        in_specs=[smem] + [vmem] * 14 + [anywhere, vmem, anywhere],
        out_specs=[vmem] * 5,
        out_shape=[
            jax.ShapeDtypeStruct((rows, used), F32),
            jax.ShapeDtypeStruct((head_rows, columns), F32),
            jax.ShapeDtypeStruct((size, width), LOW),
            jax.ShapeDtypeStruct((size, width), LOW),
            jax.ShapeDtypeStruct((8, width), F32),
        ],
        scratch_shapes=[
            pltpu.VMEM(mine, LOW),
            pltpu.VMEM(other, LOW),
            pltpu.VMEM((lat.shape[0], slim), LOW),
            pltpu.VMEM((lat.shape[0], lat.shape[1] - slim), LOW),
            pltpu.VMEM((3, size, slim), LOW),
            pltpu.VMEM((3, size, lat.shape[1] - slim), LOW),
            pltpu.VMEM((size, used), LOW),
            pltpu.VMEM((6, 8, width), F32),
            pltpu.VMEM((256, width), F32),
        ]
        + [pltpu.VMEM((16 * rows, used), LOW)] * 3
        + [
            pltpu.VMEM((3, 4 * rows, cut), LOW),
            pltpu.VMEM((3, 4 * rows, used - cut), LOW),
            pltpu.VMEM((4 * rows, used), LOW),
            pltpu.VMEM((3, rows, used), LOW),
            pltpu.VMEM((4, head_rows, columns), LOW),
            pltpu.VMEM((4, head_rows, columns), LOW),
            pltpu.VMEM((3, head_rows, columns), LOW),
            pltpu.VMEM((4, size, width), LOW),
            pltpu.VMEM((2, size, width), LOW),
            pltpu.VMEM((2, size, width), LOW),
            pltpu.SemaphoreType.DMA((21,)),
            pltpu.SemaphoreType.DMA((21,)),
            pltpu.SemaphoreType.DMA((12,)),
            pltpu.SemaphoreType.DMA((12,)),
            pltpu.SemaphoreType.DMA((4,)),
        ],
        compiler_params=pltpu.CompilerParams(collective_id=8, has_side_effects=True, vmem_limit_bytes=67 * 10**6),
        cost_estimate=pl.CostEstimate(flops=0, bytes_accessed=240 << 20, transcendentals=0),
        name="finish",
    )(sources, *cots, rope, weights, lat, latents, smalls, *tables, values, normed, downs, gain, grad, dgain, own)


def per_device(
    block_input,
    seq_lengths,
    dealt_order,
    out_cotangent,
    attn_gain,
    query_down,
    query_gain,
    latent_down,
    latent_gain,
    query_up,
    latent_up,
    output_matrix,
    mlp_gain,
    gate_weight,
    up_weight,
    down_matrix,
):
    line = special()
    tp_count = lax.axis_size("tp")
    fsdp_count = lax.axis_size("fsdp")
    group = lax.axis_index("fsdp")
    column = lax.axis_index("tp")
    _, local_len, width = block_input.shape
    full_len = local_len * tp_count
    own_len = jnp.take(seq_lengths, group)
    local_pos = column * local_len + jnp.arange(local_len, dtype=jnp.int32)
    valid = (local_pos < own_len).astype(F32)[:, None]
    order = to_line if line else (lambda values: values)
    unorder = from_line if line else (lambda values: values)
    bounds = [(0, width // 2), (width // 2, width)] if line else [(0, width)]

    qr = query_down.shape[1]
    latent_rows = query_down.shape[0]
    small_q, small_l = query_gain.shape[0], latent_gain.shape[0]
    used = qr + KR + ROPE
    padded = -(-(used + 3) // LANE) * LANE
    small = jnp.concatenate([query_gain, latent_gain, jnp.zeros((latent_rows,), F32)])
    if small_q + small_l <= latent_rows:
        small = small[:latent_rows]
        extra = 0
    else:
        small = small[: 2 * latent_rows]
        extra = 1
    down_pack = jnp.concatenate(
        [
            query_down.astype(LOW),
            latent_down.astype(LOW),
            attn_gain.astype(LOW)[:, None],
            mlp_gain.astype(LOW)[:, None],
            small.astype(LOW).reshape(1 + extra, latent_rows).T,
            jnp.zeros((latent_rows, padded - used - 3 - extra), LOW),
        ],
        axis=1,
    )

    heads = query_up.shape[1] // QKD
    even = heads + heads % 2
    q_rows, l_rows = query_up.shape[0], latent_up.shape[0]
    o_rows = output_matrix.shape[0] // 2
    half_width = even * VD

    def pad_heads(values, size, to):
        rows = values.shape[0]
        values = values.reshape(rows, heads, size)
        return jnp.pad(values, ((0, 0), (0, even - heads), (0, to - size))).reshape(rows, even * to)

    out_low = pad_heads(output_matrix.astype(LOW), VD, VD)
    qk_pack = jnp.concatenate([pad_heads(query_up.astype(LOW), QKD, LANE), pad_heads(latent_up.astype(LOW), LANE, LANE)], axis=0)
    units = gate_weight.shape[1]
    cut = 768 if units == 1600 else units // 2
    pieces = [(0, cut), (cut, units)]
    if line:
        tiles = []
        for a in range(0, units, UNIT):
            b = min(a + UNIT, units)
            tiles.append([weight[:, a:b].astype(LOW) for weight in (gate_weight, up_weight, down_matrix)])
        tiles[-1].append(jnp.zeros((gate_weight.shape[0], -3 * (units % UNIT) % LANE), LOW))
        mlp_packs = [jnp.concatenate(sum(part, []), axis=1) for part in (tiles[:3], tiles[3:])]
    else:
        mlp_packs = [
            jnp.concatenate(
                [gate_weight[:, a:b].astype(LOW), up_weight[:, a:b].astype(LOW), down_matrix[:, a:b].astype(LOW)], axis=1
            )
            for a, b in pieces
        ]
    cot_source = jnp.argsort(dealt_order).astype(jnp.int32)
    if line:
        owners = jnp.arange(fsdp_count * tp_count, dtype=jnp.int32)[:, None]
        spot = jnp.concatenate(
            [
                (owners * latent_rows + jnp.arange(small_q, dtype=jnp.int32)).reshape(-1),
                (owners * latent_rows + small_q + jnp.arange(small_l, dtype=jnp.int32)).reshape(-1),
            ]
        )
        block = width // LINE
        index = spot // block
        spot = ((index % 2) != group % 2) * (width // 2) + index // 2 * block + spot % block
        own_tables = head_tables(*rotary_tables(local_pos))
        downs, natural, out_slabs, own_cot, normed_low, latents, gain_rows, latent_all, mlp_cot, above, below, block_low = bring(
            cot_source,
            own_len[None],
            down_pack,
            qk_pack,
            out_low,
            out_cotangent[0],
            block_input[0],
            spot[None],
            own_tables,
            mlp_packs[0],
        )
        first_steps = [above, below, gather_two(above, below)]
        down_all = downs.reshape(width, padded)
        grad_out = own_cot
        out_slabs = [slab.reshape(width // 2, half_width) for slab in out_slabs]
        first_low = mlp_packs[0]
        gain_attn, gain_mlp = gain_rows[0], gain_rows[1]
        smalls = gain_rows[2].reshape(2, 4, -1)
        smalls = jnp.stack(by_core(smalls[0], smalls[1]), axis=1).reshape(-1, latent_rows)
        natural = natural.reshape(fsdp_count, q_rows + l_rows, -1)
    else:
        down_all = lax.all_gather(down_pack, ("fsdp", "tp"), axis=0, tiled=True)
        natural = lax.all_gather(qk_pack, "fsdp")
        out_slabs = [lax.all_gather(out_low, "fsdp", axis=0, tiled=True)]
        mlp_slabs = [[lax.all_gather(pack, "fsdp", axis=0, tiled=True)] for pack in mlp_packs]
        grad_out = valid * deal_plain(out_cotangent[0], cot_source).astype(F32)
        mlp_cot = lax.all_gather((RESIDUAL_SCALE * grad_out).astype(LOW), "tp", axis=0, tiled=True)
        gain_attn = down_all[:, used].astype(F32)
        gain_mlp = down_all[:, used + 1].astype(F32)
        smalls = down_all[:, used + 2 : used + 3 + extra].astype(F32).reshape(-1, latent_rows, 1 + extra)
        smalls = jnp.swapaxes(smalls, 1, 2).reshape(-1, latent_rows * (1 + extra))
        block_low = block_input[0]
    w_qup = natural[:, :q_rows].reshape(-1, even * LANE)
    w_kvup = natural[:, q_rows:].reshape(-1, even * LANE)
    w_down = down_all[:, :used]
    gain_query = smalls[:, :small_q].reshape(-1)
    gain_latent = smalls[:, small_q : small_q + small_l].reshape(-1)

    block_vals = block_low.astype(F32)
    cos_local, sin_local = rotary_tables(local_pos)
    cos_local = jnp.concatenate([cos_local, cos_local], axis=1)
    sin_local = jnp.concatenate([sin_local, sin_local], axis=1)
    if not line:
        normed_low = normalize(block_vals, gain_attn)[0].astype(LOW)
        latents = dot(normed_low, w_down)
        rope_raw = latents[:, qr + KR :]
        rotary_key = rope_raw * cos_local + turn_half(rope_raw) * sin_local
        rotary_key = jnp.pad(rotary_key, ((0, 0), (NOPE, LANE - NOPE - ROPE)))
        parts = [
            normalize(latents[:, :qr], gain_query)[0],
            normalize(latents[:, qr : qr + KR], gain_latent)[0],
            rotary_key,
        ]
        latent_all = lax.all_gather(jnp.concatenate(parts, axis=1).astype(LOW), "tp", axis=0, tiled=True)
    query_latent, kv_latent = latents[:, :qr], latents[:, qr : qr + KR]

    def factor_of(values):
        return lax.rsqrt(jnp.mean(values * values, axis=-1, keepdims=True) + EPSILON)

    query_all = latent_all[:, :qr]
    comp_all = latent_all[:, qr : qr + KR]
    rope_all = latent_all[:, qr + KR :]

    tables = head_tables(*rotary_tables(jnp.arange(full_len, dtype=jnp.int32)))
    bias = jnp.where(jnp.arange(full_len, dtype=jnp.int32) < own_len, 0.0, MASKED).astype(F32)[None, :]
    queries, key_value, mixed, lse = attend(latent_all, natural, q_rows, bias, tables)
    if line:
        mixed, first_steps[2], second_low = tie(mixed, first_steps[2], mlp_packs[1])
        second_steps = list(gather_one(second_low))
        first_steps.append(gather_three(first_steps[2]))
    after_attn, mlp_in = enter_mlp(mixed, out_slabs, block_low, gain_mlp)
    if line:
        mlp_in, *second_steps = tie(mlp_in, *second_steps)
        second_steps.append(gather_two(*second_steps))
    mlp_in = gather_tp(mlp_in, "gather_normed", 4)
    if line:
        mlp_in, first_steps[3], second_steps[2] = tie(mlp_in, first_steps[3], second_steps[2])
        second_steps.append(gather_three(second_steps[2]))
        own = assemble(first_low, *first_steps)
        mlp_slabs = [[own.reshape(width // 2, -1), swap_cores(own).reshape(width // 2, -1)]]

    def split(values):
        return values.reshape(4, -1, values.shape[-1])

    def branch_sum(parts):
        return jnp.concatenate(
            [lax.psum_scatter(piece, "tp", scatter_dimension=0, tiled=True).astype(F32) for piece in parts], axis=1
        )

    def finish(branch):
        return unorder((valid * (after_attn + RESIDUAL_SCALE * branch)).astype(LOW))

    if line:
        first_acts, first_grads = units_tiles(mlp_in, mlp_cot, mlp_slabs[0])
        own, other, second_steps[3] = tie(*first_grads, second_steps[3])
        slab = assemble(second_low, *second_steps)
        mlp_slabs.append([slab.reshape(width // 2, -1), swap_cores(slab).reshape(width // 2, -1)])
        first_part = split(plus(own, swap_cores(other)))
        first_sum = scatter_one(first_part)
        second_acts, second_grads = units_tiles(mlp_in, mlp_cot, mlp_slabs[1])
        second_acts, own, other, first_sum = tie(second_acts, *second_grads, first_sum)
        first_sums = scatter_two(first_part, first_sum)
        swapped = swap_cores(other)
        back_low, ff_low = [], []
        for k, pair in enumerate(zip(*mlp_slabs)):
            back, *ff_low = close_tiles([first_acts, second_acts], list(pair), k * (width // 2 // UNIT), ff_low)
            back_low.append(back)
        *back_low, first_up, first_down, swapped = tie(*back_low, *first_sums, swapped)
        first_sums = scatter_three(first_part, first_up, first_down)
        second_part = split(plus(own, swapped))
        second_sum = scatter_one(second_part)
    else:
        mlp_grads = []
        back, branch = 0.0, 0.0
        for (a, b), (slab,) in zip(pieces, mlp_slabs):
            size = b - a
            gate, up = dot(mlp_in, slab[:, :size]), dot(mlp_in, slab[:, size : 2 * size])
            sigma = jax.nn.sigmoid(gate)
            activated = (gate * sigma * up).astype(LOW)
            grad_act = dot(mlp_cot, slab[:, 2 * size :])
            gate_cot = (grad_act * up * sigma * (1.0 + gate * (1.0 - sigma))).astype(LOW)
            up_cot = (grad_act * gate * sigma).astype(LOW)
            back += dot_nt(gate_cot, slab[:, :size]) + dot_nt(up_cot, slab[:, size : 2 * size])
            branch += dot_nt(activated, slab[:, 2 * size :])
            grads = [dot_tn(mlp_in, gate_cot), dot_tn(mlp_in, up_cot), dot_tn(mlp_cot, activated)]
            mlp_grads.append(jnp.concatenate([grad.astype(LOW) for grad in grads], axis=1))
        back_low = [back.astype(LOW)]
        ff_low = [branch.astype(LOW)]
    grad_after, mlp_gain_grad, attn_cot = leave_mlp(back_low, after_attn, grad_out, gain_mlp)
    if line:
        attn_cot, first_up, first_down, second_sum = tie(attn_cot, *first_sums, second_sum)
        first_total = scatter_end(first_part, first_up, first_down)
        second_sums = scatter_two(second_part, second_sum)
    attn_cot = gather_tp(attn_cot, "gather_cot", 5)
    if line:
        attn_cot, second_up, second_down, *ff_low = tie(attn_cot, *second_sums, *ff_low)
        second_sums = scatter_three(second_part, second_up, second_down)
        own_output = finish(branch_sum(ff_low))
    else:
        mlp_sums = [lax.psum_scatter(grads, "fsdp", scatter_dimension=0, tiled=True).astype(F32) for grads in mlp_grads]
        block_output = deal_plain(finish(branch_sum(ff_low)), dealt_order)

    grad_mixed = 0.0
    for (a, b), slab in zip(bounds, out_slabs):
        grad_mixed += dot(attn_cot[:, a:b], slab)
    out_grads = [rowwise(dot_tn(attn_cot[:, a:b], mixed).astype(LOW)) for a, b in bounds]
    if line:
        out_part = split(plus(out_grads[0], swap_cores(out_grads[1])))
        out_step = scatter_one(out_part)
    query_cot, kv_cot, grad_rope_all = attend_back(
        queries, key_value, rope_all, bias, tables, mixed, grad_mixed.astype(LOW), lse
    )
    if line:
        query_cot, kv_cot, second_up, second_down, out_step = tie(query_cot, kv_cot, *second_sums, out_step)
        out_steps = scatter_two(out_part, out_step)
        second_total = scatter_end(second_part, second_up, second_down)
        out_sum = scatter_end(out_part, *scatter_three(out_part, *out_steps))
        query_cot, out_sum = tie(query_cot, out_sum)
        down_sum, head_sum, block_output, input_grad, gain_sums = finish_all(
            dealt_order,
            (query_cot, kv_cot),
            grad_rope_all,
            natural,
            q_rows,
            latent_all,
            latents,
            jnp.concatenate([gain_query, gain_latent])[None],
            own_tables,
            block_low,
            normed_low,
            downs.reshape(2, width // 2, padded),
            gain_attn[None],
            grad_after,
            mlp_gain_grad[None],
            own_output,
        )
        owner = group * tp_count + column
        spots = ((0, group % 2 * (width // 2) + (group // 2 * tp_count + column) * latent_rows, latent_rows),)
        spots += ((1, spots[0][1], latent_rows), (2, owner * small_q, small_q), (2, qr + owner * small_l, small_l))
        attn_gain_sum, mlp_gain_sum, query_gain_sum, latent_gain_sum = [
            lax.dynamic_slice(gain_sums, (row, at), (1, count))[0] for row, at, count in spots
        ]
    else:
        back_latents = jnp.concatenate(
            [dot_nt(query_cot, w_qup), dot_nt(kv_cot, w_kvup), grad_rope_all], axis=1
        ).astype(LOW)
        grad_latents = lax.psum_scatter(back_latents, "tp", scatter_dimension=0, tiled=True).astype(F32)
        qup_grad = dot_tn(query_all, query_cot).astype(LOW).reshape(fsdp_count, q_rows, even * LANE)
        kvup_grad = dot_tn(comp_all, kv_cot).astype(LOW).reshape(fsdp_count, l_rows, even * LANE)
        head_grads = jnp.concatenate([qup_grad, kvup_grad], axis=1)
        head_sum = lax.psum_scatter(head_grads, "fsdp", scatter_dimension=0, tiled=False).astype(F32)
        out_sum = lax.psum_scatter(out_grads[0], "fsdp", scatter_dimension=0, tiled=True).astype(F32)

    def drop_heads(values, size, to):
        return values.reshape(values.shape[0], even, to)[:, :heads, :size].reshape(values.shape[0], heads * size)

    if not line:
        grad_query_latent, query_gain_grad = norm_back(
            query_latent, factor_of(query_latent), gain_query, grad_latents[:, :qr]
        )
        grad_kv_latent, latent_gain_grad = norm_back(
            kv_latent, factor_of(kv_latent), gain_latent, grad_latents[:, qr : qr + KR]
        )
        grad_rope = grad_latents[:, qr + KR + NOPE : qr + KR + NOPE + ROPE]
        grad_rope = grad_rope * cos_local - turn_half(grad_rope) * sin_local
        latent_cot = jnp.concatenate([grad_query_latent, grad_kv_latent, grad_rope], axis=1).astype(LOW)
        grad_normed = dot_nt(latent_cot, w_down)
        extra_input, attn_gain_grad = norm_back(block_vals, factor_of(block_vals), gain_attn, grad_normed)
        input_grad = (grad_after + extra_input).astype(LOW)

    if line:
        first_cuts = [first_total[:, a : a + UNIT] for a in range(0, first_total.shape[1], UNIT)]
        full = second_total.shape[1] // (3 * UNIT) * 3 * UNIT
        second_cuts = [second_total[:, a : a + UNIT] for a in range(0, full, UNIT)]
        second_cuts += [second_total[:, full + i * REST : full + (i + 1) * REST] for i in range(3)]
        gate_grad, up_grad, down_grad = [
            jnp.concatenate(first_cuts[i::3] + second_cuts[i::3], axis=1) for i in range(3)
        ]
    else:
        down_sum = lax.psum_scatter(
            dot_tn(normed_low, latent_cot), ("fsdp", "tp"), scatter_dimension=0, tiled=True
        )
        gains = jnp.concatenate(
            [
                values.reshape(fsdp_count * tp_count, -1)
                for values in (attn_gain_grad, mlp_gain_grad, query_gain_grad, latent_gain_grad)
            ],
            axis=1,
        )
        gain_sum = lax.psum_scatter(gains, ("fsdp", "tp"), scatter_dimension=0, tiled=True)[0]
        attn_gain_sum, mlp_gain_sum, query_gain_sum, latent_gain_sum = jnp.split(
            gain_sum, [latent_rows, 2 * latent_rows, 2 * latent_rows + small_q]
        )
        sizes = [b - a for a, b in pieces]
        gate_grad, up_grad, down_grad = [
            jnp.concatenate([total[:, i * size : (i + 1) * size] for total, size in zip(mlp_sums, sizes)], axis=1)
            for i in range(3)
        ]
    query_up_grad = drop_heads(head_sum[:q_rows], QKD, LANE)
    latent_up_grad = drop_heads(head_sum[q_rows:], LANE, LANE)
    out_weight_grad = drop_heads(out_sum, VD, VD)

    return (
        block_output[None],
        input_grad[None],
        attn_gain_sum,
        down_sum[:, :qr],
        query_gain_sum,
        down_sum[:, qr:used],
        latent_gain_sum,
        query_up_grad,
        latent_up_grad,
        out_weight_grad,
        mlp_gain_sum,
        gate_grad,
        up_grad,
        down_grad,
    )


def solution(mesh):
    both = P(("fsdp", "tp"))
    rows = P(("fsdp", "tp"), None)
    grid = P("fsdp", "tp")
    tokens = P("fsdp", "tp", None)
    return jax.shard_map(
        per_device,
        mesh=mesh,
        in_specs=(tokens, P(), P(), tokens, both, rows, both, rows, both, grid, grid, grid, both, grid, grid, grid),
        out_specs=(tokens, tokens, both, rows, both, rows, both, grid, grid, grid, both, grid, grid, grid),
        check_vma=False,
    )
```

```python
import functools
import math

import jax
import jax.numpy as jnp
from jax import lax
from jax.experimental import pallas as pl
from jax.experimental.layout import Layout, with_layout_constraint
from jax.experimental.pallas import tpu as pltpu
from jax.sharding import PartitionSpec as P

KR = 256
NOPE = 64
ROPE = 32
VD = 64
QKD = 96
LANE = 128

EPSILON = 1e-05
RESIDUAL_SCALE = 1.4 / math.sqrt(62.0)
ROTARY_BASE = 10000.0
MASKED = -1e30
SCORE_SCALE = 1.0 / math.sqrt(QKD)

F32 = jnp.float32
LOW = jnp.bfloat16
NT = (((1,), (1,)), ((), ()))
TN = (((0,), (0,)), ((), ()))


def dot(left, right):
    return jnp.dot(left, right, preferred_element_type=F32)


def dot_nt(left, right):
    return lax.dot_general(left, right, NT, preferred_element_type=F32)


def dot_tn(left, right):
    return lax.dot_general(left, right, TN, preferred_element_type=F32)


def normalize(values, gain):
    factor = lax.rsqrt(jnp.mean(values * values, axis=-1, keepdims=True) + EPSILON)
    return (values * factor * gain, factor)


def norm_back(values, factor, gain, grad):
    weighted = grad * gain
    inner = jnp.mean(weighted * values, axis=-1, keepdims=True)
    dvalues = factor * weighted - values * (factor * factor * factor) * inner
    dgain = jnp.sum(grad * values * factor, axis=0)
    return (dvalues, dgain)


def rotary_tables(positions):
    halfway = ROPE // 2
    spacing = jnp.arange(halfway, dtype=F32) * (2.0 / ROPE)
    freqs = jnp.power(jnp.float32(ROTARY_BASE), -spacing)
    angle = positions.astype(F32)[:, None] * freqs[None, :]
    return (jnp.cos(angle), jnp.sin(angle))


def turn_half(values):
    halfway = values.shape[-1] // 2
    return jnp.concatenate([-values[..., halfway:], values[..., :halfway]], axis=-1)


def head_tables(cosine, sine):
    count = cosine.shape[0]
    one = jnp.ones((count, NOPE), F32)
    zero = jnp.zeros((count, NOPE), F32)
    half = jnp.zeros_like(sine)
    rest = jnp.zeros((count, LANE - NOPE - ROPE), F32)
    return (
        jnp.concatenate([one, cosine, cosine, rest], axis=1),
        jnp.concatenate([zero, half, sine, rest], axis=1),
        jnp.concatenate([zero, -sine, half, rest], axis=1),
    )


def attend_kernel(
    blocks, q_rows, lat_ref, w_ref, bias_ref, cos_ref, lift_ref, drop_ref, rot_ref, kv_ref, mix_ref, lse_ref
):
    size = lat_ref.shape[0] // blocks
    low = lax.broadcasted_iota(jnp.int32, (1, LANE), 1) < NOPE
    causal = lax.broadcasted_iota(jnp.int32, (size, size), 1) <= lax.broadcasted_iota(
        jnp.int32, (size, size), 0
    )
    half = ROPE // 2
    groups, rows_all, columns = w_ref.shape
    qr = groups * q_rows
    kv = lat_ref.shape[1] - LANE
    w_query = w_ref[:, :q_rows].reshape(qr, columns)
    w_pair = w_ref[:, q_rows:].reshape(groups * (rows_all - q_rows), columns)
    kv_ref[...] = dot(lat_ref[:, qr:kv], w_pair).astype(LOW)
    rope_ref = lat_ref.at[:, pl.ds(kv, LANE)]
    for i in range(blocks):
        rows = pl.ds(i * size, size)
        live = pl.ds(0, (i + 1) * size)
        outs = []
        projected = dot(lat_ref[rows, :qr], w_query).astype(LOW).astype(F32)
        for h in range(2):
            cols = pl.ds(h * LANE, LANE)
            query = projected[:, h * LANE : (h + 1) * LANE]
            query = (
                query * cos_ref[rows, :]
                + pltpu.roll(query, half, 1) * lift_ref[rows, :]
                + pltpu.roll(query, LANE - half, 1) * drop_ref[rows, :]
            ).astype(LOW)
            rot_ref[rows, cols] = query
            pair = kv_ref[live, cols]
            key = jnp.where(low, pair, rope_ref[live, :])
            value = jnp.where(low, jnp.ones_like(pair), pair)
            scores = dot_nt(query, key) * SCORE_SCALE + bias_ref[:, live]
            edge = jnp.where(causal, scores[:, i * size :], MASKED)
            scores = edge if i == 0 else jnp.concatenate([scores[:, : i * size], edge], axis=1)
            top = jnp.max(scores, axis=1, keepdims=True)
            expo = jnp.exp(scores - top)
            out = dot(expo.astype(LOW), value)
            total = out[:, 0:1]
            lse_ref[rows, pl.ds(h * NOPE, NOPE)] = jnp.broadcast_to(top + jnp.log(total), (size, NOPE))
            outs.append(out / total)
        mix_ref[rows, :] = jnp.where(low, pltpu.roll(outs[0], NOPE, 1), outs[1]).astype(LOW)


def attend(latents, weights, q_rows, bias, tables):
    count = latents.shape[0]
    groups, rows_all, columns = weights.shape
    steps = columns // (2 * LANE)
    blocks = 4

    def whole(shape):
        return pl.BlockSpec(shape, lambda i: (0, 0))

    wide = pl.BlockSpec((count, 2 * LANE), lambda i: (0, i))
    slim = pl.BlockSpec((count, LANE), lambda i: (0, i))
    table = whole((count, LANE))
    return pl.pallas_call(
        functools.partial(attend_kernel, blocks, q_rows),
        grid=(steps,),
        in_specs=[
            whole(latents.shape),
            pl.BlockSpec((groups, rows_all, 2 * LANE), lambda i: (0, 0, i)),
            whole((1, count)),
            table,
            table,
            table,
        ],
        out_specs=[wide, wide, slim, slim],
        out_shape=[
            jax.ShapeDtypeStruct((count, columns), LOW),
            jax.ShapeDtypeStruct((count, columns), LOW),
            jax.ShapeDtypeStruct((count, steps * LANE), LOW),
            jax.ShapeDtypeStruct((count, steps * LANE), F32),
        ],
        cost_estimate=pl.CostEstimate(flops=0, bytes_accessed=1 << 20, transcendentals=0),
        name="attend",
    )(latents, weights, bias, *tables)


def attend_back_kernel(
    blocks,
    q_ref,
    kv_ref,
    rope_ref,
    bias_ref,
    cos_ref,
    lift_ref,
    drop_ref,
    mix_ref,
    grad_ref,
    lse_ref,
    dq_ref,
    dkv_ref,
    drope_ref,
    dkey,
    dval,
    drope,
):
    size = q_ref.shape[0] // blocks
    low = lax.broadcasted_iota(jnp.int32, (1, LANE), 1) < NOPE
    causal = lax.broadcasted_iota(jnp.int32, (size, size), 1) <= lax.broadcasted_iota(
        jnp.int32, (size, size), 0
    )
    half = ROPE // 2

    @pl.when(pl.program_id(0) == 0)
    def _():
        drope[...] = jnp.zeros_like(drope)

    for h in range(2):
        cols = pl.ds(h * LANE, LANE)
        for i in range(blocks):
            rows = pl.ds(i * size, size)
            past = i * size
            live = pl.ds(0, past + size)
            query = q_ref[rows, cols]
            pair = kv_ref[live, cols]
            key = jnp.where(low, pair, rope_ref[live, :])
            both = grad_ref[rows, :]
            turned = pltpu.roll(both.astype(F32), NOPE, 1).astype(LOW) if h == 0 else both
            grad = jnp.where(low, jnp.zeros_like(both), turned)
            product = both.astype(F32) * mix_ref[rows, :].astype(F32)
            mine = low if h == 0 else ~low
            inner = jnp.sum(jnp.where(mine, product, 0.0), axis=1, keepdims=True)
            scores = dot_nt(query, key) * SCORE_SCALE + bias_ref[:, live]
            probs = jnp.exp(scores - lse_ref[rows, pl.ds(h * NOPE, 1)])
            edge = jnp.where(causal, probs[:, past:], 0.0)
            probs = edge if i == 0 else jnp.concatenate([probs[:, :past], edge], axis=1)
            score_cot = (probs * (dot_nt(grad, pair) - inner)).astype(LOW)
            dquery = dot(score_cot, key) * SCORE_SCALE
            dq_ref[rows, cols] = (
                dquery * cos_ref[rows, :]
                - pltpu.roll(dquery, half, 1) * lift_ref[rows, :]
                - pltpu.roll(dquery, LANE - half, 1) * drop_ref[rows, :]
            ).astype(LOW)
            dk = dot_tn(score_cot, query) * SCORE_SCALE
            dv = dot_tn(probs.astype(LOW), grad)
            if i > 0:
                dkey[pl.ds(0, past), :] += dk[:past]
                dval[pl.ds(0, past), :] += dv[:past]
            dkey[rows, :] = dk[past:]
            dval[rows, :] = dv[past:]
        dkv_ref[:, cols] = jnp.where(low, dkey[...], dval[...]).astype(LOW)
        drope[...] += dkey[...]
    drope_ref[...] = drope[...].astype(LOW)


def attend_back(query, pair, rope, bias, tables, mixed, grad, lse):
    count = query.shape[0]
    steps = query.shape[1] // (2 * LANE)
    blocks = 4

    def whole(shape):
        return pl.BlockSpec(shape, lambda i: (0, 0))

    wide = pl.BlockSpec((count, 2 * LANE), lambda i: (0, i))
    slim = pl.BlockSpec((count, LANE), lambda i: (0, i))
    table = whole((count, LANE))
    return pl.pallas_call(
        functools.partial(attend_back_kernel, blocks),
        grid=(steps,),
        in_specs=[wide, wide, table, whole((1, count)), table, table, table, slim, slim, slim],
        out_specs=[wide, wide, table],
        out_shape=[
            jax.ShapeDtypeStruct(query.shape, LOW),
            jax.ShapeDtypeStruct(query.shape, LOW),
            jax.ShapeDtypeStruct((count, LANE), LOW),
        ],
        scratch_shapes=[pltpu.VMEM((count, LANE), F32)] * 3,
        cost_estimate=pl.CostEstimate(flops=0, bytes_accessed=1 << 20, transcendentals=0),
        name="attend_back",
    )(query, pair, rope, bias, *tables, mixed, grad, lse)


LINE = 8
PLANE = 4


def special():
    return lax.axis_size("fsdp") == LINE and lax.axis_size("tp") == PLANE


def tie(*values):
    return lax.optimization_barrier(values)


def hop(values, pairs):
    moves = [(2 * a + core, 2 * b + core) for a, b in pairs for core in range(2)]
    return lax.ppermute(values, "fsdp", moves)


def swap_cores(values):
    return lax.ppermute(values, "fsdp", [(i, i ^ 1) for i in range(LINE)])


UP = [(0, 1), (1, 2), (2, 3)]
DOWN = [(1, 0), (2, 1), (3, 2)]


def line_index():
    return lax.axis_index("fsdp") // 2


def gather_one(values):
    return hop(values, UP), hop(values, DOWN)


def gather_two(above, below):
    return hop(above, UP[1:]) + hop(below, DOWN[:2])


def gather_three(far):
    return hop(far, [(1, 0), (2, 3)])


def assemble(own, above, below, far, last):
    z = line_index()
    whole = jnp.broadcast_to(own[None], (4,) + own.shape)
    put = lax.dynamic_update_index_in_dim
    whole = put(whole, far, (z + 2) % 4, 0)
    whole = put(whole, jnp.where(z == 0, last, above), (z + 3) % 4, 0)
    return put(whole, jnp.where(z == 3, last, below), (z + 1) % 4, 0)


def plus(left, right):
    return (left.astype(F32) + right.astype(F32)).astype(LOW)


def line_sum(part):
    lines = [[2 * z + core for z in range(4)] for core in range(2)]
    return lax.psum_scatter(part, "fsdp", scatter_dimension=0, axis_index_groups=lines, tiled=False)


def rowwise(values):
    return with_layout_constraint(values, Layout(major_to_minor=tuple(range(values.ndim))))


def by_core(own, other):
    first = lax.axis_index("fsdp") % 2 == 0
    return jnp.where(first, own, other), jnp.where(first, other, own)


def to_line(values):
    block = values.shape[-1] // LINE
    parts = [values[..., i * block : (i + 1) * block] for i in range(LINE)]
    return jnp.concatenate(by_core(jnp.concatenate(parts[0::2], axis=-1), jnp.concatenate(parts[1::2], axis=-1)), axis=-1)


def from_line(values):
    block = values.shape[-1] // LINE
    half = values.shape[-1] // 2
    even, odd = by_core(values[..., :half], values[..., half:])
    parts = [p[..., i * block : (i + 1) * block] for i in range(LINE // 2) for p in (even, odd)]
    return jnp.concatenate(parts, axis=-1)


def deal_plain(values, sources):
    group = lax.axis_index("fsdp")
    return lax.dynamic_index_in_dim(lax.all_gather(values, "fsdp"), jnp.take(sources, group), 0, keepdims=False)


MESH = pl.DeviceIdType.MESH


def square():
    me = lax.axis_index("tp")
    y, x = me // 2, me % 2
    beside, across = 2 * y + (1 - x), 2 * (1 - y) + x
    return me, beside, across, 3 - me


def greet(beside, across):
    barrier = pltpu.get_barrier_semaphore()
    for peer in (beside, across):
        pl.semaphore_signal(barrier, inc=1, device_id={"tp": peer}, device_id_type=MESH)
    pl.semaphore_wait(barrier, 2)


def send(source, target, sems, slot, peer):
    copy = pltpu.make_async_remote_copy(
        src_ref=source,
        dst_ref=target,
        send_sem=sems[0].at[slot],
        recv_sem=sems[1].at[slot],
        device_id={"tp": peer},
        device_id_type=MESH,
    )
    copy.start()
    return copy


def rows_of(position, size):
    return pl.ds(pl.multiple_of(position * size, size), size)


def reduce_square(parts, got, sems, prepare=lambda position: None, meanwhile=lambda: None):
    size = got[0].shape[1]
    me, beside, across, corner = square()
    peers = ((beside, across), (across, beside))
    prepare(corner)
    early = [
        send(parts[k].at[rows_of(corner, size), :], got[k].at[0], sems, 3 * k, first) for k, (first, _) in enumerate(peers)
    ]
    for k, (first, _) in enumerate(peers):
        prepare(first)
        early.append(send(parts[k].at[rows_of(first, size), :], got[k].at[1], sems, 3 * k + 1, first))
    for k, (_, second) in enumerate(peers):
        early[k].wait_recv()
        onward = rows_of(second, size)
        parts[k][onward, :] = (parts[k][onward, :].astype(F32) + got[k][0].astype(F32)).astype(LOW)
        early.append(send(parts[k].at[onward, :], got[k].at[2], sems, 3 * k + 2, second))
    prepare(me)
    meanwhile()
    for copy in early[2:]:
        copy.wait_recv()
    return early


def spread_square(full, columns, sems, base):
    me, beside, across, corner = square()
    size = full.shape[0] // PLANE
    own = rows_of(me, size)

    def piece(position, k):
        return full.at[rows_of(position, size), columns[k]]

    def pass_on(position, k, slot, peer):
        return send(piece(position, k), piece(position, k), sems, base + slot, peer)

    one = pass_on(me, 0, 0, across)
    two = pass_on(me, 1, 1, beside)
    three = pass_on(me, 0, 2, beside)
    four = pass_on(me, 1, 3, across)
    one.wait_recv()
    five = pass_on(across, 0, 4, beside)
    two.wait_recv()
    six = pass_on(beside, 1, 5, across)
    for copy in (three, four, five, six):
        copy.wait_recv()
    return [one, two, three, four, five, six]


def gather_kernel(cut, own_ref, full_ref, send_sems, recv_sems):
    me, beside, across, _ = square()
    size, width = own_ref.shape
    full_ref[rows_of(me, size), :] = own_ref[...]
    greet(beside, across)
    for copy in spread_square(full_ref, (pl.ds(0, cut), pl.ds(cut, width - cut)), (send_sems, recv_sems), 0):
        copy.wait_send()


def gather_tp(values, name, ident):
    if not special():
        return lax.all_gather(values, "tp", axis=0, tiled=True)
    rows, columns = values.shape
    cut = columns // LANE // 2 * LANE
    return pl.pallas_call(
        functools.partial(gather_kernel, cut),
        in_specs=[pl.BlockSpec(memory_space=pltpu.VMEM)],
        out_specs=pl.BlockSpec(memory_space=pltpu.VMEM),
        out_shape=jax.ShapeDtypeStruct((PLANE * rows, columns), values.dtype),
        scratch_shapes=[pltpu.SemaphoreType.DMA((6,)), pltpu.SemaphoreType.DMA((6,))],
        compiler_params=pltpu.CompilerParams(collective_id=ident, has_side_effects=True),
        cost_estimate=pl.CostEstimate(flops=0, bytes_accessed=1 << 20, transcendentals=0),
        name=name,
    )(values)


ROW_STEP = 32


def enter_kernel(
    mix_ref, w0_ref, w1_ref, x_ref, gain_ref, after_ref, low_ref, p0_ref, p1_ref, got0, got1, send_sems, recv_sems
):
    me, beside, across, _ = square()
    size = after_ref.shape[0]
    greet(beside, across)
    parts, gots = (p0_ref, p1_ref), (got0, got1)

    def prepare(position):
        here = rows_of(position, size)
        for part, weight in zip(parts, (w0_ref, w1_ref)):
            part[here, :] = dot_nt(mix_ref[here, :], weight[...]).astype(LOW)

    copies = reduce_square(parts, gots, (send_sems, recv_sems), prepare)

    def rows_step(step, carry):
        here = pl.ds(pl.multiple_of(step * ROW_STEP, ROW_STEP), ROW_STEP)
        mine = pl.ds(pl.multiple_of(me * size + step * ROW_STEP, ROW_STEP), ROW_STEP)
        total = jnp.concatenate(
            [
                part[mine, :].astype(F32) + got[1, here, :].astype(F32) + got[2, here, :].astype(F32)
                for part, got in zip(parts, gots)
            ],
            axis=1,
        )
        after = x_ref[here, :].astype(F32) + RESIDUAL_SCALE * total
        after_ref[here, :] = after
        factor = lax.rsqrt(jnp.mean(after * after, axis=-1, keepdims=True) + EPSILON)
        low_ref[here, :] = (after * factor * gain_ref[...]).astype(LOW)
        return carry

    lax.fori_loop(0, size // ROW_STEP, rows_step, 0)
    for copy in copies:
        copy.wait_send()


def leave_kernel(
    p0_ref, p1_ref, after_ref, cot_ref, gain_ref, grad_ref, dgain_ref, low_ref, got0, got1, send_sems, recv_sems
):
    me, beside, across, _ = square()
    size = after_ref.shape[0]
    greet(beside, across)
    parts, gots = (p0_ref, p1_ref), (got0, got1)
    copies = reduce_square(parts, gots, (send_sems, recv_sems))
    dgain_ref[...] = jnp.zeros_like(dgain_ref)

    def rows_step(step, carry):
        here = pl.ds(pl.multiple_of(step * ROW_STEP, ROW_STEP), ROW_STEP)
        mine = pl.ds(pl.multiple_of(me * size + step * ROW_STEP, ROW_STEP), ROW_STEP)
        grad = jnp.concatenate(
            [
                part[mine, :].astype(F32) + got[1, here, :].astype(F32) + got[2, here, :].astype(F32)
                for part, got in zip(parts, gots)
            ],
            axis=1,
        )
        after = after_ref[here, :]
        factor = lax.rsqrt(jnp.mean(after * after, axis=-1, keepdims=True) + EPSILON)
        weighted = grad * gain_ref[...]
        inner = jnp.mean(weighted * after, axis=-1, keepdims=True)
        dgain_ref[...] += jnp.sum(grad * after * factor, axis=0, keepdims=True)
        total = cot_ref[here, :].astype(F32) + factor * weighted - after * (factor * factor * factor) * inner
        grad_ref[here, :] = total
        low_ref[here, :] = (RESIDUAL_SCALE * total).astype(LOW)
        return carry

    lax.fori_loop(0, size // ROW_STEP, rows_step, 0)
    for copy in copies:
        copy.wait_send()


def square_scratch(size, half):
    return [
        pltpu.VMEM((3, size, half), LOW),
        pltpu.VMEM((3, size, half), LOW),
        pltpu.SemaphoreType.DMA((6,)),
        pltpu.SemaphoreType.DMA((6,)),
    ]


def enter_mlp(mixed, slabs, x_low, gain):
    rows, half = mixed.shape[0], x_low.shape[1] // 2
    if not special():
        piece = dot_nt(mixed, slabs[0]).astype(LOW)
        branch = lax.psum_scatter(piece, "tp", scatter_dimension=0, tiled=True).astype(F32)
        after = x_low.astype(F32) + RESIDUAL_SCALE * branch
        normed, _ = normalize(after, gain)
        return after, normed.astype(LOW)
    size = x_low.shape[0]
    vmem = pl.BlockSpec(memory_space=pltpu.VMEM)
    return pl.pallas_call(
        enter_kernel,
        in_specs=[vmem] * 5,
        out_specs=[vmem] * 2,
        out_shape=[jax.ShapeDtypeStruct((size, 2 * half), F32), jax.ShapeDtypeStruct((size, 2 * half), LOW)],
        scratch_shapes=[pltpu.VMEM((rows, half), LOW)] * 2 + square_scratch(size, half),
        compiler_params=pltpu.CompilerParams(collective_id=2, has_side_effects=True, vmem_limit_bytes=48 << 20),
        cost_estimate=pl.CostEstimate(flops=0, bytes_accessed=1 << 20, transcendentals=0),
        name="enter_mlp",
    )(mixed, *slabs, x_low, gain[None])


def leave_mlp(pieces, after, grad_out, gain):
    rows, half = pieces[0].shape[0], after.shape[1] // 2
    if not special():
        grad = lax.psum_scatter(pieces[0], "tp", scatter_dimension=0, tiled=True).astype(F32)
        factor = lax.rsqrt(jnp.mean(after * after, axis=-1, keepdims=True) + EPSILON)
        extra, dgain = norm_back(after, factor, gain, grad)
        total = grad_out + extra
        return total, dgain, (RESIDUAL_SCALE * total).astype(LOW)
    size = after.shape[0]
    vmem = pl.BlockSpec(memory_space=pltpu.VMEM)
    total, dgain, full = pl.pallas_call(
        leave_kernel,
        in_specs=[vmem] * 5,
        out_specs=[vmem] * 3,
        out_shape=[
            jax.ShapeDtypeStruct((size, 2 * half), F32),
            jax.ShapeDtypeStruct((1, 2 * half), F32),
            jax.ShapeDtypeStruct((size, 2 * half), LOW),
        ],
        scratch_shapes=square_scratch(size, half),
        compiler_params=pltpu.CompilerParams(collective_id=3, has_side_effects=True, vmem_limit_bytes=48 << 20),
        cost_estimate=pl.CostEstimate(flops=0, bytes_accessed=1 << 20, transcendentals=0),
        name="leave_mlp",
    )(*pieces, after, grad_out.astype(LOW), gain[None])
    return total, dgain[0], full


UNIT = 256
REST = 64
TOKEN_STEP = 512
FEATURE_STEP = 640


def units_kernel(unit, slabs, begun, x_ref, cot_ref, *refs):
    weights, rest = refs[:slabs], refs[slabs + begun :]
    act_ref, grads = rest[0], rest[1:]
    half = weights[0].shape[0]
    wide = 2 * unit

    def tokens(step, carry):
        rows = pl.ds(pl.multiple_of(step * TOKEN_STEP, TOKEN_STEP), TOKEN_STEP)
        both = 0.0
        grad = 0.0
        for k in range(slabs):
            part = pl.ds(k * half, half)
            both = both + dot(x_ref[rows, part], weights[k][:, 0:wide])
            grad = grad + dot(cot_ref[rows, part], weights[k][:, wide : wide + max(unit, LANE)])
        gate = both[:, : max(unit, LANE)]
        up = both[:, unit:] if unit >= LANE else pltpu.roll(both, unit, 1)
        sigma = 1.0 / (1.0 + jnp.exp(-gate))
        silu = gate * sigma
        activated = silu * up
        gate_cot = grad * up * (sigma * (1.0 + gate * (1.0 - sigma)))
        up_cot = grad * silu
        if unit >= LANE:
            act_ref[rows, 0:unit] = gate_cot.astype(LOW)
            act_ref[rows, unit:wide] = up_cot.astype(LOW)
            act_ref[rows, wide : wide + unit] = activated.astype(LOW)
        else:
            low = lax.broadcasted_iota(jnp.int32, (1, LANE), 1) < unit
            act_ref[rows, 0:LANE] = jnp.where(low, gate_cot, pltpu.roll(up_cot, unit, 1)).astype(LOW)
            act_ref[rows, LANE : 2 * LANE] = jnp.where(low, activated, 0.0).astype(LOW)
        return carry

    lax.fori_loop(0, x_ref.shape[0] // TOKEN_STEP, tokens, 0)
    columns = act_ref.shape[1]
    for k in range(slabs):

        def features(step, carry):
            rows = pl.ds(pl.multiple_of(step * FEATURE_STEP, FEATURE_STEP), FEATURE_STEP)
            part = pl.ds(pl.multiple_of(k * half + step * FEATURE_STEP, LANE), FEATURE_STEP)
            grads[k][rows, 0:wide] = dot_tn(x_ref[:, part], act_ref[:, 0:wide]).astype(LOW)
            grads[k][rows, wide:columns] = dot_tn(cot_ref[:, part], act_ref[:, wide:columns]).astype(LOW)
            return carry

        lax.fori_loop(0, half // FEATURE_STEP, features, 0)


def units_call(values, cot, slabs, unit, first, count, begun):
    rows, width = values.shape
    half, total = slabs[0].shape
    columns = 3 * unit if unit >= LANE else 2 * LANE
    whole = pl.BlockSpec((rows, width), lambda j: (0, 0), pipeline_mode=pl.Buffered(1))
    block = pl.BlockSpec((half, columns), lambda j: (0, j + first))
    shapes = [(rows, total)] + [(half, total)] * len(slabs)
    lead = 2 + len(slabs)
    return pl.pallas_call(
        functools.partial(units_kernel, unit, len(slabs), len(begun)),
        grid=(count,),
        in_specs=[whole, whole] + [block] * len(slabs) + [pl.BlockSpec(memory_space=pl.ANY)] * len(begun),
        out_specs=[pl.BlockSpec((rows, columns), lambda j: (0, j + first))] + [block] * len(slabs),
        out_shape=[jax.ShapeDtypeStruct(shape, LOW) for shape in shapes],
        input_output_aliases={lead + i: i for i in range(len(begun))},
        compiler_params=pltpu.CompilerParams(vmem_limit_bytes=60 << 20),
        cost_estimate=pl.CostEstimate(flops=0, bytes_accessed=1 << 20, transcendentals=0),
        name="units",
    )(values, cot, *slabs, *begun)


def units_tiles(values, cot, slabs):
    total = slabs[0].shape[1]
    full = total // (3 * UNIT)
    results = units_call(values, cot, slabs, UNIT, 0, full, [])
    if total % (3 * UNIT):
        results = units_call(values, cot, slabs, REST, full * 3, 1, results)
    return results[0], results[1:]


def close_kernel(counts, begun, *refs):
    acts, weights = refs[: len(counts)], refs[len(counts) : 2 * len(counts)]
    back_ref, branch_ref = refs[2 * len(counts) + begun :]

    def tokens(step, carry):
        rows = pl.ds(pl.multiple_of(step * TOKEN_STEP, TOKEN_STEP), TOKEN_STEP)
        back = 0.0
        branch = 0.0
        for (full, rest), act, weight in zip(counts, acts, weights):
            for j in range(full):
                a = 3 * UNIT * j
                b = a + 2 * UNIT
                back = back + dot_nt(act[rows, a:b], weight[:, a:b])
                branch = branch + dot_nt(act[rows, b : b + UNIT], weight[:, b : b + UNIT])
            if rest:
                a = 3 * UNIT * full
                b = a + LANE
                back = back + dot_nt(act[rows, a:b], weight[:, a:b])
                branch = branch + dot_nt(act[rows, b : b + LANE], weight[:, b : b + LANE])
        back_ref[rows, :] = back.astype(LOW)
        branch_ref[rows, :] = branch.astype(LOW)
        return carry

    lax.fori_loop(0, back_ref.shape[0] // TOKEN_STEP, tokens, 0)


def close_tiles(acts, slabs, first, begun):
    rows = acts[0].shape[0]
    half = slabs[0].shape[0]
    counts = [(act.shape[1] // (3 * UNIT), act.shape[1] % (3 * UNIT)) for act in acts]
    total = sum(act.shape[1] for act in acts)
    return pl.pallas_call(
        functools.partial(close_kernel, counts, len(begun)),
        grid=(half // UNIT,),
        in_specs=[pl.BlockSpec(act.shape, lambda j: (0, 0), pipeline_mode=pl.Buffered(1)) for act in acts]
        + [pl.BlockSpec((UNIT, slab.shape[1]), lambda j: (j, 0)) for slab in slabs]
        + [pl.BlockSpec(memory_space=pl.ANY)] * len(begun),
        out_specs=[
            pl.BlockSpec((rows, UNIT), lambda j: (0, j)),
            pl.BlockSpec((rows, UNIT), lambda j: (0, j + first)),
        ],
        out_shape=[jax.ShapeDtypeStruct((rows, half), LOW), jax.ShapeDtypeStruct((rows, 2 * half), LOW)],
        input_output_aliases={2 * len(acts): 1} if begun else {},
        compiler_params=pltpu.CompilerParams(vmem_limit_bytes=60 << 20),
        cost_estimate=pl.CostEstimate(flops=0, bytes_accessed=1 << 20, transcendentals=0),
        name="close",
    )(*acts, *slabs, *begun)


class Wires:
    def __init__(self, send_sems, recv_sems):
        self.send_sems, self.recv_sems = send_sems, recv_sems

    def _copy(self, source, target, number, peer):
        return pltpu.make_async_remote_copy(
            src_ref=source,
            dst_ref=target,
            send_sem=self.send_sems.at[number],
            recv_sem=self.recv_sems.at[number],
            device_id=peer,
            device_id_type=MESH,
        )

    def start(self, source, target, number, peer):
        self._copy(source, target, number, peer).start()

    def sent(self, source, number, peer):
        self._copy(source, source, number, peer).wait_send()

    def arrived(self, target, number, peer):
        self._copy(target, target, number, peer).wait_recv()


def line_peers():
    group = lax.axis_index("fsdp")
    z, core = group // 2, group % 2
    return z, core, {"fsdp": group + 1 - 2 * core}


def line_peer(z, core):
    return {"fsdp": 2 * z + core}


def greet_all(peers):
    barrier = pltpu.get_barrier_semaphore()
    for peer in peers:
        pl.semaphore_signal(barrier, inc=1, device_id=peer, device_id_type=MESH)
    pl.semaphore_wait(barrier, len(peers))


def gather_square(piece, sources, wires, base):
    me, beside, across, corner = square()
    beside_peer, across_peer = {"tp": beside}, {"tp": across}
    for number, (k, peer) in enumerate(((0, across_peer), (1, beside_peer), (0, beside_peer), (1, across_peer))):
        wires.start(sources[k], piece(me, k), base + number, peer)

    def relay():
        wires.arrived(piece(across, 0), base, across_peer)
        wires.start(piece(across, 0), piece(across, 0), base + 4, beside_peer)
        wires.arrived(piece(beside, 1), base + 1, beside_peer)
        wires.start(piece(beside, 1), piece(beside, 1), base + 5, across_peer)

    def neighbours():
        wires.arrived(piece(beside, 0), base + 2, beside_peer)
        wires.arrived(piece(across, 1), base + 3, across_peer)

    def finish():
        wires.arrived(piece(corner, 0), base + 4, beside_peer)
        wires.arrived(piece(corner, 1), base + 5, across_peer)

    def leave():
        for number, k in enumerate((0, 1, 0, 1, 0, 1)):
            wires.sent(piece(me, k), base + number, beside_peer)

    return relay, neighbours, finish, leave


def store_line(ref, rows, values, core):
    half = values.shape[1] // 2
    block = half // 4
    for i in range(4):
        even = values[:, 2 * i * block : (2 * i + 1) * block]
        odd = values[:, (2 * i + 1) * block : (2 * i + 2) * block]
        ref[rows, i * block : (i + 1) * block] = jnp.where(core == 0, even, odd).astype(ref.dtype)
        ref[rows, half + i * block : half + (i + 1) * block] = jnp.where(core == 0, odd, even).astype(ref.dtype)


def bring_kernel(
    sources_ref,
    length_ref,
    down_ref,
    qk_ref,
    out_ref,
    cot_ref,
    input_ref,
    spot_ref,
    cos_ref,
    lift_ref,
    drop_ref,
    part_ref,
    downs_ref,
    qks_ref,
    outs_ref,
    own_cot_ref,
    normed_ref,
    latents_ref,
    gains_ref,
    all_ref,
    cots_ref,
    above_ref,
    below_ref,
    x_ref,
    scaled,
    blocks,
    got,
    theirs,
    stage,
    send_sems,
    recv_sems,
    local_sems,
):
    z, core, sibling = line_peers()
    me, beside, across, corner = square()
    wires = Wires(send_sems, recv_sems)
    size, width = cot_ref.shape
    half = width // 2
    turns = [line_peer((z + r) % 4, core) for r in (1, 2, 3)]
    greet_all([sibling, {"tp": beside}, {"tp": across}] + turns)
    up, down = line_peer((z + 1) % 4, core), line_peer((z + 3) % 4, core)
    edge = (z == 0) | (z == 3)
    inner = (z == 1) | (z == 2)

    def when(condition, action):
        @pl.when(condition)
        def _():
            action()

    heads = ((qk_ref, lambda at, side: qks_ref.at[at, (core + side) % 2], 0), (out_ref, lambda at, side: outs_ref.at[side, at], 1))

    def head_hop(at, number, peer, own=False):
        for ref, slot, k in heads:
            wires.start(ref if own else slot(at, 0), slot(at, 0), number + k, peer)

    def head_in(at, number, peer):
        for _, slot, k in heads:
            wires.arrived(slot(at, 0), number + k, peer)

    def head_over(at, number):
        for ref, slot, k in heads:
            target = qks_ref.at[at, core] if k == 0 else outs_ref.at[1, at]
            wires.start(slot(at, 0), target, number + k, sibling)

    def head_back(at, number):
        for _, slot, k in heads:
            wires.arrived(slot(at, 1), number + k, sibling)

    blocks[pl.ds(z, 1)] = cot_ref[...][None]
    downs_ref[0, pl.ds(z, 1), pl.ds(me, 1)] = down_ref[...][None, None]
    keeps = [pltpu.make_async_copy(ref, slot(z, 0), local_sems.at[k]) for ref, slot, k in heads]
    for keep in keeps:
        keep.start()

    for r in (1, 2, 3):
        wires.start(down_ref, downs_ref.at[0, z, me], r, turns[r - 1])
    wires.start(down_ref, downs_ref.at[1, z, me], 4, sibling)
    when(z < 2, lambda: wires.start(cot_ref, blocks.at[z], 0, up))
    when(z > 1, lambda: wires.start(cot_ref, blocks.at[z], 5, down))
    when((z == 0) | (z == 2), lambda: head_hop(z, 6, up, True))
    when((z == 1) | (z == 3), lambda: head_hop(z, 8, down, True))
    when((z == 0) | (z == 2), lambda: wires.start(part_ref, above_ref, 48, up))
    when((z == 1) | (z == 3), lambda: wires.start(part_ref, below_ref, 49, down))
    for keep in keeps:
        keep.wait()
    head_over(z, 10)

    for r in (1, 2, 3):
        wires.arrived(downs_ref.at[0, (z + 4 - r) % 4, me], r, turns[r - 1])
    relay, neighbours, finish, leave_downs = gather_square(
        lambda position, k: downs_ref.at[0, pl.ds(2 * k, 2), position],
        [downs_ref.at[0, pl.ds(2 * k, 2), me] for k in range(2)],
        wires,
        12,
    )
    for r in (1, 2, 3):
        here = (z + r) % 4
        wires.start(downs_ref.at[0, here, me], downs_ref.at[1, here, me], 17 + r, sibling)

    @pl.when(inner)
    def _():
        wires.arrived(blocks.at[z - 1], 0, down)
        wires.arrived(blocks.at[z + 1], 5, up)

    @pl.when(z == 1)
    def _():
        wires.start(blocks.at[0], blocks.at[0], 21, up)
        head_hop(z, 6, up, True)
        head_in(0, 6, down)
        head_hop(0, 22, up)
        wires.start(part_ref, above_ref, 48, up)
        head_over(0, 24)

    @pl.when(z == 2)
    def _():
        wires.start(blocks.at[3], blocks.at[3], 21, down)
        head_hop(z, 8, down, True)
        head_in(3, 8, up)
        head_hop(3, 22, down)
        wires.start(part_ref, below_ref, 49, down)
        head_over(3, 24)

    relay()
    neighbours()
    wires.start(downs_ref.at[0, :, beside], downs_ref.at[1, :, beside], 26, sibling)
    wires.start(downs_ref.at[0, :, across], downs_ref.at[1, :, across], 27, sibling)
    finish()
    wires.start(downs_ref.at[0, :, corner], downs_ref.at[1, :, corner], 28, sibling)
    wires.arrived(downs_ref.at[1, z, me], 4, sibling)
    for r in (1, 2, 3):
        wires.arrived(downs_ref.at[1, (z + r) % 4, me], 17 + r, sibling)
    for number, position in ((26, beside), (27, across), (28, corner)):
        wires.arrived(downs_ref.at[1, :, position], number, sibling)

    kv = all_ref.shape[1] - LANE
    used = kv + ROPE
    tail = jnp.concatenate([downs_ref[k, :, :, :, kv:].reshape(half, LANE) for k in range(2)], axis=0).astype(F32).T
    gains_ref[...] = tail[ROPE : ROPE + 8]
    lead = tail[ROPE : ROPE + 8].astype(LOW)
    small = 0.0
    chunk = 4 * LANE
    for a in range(0, width, chunk):
        row = lax.broadcasted_iota(jnp.int32, (chunk, spot_ref.shape[1]), 0) + a
        here = jnp.where(row == spot_ref[...], 1.0, 0.0).astype(LOW)
        small = small + dot(lead[:, a : a + chunk], here)
    small = small[2:3]
    gain = tail[ROPE : ROPE + 1]

    def normed_step(step, carry):
        here = pl.ds(pl.multiple_of(step * ROW_STEP, ROW_STEP), ROW_STEP)
        store_line(x_ref, here, input_ref[here, :].astype(F32), core)
        value = x_ref[here, :].astype(F32)
        factor = lax.rsqrt(jnp.mean(value * value, axis=-1, keepdims=True) + EPSILON)
        normed_ref[here, :] = (value * factor * gain).astype(LOW)
        return carry

    lax.fori_loop(0, size // ROW_STEP, normed_step, 0)
    for a in range(0, kv + LANE, 3 * LANE):
        b = min(a + 3 * LANE, kv + LANE)
        total = 0.0
        for k in range(2):
            total = total + dot(normed_ref[:, k * half : (k + 1) * half], downs_ref[k, :, :, :, a:b].reshape(half, b - a))
        latents_ref[:, a:b] = total
    low = lax.broadcasted_iota(jnp.int32, (1, LANE), 1) < ROPE
    cuts = ((0, kv - KR), (kv - KR, kv))

    def latent_step(step, carry):
        here = pl.ds(pl.multiple_of(step * ROW_STEP, ROW_STEP), ROW_STEP)
        mine = pl.ds(pl.multiple_of(me * size + step * ROW_STEP, ROW_STEP), ROW_STEP)
        for a, b in cuts:
            value = latents_ref[here, a:b]
            factor = lax.rsqrt(jnp.mean(value * value, axis=-1, keepdims=True) + EPSILON)
            all_ref[mine, a:b] = (value * factor * small[:, a:b]).astype(LOW)
        rope = pltpu.roll(jnp.where(low, latents_ref[here, kv:], 0.0), NOPE, 1)
        rope = (
            rope * cos_ref[here, :]
            + pltpu.roll(rope, ROPE // 2, 1) * lift_ref[here, :]
            + pltpu.roll(rope, LANE - ROPE // 2, 1) * drop_ref[here, :]
        )
        all_ref[mine, kv:] = rope.astype(LOW)
        return carry

    lax.fori_loop(0, size // ROW_STEP, latent_step, 0)
    cut = (kv + LANE) // LANE // 2 * LANE
    columns = (pl.ds(0, cut), pl.ds(cut, kv + LANE - cut))
    relay, neighbours, finish, leave_latents = gather_square(
        lambda position, k: all_ref.at[rows_of(position, size), columns[k]],
        [all_ref.at[rows_of(me, size), columns[k]] for k in range(2)],
        wires,
        30,
    )

    when(z == 2, lambda: wires.arrived(blocks.at[0], 21, down))
    when(z == 1, lambda: wires.arrived(blocks.at[3], 21, up))
    end = jnp.where(z == 2, 6, 0)
    inner_want, inner_asked = sources_ref[end + core], sources_ref[end + 1 - core]
    want, asked = sources_ref[2 * z + core], sources_ref[2 * z + 1 - core]
    stage[0] = blocks[inner_asked // 2]
    wires.start(stage.at[0], theirs.at[0], 36, sibling)
    stage[1] = jnp.where(edge, cot_ref[...], blocks[asked // 2])
    wires.start(stage.at[1], theirs.at[1], 37, sibling)
    wires.arrived(theirs.at[0], 36, sibling)
    stage[2] = jnp.where(inner_want % 2 == core, blocks[inner_want // 2], theirs[0])
    when(z == 2, lambda: wires.start(stage.at[2], got, 38, up))
    when(z == 1, lambda: wires.start(stage.at[2], got, 38, down))
    relay()
    neighbours()
    finish()

    @pl.when(z == 1)
    def _():
        head_in(2, 8, up)
        head_hop(2, 40, down)
        head_over(2, 42)
        head_in(3, 22, up)
        head_hop(3, 44, down)
        head_over(3, 46)

    @pl.when(z == 2)
    def _():
        head_in(1, 6, down)
        head_hop(1, 40, up)
        head_over(1, 42)
        head_in(0, 22, down)
        head_hop(0, 44, up)
        head_over(0, 46)

    when(z == 0, lambda: wires.arrived(got, 38, up))
    when(z == 3, lambda: wires.arrived(got, 38, down))
    wires.arrived(theirs.at[1], 37, sibling)

    def rows_step(step, carry):
        here = pl.ds(pl.multiple_of(step * ROW_STEP, ROW_STEP), ROW_STEP)
        mine = jnp.where(edge, cot_ref[here, :], blocks[want // 2, here, :])
        local = jnp.where(want % 2 == core, mine, theirs[1, here, :])
        value = jnp.where(edge & (want // 2 != z), got[here, :], local).astype(F32)
        position = me * size + step * ROW_STEP + lax.broadcasted_iota(jnp.int32, (ROW_STEP, 1), 0)
        value = jnp.where(position < length_ref[0], value, 0.0)
        store_line(own_cot_ref, here, value, core)
        store_line(scaled, here, RESIDUAL_SCALE * value, core)
        return carry

    lax.fori_loop(0, size // ROW_STEP, rows_step, 0)

    keep_cot = pltpu.make_async_copy(scaled, cots_ref.at[rows_of(me, size), :], local_sems.at[2])
    keep_cot.start()
    halves = (pl.ds(0, half), pl.ds(half, half))
    relay, neighbours, finish, leave_cots = gather_square(
        lambda position, k: cots_ref.at[rows_of(position, size), halves[k]],
        [scaled.at[:, halves[k]] for k in range(2)],
        wires,
        50,
    )

    @pl.when(z == 0)
    def _():
        head_in(1, 8, up)
        head_over(1, 24)
        head_in(2, 40, up)
        head_over(2, 42)

    @pl.when(z == 3)
    def _():
        head_in(2, 6, down)
        head_over(2, 24)
        head_in(1, 40, down)
        head_over(1, 42)

    relay()

    @pl.when(z == 0)
    def _():
        head_in(3, 44, up)
        head_over(3, 46)

    @pl.when(z == 3)
    def _():
        head_in(0, 44, down)
        head_over(0, 46)


    head_back(z, 10)
    when(z == 1, lambda: [head_back(at, number) for at, number in ((0, 24), (2, 42), (3, 46))])
    when(z == 2, lambda: [head_back(at, number) for at, number in ((3, 24), (1, 42), (0, 46))])
    when(z == 0, lambda: [head_back(at, number) for at, number in ((1, 24), (2, 42), (3, 46))])
    when(z == 3, lambda: [head_back(at, number) for at, number in ((2, 24), (1, 42), (0, 46))])

    neighbours()
    finish()
    keep_cot.wait()
    when(z > 0, lambda: wires.arrived(above_ref, 48, down))
    when(z < 3, lambda: wires.arrived(below_ref, 49, up))

    leave_cots()
    when(z < 3, lambda: wires.sent(part_ref, 48, up))
    when(z > 0, lambda: wires.sent(part_ref, 49, down))
    for number in (1, 2, 3, 4, 18, 19, 20):
        wires.sent(down_ref, number, sibling)
    leave_downs()
    for number in (26, 27, 28):
        wires.sent(downs_ref.at[0, :, me], number, sibling)
    leave_latents()
    for number in (36, 37):
        wires.sent(stage.at[0], number, sibling)

    def head_sent(*numbers):
        for number in numbers:
            for ref, _, k in heads:
                wires.sent(ref, number + k, sibling)

    head_sent(10, 24, 42, 46)
    when(z < 2, lambda: wires.sent(cot_ref, 0, sibling))
    when(z > 1, lambda: wires.sent(cot_ref, 5, sibling))
    when(z < 3, lambda: head_sent(6))
    when(z > 0, lambda: head_sent(8))

    @pl.when(inner)
    def _():
        wires.sent(cot_ref, 21, sibling)
        wires.sent(cot_ref, 38, sibling)
        head_sent(22, 40, 44)


def bring(sources, length, down_pack, qk_pack, out_pack, cot, values, spot, tables, part):
    size, width = cot.shape
    columns = down_pack.shape[1]
    vmem, anywhere = pl.BlockSpec(memory_space=pltpu.VMEM), pl.BlockSpec(memory_space=pl.ANY)
    smem = pl.BlockSpec(memory_space=pltpu.SMEM)
    return pl.pallas_call(
        bring_kernel,
        in_specs=[smem, smem] + [vmem] * 9 + [anywhere],
        out_specs=[vmem, anywhere, anywhere] + [vmem] * 5 + [anywhere] * 3 + [vmem],
        out_shape=[
            jax.ShapeDtypeStruct((2, 4, PLANE) + down_pack.shape, LOW),
            jax.ShapeDtypeStruct((4, 2) + qk_pack.shape, LOW),
            jax.ShapeDtypeStruct((2, 4) + out_pack.shape, LOW),
            jax.ShapeDtypeStruct((size, width), LOW),
            jax.ShapeDtypeStruct((size, width), LOW),
            jax.ShapeDtypeStruct((size, columns), F32),
            jax.ShapeDtypeStruct((8, width), F32),
            jax.ShapeDtypeStruct((PLANE * size, columns), LOW),
            jax.ShapeDtypeStruct((PLANE * size, width), LOW),
            jax.ShapeDtypeStruct(part.shape, LOW),
            jax.ShapeDtypeStruct(part.shape, LOW),
            jax.ShapeDtypeStruct((size, width), LOW),
        ],
        scratch_shapes=[
            pltpu.VMEM((size, width), LOW),
            pltpu.VMEM((4, size, width), LOW),
            pltpu.VMEM((size, width), LOW),
            pltpu.VMEM((2, size, width), LOW),
            pltpu.VMEM((3, size, width), LOW),
            pltpu.SemaphoreType.DMA((56,)),
            pltpu.SemaphoreType.DMA((56,)),
            pltpu.SemaphoreType.DMA((3,)),
        ],
        compiler_params=pltpu.CompilerParams(collective_id=7, has_side_effects=True, vmem_limit_bytes=56 << 20),
        cost_estimate=pl.CostEstimate(flops=0, bytes_accessed=1 << 20, transcendentals=0),
        name="bring",
    )(sources, length, down_pack, qk_pack, out_pack, cot, values, spot, *tables, part)


def finish_kernel(
    sources_ref,
    qcot_ref,
    kvcot_ref,
    rope_ref,
    weight_ref,
    lat_ref,
    latents_ref,
    smalls_ref,
    cos_ref,
    lift_ref,
    drop_ref,
    x_ref,
    normed_ref,
    downs_ref,
    gain_ref,
    after_grad_ref,
    mlp_dgain_ref,
    own_ref,
    down_ref,
    head_ref,
    dealt_ref,
    input_ref,
    gains,
    query_ref,
    key_ref,
    part0,
    part1,
    got2,
    got3,
    cot_ref,
    gains_came,
    grad_block,
    keep,
    away,
    came,
    got0,
    got1,
    line,
    lines,
    head_came,
    head_part,
    head_lines,
    blocks,
    theirs,
    stage,
    send_sems,
    recv_sems,
    square_send,
    square_recv,
    local_sems,
):
    z, core, sibling = line_peers()
    me, beside, across, corner = square()
    wires = Wires(send_sems, recv_sems)
    turns = [line_peer((z + r) % 4, core) for r in (1, 2, 3)]
    greet_all([sibling, {"tp": beside}, {"tp": across}] + turns)
    up, down = line_peer((z + 1) % 4, core), line_peer((z + 3) % 4, core)
    edge = (z == 0) | (z == 3)
    half = normed_ref.shape[1] // 2
    used = cot_ref.shape[1]
    size = normed_ref.shape[0]
    groups, rows_all, columns = weight_ref.shape
    q_rows = query_ref.shape[2]
    qr = groups * q_rows
    kv = lat_ref.shape[1] - LANE
    slim = part0.shape[1]

    keep_own = pltpu.make_async_copy(own_ref, blocks.at[z], local_sems.at[0])
    keep_own.start()

    @pl.when(z < 2)
    def _():
        wires.start(own_ref, blocks.at[z], 0, up)

    @pl.when(z > 1)
    def _():
        wires.start(own_ref, blocks.at[z], 12, down)

    w_query = weight_ref[:, :q_rows].reshape(qr, columns)
    w_pair = weight_ref[:, q_rows:].reshape(groups * (rows_all - q_rows), columns)

    def prepare(position):
        here = rows_of(position, size)
        back = dot_nt(qcot_ref[here, :], w_query)
        part0[here, :] = back[:, :slim].astype(LOW)
        part1[here, 0 : qr - slim] = back[:, slim:].astype(LOW)
        part1[here, qr - slim : kv - slim] = dot_nt(kvcot_ref[here, :], w_pair).astype(LOW)
        part1[here, kv - slim :] = rope_ref[here, :]

    def head_gradients():
        for i in range(4):
            for c in range(2):
                g = 2 * i + c
                if g % 4 == 0:
                    grads = dot_tn(lat_ref[:, g * q_rows : (g + 4) * q_rows], qcot_ref[...]).astype(LOW)
                query_ref[i, c] = grads[(g % 4) * q_rows : (g % 4 + 1) * q_rows]
        pair_rows = rows_all - q_rows
        grads = dot_tn(lat_ref[:, qr:kv], kvcot_ref[...]).astype(LOW)
        for i in range(4):
            for c in range(2):
                g = 2 * i + c
                key_ref[i, c] = grads[g * pair_rows : (g + 1) * pair_rows]
        wires.start(query_ref.at[:, 1 - core], head_came.at[:, pl.ds(0, q_rows)], 1, sibling)
        wires.start(key_ref.at[:, 1 - core], head_came.at[:, pl.ds(q_rows, pair_rows)], 2, sibling)

    copies = reduce_square(
        (part0, part1),
        (got2, got3),
        (square_send.at[pl.ds(6, 6)], square_recv.at[pl.ds(6, 6)]),
        prepare,
        head_gradients,
    )
    gains[...] = jnp.zeros_like(gains)
    keep_own.wait()

    @pl.when((z == 1) | (z == 2))
    def _():
        wires.arrived(blocks.at[z - 1], 0, down)
        wires.arrived(blocks.at[z + 1], 12, up)

    @pl.when(z == 1)
    def _():
        wires.start(blocks.at[0], blocks.at[0], 19, up)

    @pl.when(z == 2)
    def _():
        wires.start(blocks.at[3], blocks.at[3], 19, down)

    end = jnp.where(z == 2, 6, 0)
    inner_want, inner_asked = sources_ref[end + core], sources_ref[end + 1 - core]
    want, asked = sources_ref[2 * z + core], sources_ref[2 * z + 1 - core]

    def last_hop():
        @pl.when(z == 2)
        def _():
            wires.arrived(blocks.at[0], 19, down)

        @pl.when(z == 1)
        def _():
            wires.arrived(blocks.at[3], 19, up)

        stage[0] = blocks[inner_asked // 2]
        wires.start(stage.at[0], theirs.at[0], 10, sibling)
        stage[1] = jnp.where(edge, blocks[z], blocks[asked // 2])
        wires.start(stage.at[1], theirs.at[1], 11, sibling)
        wires.arrived(theirs.at[0], 10, sibling)
        wires.sent(stage.at[0], 10, sibling)
        stage[0] = jnp.where(inner_want % 2 == core, blocks[inner_want // 2], theirs[0])

        @pl.when(z == 2)
        def _():
            wires.start(stage.at[0], dealt_ref, 20, up)

        @pl.when(z == 1)
        def _():
            wires.start(stage.at[0], dealt_ref, 20, down)

    def latent_step(step, carry):
        here = pl.ds(pl.multiple_of(step * ROW_STEP, ROW_STEP), ROW_STEP)
        mine = pl.ds(pl.multiple_of(me * size + step * ROW_STEP, ROW_STEP), ROW_STEP)
        total = jnp.concatenate(
            [
                part[mine, :].astype(F32) + come[1, here, :].astype(F32) + come[2, here, :].astype(F32)
                for part, come in ((part0, got2), (part1, got3))
            ],
            axis=1,
        )
        for a, b in ((0, qr), (qr, kv)):
            grad, value = total[:, a:b], latents_ref[here, a:b]
            factor = lax.rsqrt(jnp.mean(value * value, axis=-1, keepdims=True) + EPSILON)
            weighted = grad * smalls_ref[:, a:b]
            inside = jnp.mean(weighted * value, axis=-1, keepdims=True)
            gains[2:3, a:b] += jnp.sum(grad * value * factor, axis=0, keepdims=True)
            cot_ref[here, a:b] = (factor * weighted - value * (factor * factor * factor) * inside).astype(LOW)
        rope = total[:, kv:]
        rope = (
            rope * cos_ref[here, :]
            - pltpu.roll(rope, ROPE // 2, 1) * lift_ref[here, :]
            - pltpu.roll(rope, LANE - ROPE // 2, 1) * drop_ref[here, :]
        )
        cot_ref[here, kv:] = pltpu.roll(rope, NOPE, 1)[:, : used - kv].astype(LOW)
        return carry

    lax.fori_loop(0, size // ROW_STEP, latent_step, 0)
    rows = keep.shape[0] // 16
    block = half // 4

    def gradients(k, target):
        for pair in range(2):
            a = k * half + pair * 2 * block
            grads = dot_tn(normed_ref[:, a : a + 2 * block], cot_ref[...]).astype(LOW)
            for i in range(2):
                for t in range(PLANE):
                    row = (t * 4 + pair * 2 + i) * rows
                    target[row : row + rows, :] = grads[i * block + t * rows : i * block + (t + 1) * rows]

    gradients(1, away)
    wires.start(away, came, 3, sibling)
    gradients(0, keep)

    wires.arrived(head_came.at[:, pl.ds(0, q_rows)], 1, sibling)
    wires.arrived(head_came.at[:, pl.ds(q_rows, key_ref.shape[2])], 2, sibling)
    for i in range(4):
        for ref, a in ((query_ref, 0), (key_ref, q_rows)):
            b = a + ref.shape[2]
            head_part[i, a:b] = (ref[i, core].astype(F32) + head_came[i, a:b].astype(F32)).astype(LOW)
    for r in (1, 2, 3):
        wires.start(head_part.at[(z + r) % 4], head_lines.at[r - 1], 3 + r, turns[r - 1])
    wires.arrived(came, 3, sibling)

    def add_step(step, carry):
        here = pl.ds(pl.multiple_of(step * rows, 16), rows)
        keep[here, :] = (keep[here, :].astype(F32) + came[here, :].astype(F32)).astype(LOW)
        return carry

    lax.fori_loop(0, 16, add_step, 0)
    cut = got0.shape[2]
    parts = (keep.at[:, pl.ds(0, cut)], keep.at[:, pl.ds(cut, used - cut)])
    input_rows = grad_block.shape[0]

    def input_gradient():
        last_hop()

        def input_step(step, carry):
            here = pl.ds(pl.multiple_of(step * input_rows, input_rows), input_rows)
            bring_block = pltpu.make_async_copy(after_grad_ref.at[here, :], grad_block, local_sems.at[3])
            bring_block.start()
            cot = cot_ref[here, :]
            grad = jnp.concatenate([dot_nt(cot, downs_ref[k, :, :used]) for k in range(2)], axis=1)
            value = x_ref[here, :].astype(F32)
            factor = lax.rsqrt(jnp.mean(value * value, axis=-1, keepdims=True) + EPSILON)
            weighted = grad * gain_ref[...]
            inside = jnp.mean(weighted * value, axis=-1, keepdims=True)
            gains[0:1, :] += jnp.sum(grad * value * factor, axis=0, keepdims=True)
            total = factor * weighted - value * (factor * factor * factor) * inside
            bring_block.wait()
            total = total + grad_block[...]
            first, second = total[:, :half], total[:, half:]
            evens, odds = jnp.where(core == 0, first, second), jnp.where(core == 0, second, first)
            for i in range(4):
                piece = slice(i * block, (i + 1) * block)
                input_ref[here, 2 * i * block : (2 * i + 1) * block] = evens[:, piece].astype(LOW)
                input_ref[here, (2 * i + 1) * block : (2 * i + 2) * block] = odds[:, piece].astype(LOW)
            return carry

        lax.fori_loop(0, size // input_rows, input_step, 0)
        gains[1:2, :] = mlp_dgain_ref[...]
        for row in range(2):
            first, second = gains[row : row + 1, :half], gains[row : row + 1, half:]
            gains[row : row + 1, :half] = jnp.where(core == 0, first, second)
            gains[row : row + 1, half:] = jnp.where(core == 0, second, first)
        wires.start(gains, gains_came.at[0], 13, sibling)

    copies += reduce_square(
        parts,
        (got0, got1),
        (square_send.at[pl.ds(0, 6)], square_recv.at[pl.ds(0, 6)]),
        lambda position: None,
        input_gradient,
    )
    for k, (a, b) in enumerate(((0, cut), (cut, used))):
        got_k = (got0, got1)[k]
        total = keep[rows_of(me, 4 * rows), a:b].astype(F32) + got_k[1].astype(F32) + got_k[2].astype(F32)
        line[:, a:b] = total.astype(LOW)
    for r in (1, 2, 3):
        wires.start(line.at[rows_of((z + r) % 4, rows), :], lines.at[r - 1], 6 + r, turns[r - 1])

    for number, (slot, peer) in enumerate(((0, sibling), (1, {"tp": beside}), (2, {"tp": across}))):
        wires.arrived(gains_came.at[slot], 13 + number, peer)
        wires.sent(gains, 13 + number, peer)
        gains[...] += gains_came[slot]
        if number < 2:
            wires.start(gains, gains_came.at[slot + 1], 14 + number, ({"tp": beside}, {"tp": across})[number])
    for r in (1, 2, 3):
        wires.start(gains, gains_came.at[2 + r], 15 + r, turns[r - 1])
    for r in (1, 2, 3):
        wires.arrived(head_lines.at[r - 1], 3 + r, turns[r - 1])
    head_ref[...] = head_part[z].astype(F32) + (
        head_lines[0].astype(F32) + head_lines[1].astype(F32) + head_lines[2].astype(F32)
    )
    for r in (1, 2, 3):
        wires.arrived(lines.at[r - 1], 6 + r, turns[r - 1])
    down_ref[...] = line[rows_of(z, rows), :].astype(F32) + (
        lines[0].astype(F32) + lines[1].astype(F32) + lines[2].astype(F32)
    )
    for r in (1, 2, 3):
        wires.arrived(gains_came.at[2 + r], 15 + r, turns[r - 1])
    for r in (1, 2, 3):
        wires.sent(gains, 15 + r, turns[r - 1])
    gains[...] += gains_came[3] + (gains_came[4] + gains_came[5])
    wires.arrived(theirs.at[1], 11, sibling)

    @pl.when(z == 3)
    def _():
        wires.arrived(dealt_ref, 20, down)

    @pl.when(z == 0)
    def _():
        wires.arrived(dealt_ref, 20, up)

    mine = jnp.where(edge, blocks[z], blocks[want // 2])
    local = jnp.where(want % 2 == core, mine, theirs[1])
    dealt_ref[...] = jnp.where(edge & (want // 2 != z), dealt_ref[...], local)
    for copy in copies:
        copy.wait_send()
    wires.sent(query_ref.at[:, 0], 1, sibling)
    wires.sent(key_ref.at[:, 0], 2, sibling)
    wires.sent(away, 3, sibling)
    for r in (1, 2, 3):
        wires.sent(head_part.at[0], 3 + r, sibling)
        wires.sent(line.at[pl.ds(0, rows), :], 6 + r, sibling)
    wires.sent(stage.at[1], 11, sibling)

    @pl.when(z < 2)
    def _():
        wires.sent(own_ref, 0, sibling)

    @pl.when(z > 1)
    def _():
        wires.sent(own_ref, 12, sibling)

    @pl.when((z == 1) | (z == 2))
    def _():
        wires.sent(stage.at[0], 19, sibling)
        wires.sent(stage.at[0], 20, sibling)


def finish_all(sources, cots, rope, weights, q_rows, lat, latents, smalls, tables, values, normed, downs, gain, grad, dgain, own):
    size, width = normed.shape
    used = lat.shape[1] - LANE + ROPE
    rows = width // (LINE * PLANE)
    groups, head_rows, columns = weights.shape
    slim = lat.shape[1] // LANE // 2 * LANE + LANE
    cut = used // LANE // 2 * LANE
    vmem, smem = pl.BlockSpec(memory_space=pltpu.VMEM), pl.BlockSpec(memory_space=pltpu.SMEM)
    anywhere = pl.BlockSpec(memory_space=pl.ANY)
    mine, other = (4, 2, q_rows, columns), (4, 2, head_rows - q_rows, columns)
    return pl.pallas_call(
        finish_kernel,
        in_specs=[smem] + [vmem] * 14 + [anywhere, vmem, anywhere],
        out_specs=[vmem] * 5,
        out_shape=[
            jax.ShapeDtypeStruct((rows, used), F32),
            jax.ShapeDtypeStruct((head_rows, columns), F32),
            jax.ShapeDtypeStruct((size, width), LOW),
            jax.ShapeDtypeStruct((size, width), LOW),
            jax.ShapeDtypeStruct((8, width), F32),
        ],
        scratch_shapes=[
            pltpu.VMEM(mine, LOW),
            pltpu.VMEM(other, LOW),
            pltpu.VMEM((lat.shape[0], slim), LOW),
            pltpu.VMEM((lat.shape[0], lat.shape[1] - slim), LOW),
            pltpu.VMEM((3, size, slim), LOW),
            pltpu.VMEM((3, size, lat.shape[1] - slim), LOW),
            pltpu.VMEM((size, used), LOW),
            pltpu.VMEM((6, 8, width), F32),
            pltpu.VMEM((256, width), F32),
        ]
        + [pltpu.VMEM((16 * rows, used), LOW)] * 3
        + [
            pltpu.VMEM((3, 4 * rows, cut), LOW),
            pltpu.VMEM((3, 4 * rows, used - cut), LOW),
            pltpu.VMEM((4 * rows, used), LOW),
            pltpu.VMEM((3, rows, used), LOW),
            pltpu.VMEM((4, head_rows, columns), LOW),
            pltpu.VMEM((4, head_rows, columns), LOW),
            pltpu.VMEM((3, head_rows, columns), LOW),
            pltpu.VMEM((4, size, width), LOW),
            pltpu.VMEM((2, size, width), LOW),
            pltpu.VMEM((2, size, width), LOW),
            pltpu.SemaphoreType.DMA((21,)),
            pltpu.SemaphoreType.DMA((21,)),
            pltpu.SemaphoreType.DMA((12,)),
            pltpu.SemaphoreType.DMA((12,)),
            pltpu.SemaphoreType.DMA((4,)),
        ],
        compiler_params=pltpu.CompilerParams(collective_id=8, has_side_effects=True, vmem_limit_bytes=67 * 10**6),
        cost_estimate=pl.CostEstimate(flops=0, bytes_accessed=240 << 20, transcendentals=0),
        name="finish",
    )(sources, *cots, rope, weights, lat, latents, smalls, *tables, values, normed, downs, gain, grad, dgain, own)


def per_device(
    block_input,
    seq_lengths,
    dealt_order,
    out_cotangent,
    attn_gain,
    query_down,
    query_gain,
    latent_down,
    latent_gain,
    query_up,
    latent_up,
    output_matrix,
    mlp_gain,
    gate_weight,
    up_weight,
    down_matrix,
):
    line = special()
    tp_count = lax.axis_size("tp")
    fsdp_count = lax.axis_size("fsdp")
    group = lax.axis_index("fsdp")
    column = lax.axis_index("tp")
    _, local_len, width = block_input.shape
    full_len = local_len * tp_count
    own_len = jnp.take(seq_lengths, group)
    local_pos = column * local_len + jnp.arange(local_len, dtype=jnp.int32)
    valid = (local_pos < own_len).astype(F32)[:, None]
    order = to_line if line else (lambda values: values)
    unorder = from_line if line else (lambda values: values)
    bounds = [(0, width // 2), (width // 2, width)] if line else [(0, width)]

    qr = query_down.shape[1]
    latent_rows = query_down.shape[0]
    small_q, small_l = query_gain.shape[0], latent_gain.shape[0]
    used = qr + KR + ROPE
    padded = -(-(used + 3) // LANE) * LANE
    small = jnp.concatenate([query_gain, latent_gain, jnp.zeros((latent_rows,), F32)])
    if small_q + small_l <= latent_rows:
        small = small[:latent_rows]
        extra = 0
    else:
        small = small[: 2 * latent_rows]
        extra = 1
    down_pack = jnp.concatenate(
        [
            query_down.astype(LOW),
            latent_down.astype(LOW),
            attn_gain.astype(LOW)[:, None],
            mlp_gain.astype(LOW)[:, None],
            small.astype(LOW).reshape(1 + extra, latent_rows).T,
            jnp.zeros((latent_rows, padded - used - 3 - extra), LOW),
        ],
        axis=1,
    )

    heads = query_up.shape[1] // QKD
    even = heads + heads % 2
    q_rows, l_rows = query_up.shape[0], latent_up.shape[0]
    o_rows = output_matrix.shape[0] // 2
    half_width = even * VD

    def pad_heads(values, size, to):
        rows = values.shape[0]
        values = values.reshape(rows, heads, size)
        return jnp.pad(values, ((0, 0), (0, even - heads), (0, to - size))).reshape(rows, even * to)

    out_low = pad_heads(output_matrix.astype(LOW), VD, VD)
    qk_pack = jnp.concatenate([pad_heads(query_up.astype(LOW), QKD, LANE), pad_heads(latent_up.astype(LOW), LANE, LANE)], axis=0)
    units = gate_weight.shape[1]
    cut = 768 if units == 1600 else units // 2
    pieces = [(0, cut), (cut, units)]
    if line:
        tiles = []
        for a in range(0, units, UNIT):
            b = min(a + UNIT, units)
            tiles.append([weight[:, a:b].astype(LOW) for weight in (gate_weight, up_weight, down_matrix)])
        tiles[-1].append(jnp.zeros((gate_weight.shape[0], -3 * (units % UNIT) % LANE), LOW))
        mlp_packs = [jnp.concatenate(sum(part, []), axis=1) for part in (tiles[:3], tiles[3:])]
    else:
        mlp_packs = [
            jnp.concatenate(
                [gate_weight[:, a:b].astype(LOW), up_weight[:, a:b].astype(LOW), down_matrix[:, a:b].astype(LOW)], axis=1
            )
            for a, b in pieces
        ]
    cot_source = jnp.argsort(dealt_order).astype(jnp.int32)
    if line:
        owners = jnp.arange(fsdp_count * tp_count, dtype=jnp.int32)[:, None]
        spot = jnp.concatenate(
            [
                (owners * latent_rows + jnp.arange(small_q, dtype=jnp.int32)).reshape(-1),
                (owners * latent_rows + small_q + jnp.arange(small_l, dtype=jnp.int32)).reshape(-1),
            ]
        )
        block = width // LINE
        index = spot // block
        spot = ((index % 2) != group % 2) * (width // 2) + index // 2 * block + spot % block
        own_tables = head_tables(*rotary_tables(local_pos))
        downs, natural, out_slabs, own_cot, normed_low, latents, gain_rows, latent_all, mlp_cot, above, below, block_low = bring(
            cot_source,
            own_len[None],
            down_pack,
            qk_pack,
            out_low,
            out_cotangent[0],
            block_input[0],
            spot[None],
            own_tables,
            mlp_packs[0],
        )
        first_steps = [above, below, gather_two(above, below)]
        down_all = downs.reshape(width, padded)
        grad_out = own_cot
        out_slabs = [slab.reshape(width // 2, half_width) for slab in out_slabs]
        first_low = mlp_packs[0]
        gain_attn, gain_mlp = gain_rows[0], gain_rows[1]
        smalls = gain_rows[2].reshape(2, 4, -1)
        smalls = jnp.stack(by_core(smalls[0], smalls[1]), axis=1).reshape(-1, latent_rows)
        natural = natural.reshape(fsdp_count, q_rows + l_rows, -1)
    else:
        down_all = lax.all_gather(down_pack, ("fsdp", "tp"), axis=0, tiled=True)
        natural = lax.all_gather(qk_pack, "fsdp")
        out_slabs = [lax.all_gather(out_low, "fsdp", axis=0, tiled=True)]
        mlp_slabs = [[lax.all_gather(pack, "fsdp", axis=0, tiled=True)] for pack in mlp_packs]
        grad_out = valid * deal_plain(out_cotangent[0], cot_source).astype(F32)
        mlp_cot = lax.all_gather((RESIDUAL_SCALE * grad_out).astype(LOW), "tp", axis=0, tiled=True)
        gain_attn = down_all[:, used].astype(F32)
        gain_mlp = down_all[:, used + 1].astype(F32)
        smalls = down_all[:, used + 2 : used + 3 + extra].astype(F32).reshape(-1, latent_rows, 1 + extra)
        smalls = jnp.swapaxes(smalls, 1, 2).reshape(-1, latent_rows * (1 + extra))
        block_low = block_input[0]
    w_qup = natural[:, :q_rows].reshape(-1, even * LANE)
    w_kvup = natural[:, q_rows:].reshape(-1, even * LANE)
    w_down = down_all[:, :used]
    gain_query = smalls[:, :small_q].reshape(-1)
    gain_latent = smalls[:, small_q : small_q + small_l].reshape(-1)

    block_vals = block_low.astype(F32)
    cos_local, sin_local = rotary_tables(local_pos)
    cos_local = jnp.concatenate([cos_local, cos_local], axis=1)
    sin_local = jnp.concatenate([sin_local, sin_local], axis=1)
    if not line:
        normed_low = normalize(block_vals, gain_attn)[0].astype(LOW)
        latents = dot(normed_low, w_down)
        rope_raw = latents[:, qr + KR :]
        rotary_key = rope_raw * cos_local + turn_half(rope_raw) * sin_local
        rotary_key = jnp.pad(rotary_key, ((0, 0), (NOPE, LANE - NOPE - ROPE)))
        parts = [
            normalize(latents[:, :qr], gain_query)[0],
            normalize(latents[:, qr : qr + KR], gain_latent)[0],
            rotary_key,
        ]
        latent_all = lax.all_gather(jnp.concatenate(parts, axis=1).astype(LOW), "tp", axis=0, tiled=True)
    query_latent, kv_latent = latents[:, :qr], latents[:, qr : qr + KR]

    def factor_of(values):
        return lax.rsqrt(jnp.mean(values * values, axis=-1, keepdims=True) + EPSILON)

    query_all = latent_all[:, :qr]
    comp_all = latent_all[:, qr : qr + KR]
    rope_all = latent_all[:, qr + KR :]

    tables = head_tables(*rotary_tables(jnp.arange(full_len, dtype=jnp.int32)))
    bias = jnp.where(jnp.arange(full_len, dtype=jnp.int32) < own_len, 0.0, MASKED).astype(F32)[None, :]
    queries, key_value, mixed, lse = attend(latent_all, natural, q_rows, bias, tables)
    if line:
        mixed, first_steps[2], second_low = tie(mixed, first_steps[2], mlp_packs[1])
        second_steps = list(gather_one(second_low))
        first_steps.append(gather_three(first_steps[2]))
    after_attn, mlp_in = enter_mlp(mixed, out_slabs, block_low, gain_mlp)
    if line:
        mlp_in, *second_steps = tie(mlp_in, *second_steps)
        second_steps.append(gather_two(*second_steps))
    mlp_in = gather_tp(mlp_in, "gather_normed", 4)
    if line:
        mlp_in, first_steps[3], second_steps[2] = tie(mlp_in, first_steps[3], second_steps[2])
        second_steps.append(gather_three(second_steps[2]))
        own = assemble(first_low, *first_steps)
        mlp_slabs = [[own.reshape(width // 2, -1), swap_cores(own).reshape(width // 2, -1)]]

    def split(values):
        return values.reshape(4, -1, values.shape[-1])

    def branch_sum(parts):
        return jnp.concatenate(
            [lax.psum_scatter(piece, "tp", scatter_dimension=0, tiled=True).astype(F32) for piece in parts], axis=1
        )

    def finish(branch):
        return unorder((valid * (after_attn + RESIDUAL_SCALE * branch)).astype(LOW))

    if line:
        first_acts, first_grads = units_tiles(mlp_in, mlp_cot, mlp_slabs[0])
        own, other, second_steps[3] = tie(*first_grads, second_steps[3])
        slab = assemble(second_low, *second_steps)
        mlp_slabs.append([slab.reshape(width // 2, -1), swap_cores(slab).reshape(width // 2, -1)])
        first_total = line_sum(split(plus(own, swap_cores(other))))
        second_acts, second_grads = units_tiles(mlp_in, mlp_cot, mlp_slabs[1])
        second_acts, own, other = tie(second_acts, *second_grads)
        swapped = swap_cores(other)
        back_low, ff_low = [], []
        for k, pair in enumerate(zip(*mlp_slabs)):
            back, *ff_low = close_tiles([first_acts, second_acts], list(pair), k * (width // 2 // UNIT), ff_low)
            back_low.append(back)
        second_part = split(plus(own, swapped))
        *back_low, first_total, second_part = tie(*back_low, first_total, second_part)
        second_total = line_sum(second_part)
    else:
        mlp_grads = []
        back, branch = 0.0, 0.0
        for (a, b), (slab,) in zip(pieces, mlp_slabs):
            size = b - a
            gate, up = dot(mlp_in, slab[:, :size]), dot(mlp_in, slab[:, size : 2 * size])
            sigma = jax.nn.sigmoid(gate)
            activated = (gate * sigma * up).astype(LOW)
            grad_act = dot(mlp_cot, slab[:, 2 * size :])
            gate_cot = (grad_act * up * sigma * (1.0 + gate * (1.0 - sigma))).astype(LOW)
            up_cot = (grad_act * gate * sigma).astype(LOW)
            back += dot_nt(gate_cot, slab[:, :size]) + dot_nt(up_cot, slab[:, size : 2 * size])
            branch += dot_nt(activated, slab[:, 2 * size :])
            grads = [dot_tn(mlp_in, gate_cot), dot_tn(mlp_in, up_cot), dot_tn(mlp_cot, activated)]
            mlp_grads.append(jnp.concatenate([grad.astype(LOW) for grad in grads], axis=1))
        back_low = [back.astype(LOW)]
        ff_low = [branch.astype(LOW)]
    grad_after, mlp_gain_grad, attn_cot = leave_mlp(back_low, after_attn, grad_out, gain_mlp)
    attn_cot = gather_tp(attn_cot, "gather_cot", 5)
    if line:
        attn_cot, second_total, *ff_low = tie(attn_cot, second_total, *ff_low)
        ff_sum = branch_sum(ff_low)
    else:
        mlp_sums = [lax.psum_scatter(grads, "fsdp", scatter_dimension=0, tiled=True).astype(F32) for grads in mlp_grads]
        block_output = deal_plain(finish(branch_sum(ff_low)), dealt_order)

    grad_mixed = 0.0
    for (a, b), slab in zip(bounds, out_slabs):
        grad_mixed += dot(attn_cot[:, a:b], slab)
    out_grads = [rowwise(dot_tn(attn_cot[:, a:b], mixed).astype(LOW)) for a, b in bounds]
    if line:
        out_part = split(plus(out_grads[0], swap_cores(out_grads[1])))
    query_cot, kv_cot, grad_rope_all = attend_back(
        queries, key_value, rope_all, bias, tables, mixed, grad_mixed.astype(LOW), lse
    )
    if line:
        query_cot, kv_cot, out_part, ff_sum = tie(query_cot, kv_cot, out_part, ff_sum)
        out_sum = line_sum(out_part)
        own_output = finish(ff_sum)
        down_sum, head_sum, block_output, input_grad, gain_sums = finish_all(
            dealt_order,
            (query_cot, kv_cot),
            grad_rope_all,
            natural,
            q_rows,
            latent_all,
            latents,
            jnp.concatenate([gain_query, gain_latent])[None],
            own_tables,
            block_low,
            normed_low,
            downs.reshape(2, width // 2, padded),
            gain_attn[None],
            grad_after,
            mlp_gain_grad[None],
            own_output,
        )
        out_sum, gain_sums = tie(out_sum, gain_sums)
        out_sum = out_sum.astype(F32)
        owner = group * tp_count + column
        spots = ((0, group % 2 * (width // 2) + (group // 2 * tp_count + column) * latent_rows, latent_rows),)
        spots += ((1, spots[0][1], latent_rows), (2, owner * small_q, small_q), (2, qr + owner * small_l, small_l))
        attn_gain_sum, mlp_gain_sum, query_gain_sum, latent_gain_sum = [
            lax.dynamic_slice(gain_sums, (row, at), (1, count))[0] for row, at, count in spots
        ]
    else:
        back_latents = jnp.concatenate(
            [dot_nt(query_cot, w_qup), dot_nt(kv_cot, w_kvup), grad_rope_all], axis=1
        ).astype(LOW)
        grad_latents = lax.psum_scatter(back_latents, "tp", scatter_dimension=0, tiled=True).astype(F32)
        qup_grad = dot_tn(query_all, query_cot).astype(LOW).reshape(fsdp_count, q_rows, even * LANE)
        kvup_grad = dot_tn(comp_all, kv_cot).astype(LOW).reshape(fsdp_count, l_rows, even * LANE)
        head_grads = jnp.concatenate([qup_grad, kvup_grad], axis=1)
        head_sum = lax.psum_scatter(head_grads, "fsdp", scatter_dimension=0, tiled=False).astype(F32)
        out_sum = lax.psum_scatter(out_grads[0], "fsdp", scatter_dimension=0, tiled=True).astype(F32)

    def drop_heads(values, size, to):
        return values.reshape(values.shape[0], even, to)[:, :heads, :size].reshape(values.shape[0], heads * size)

    if not line:
        grad_query_latent, query_gain_grad = norm_back(
            query_latent, factor_of(query_latent), gain_query, grad_latents[:, :qr]
        )
        grad_kv_latent, latent_gain_grad = norm_back(
            kv_latent, factor_of(kv_latent), gain_latent, grad_latents[:, qr : qr + KR]
        )
        grad_rope = grad_latents[:, qr + KR + NOPE : qr + KR + NOPE + ROPE]
        grad_rope = grad_rope * cos_local - turn_half(grad_rope) * sin_local
        latent_cot = jnp.concatenate([grad_query_latent, grad_kv_latent, grad_rope], axis=1).astype(LOW)
        grad_normed = dot_nt(latent_cot, w_down)
        extra_input, attn_gain_grad = norm_back(block_vals, factor_of(block_vals), gain_attn, grad_normed)
        input_grad = (grad_after + extra_input).astype(LOW)

    if line:
        first_total, second_total = first_total.astype(F32), second_total.astype(F32)
        first_cuts = [first_total[:, a : a + UNIT] for a in range(0, first_total.shape[1], UNIT)]
        full = second_total.shape[1] // (3 * UNIT) * 3 * UNIT
        second_cuts = [second_total[:, a : a + UNIT] for a in range(0, full, UNIT)]
        second_cuts += [second_total[:, full + i * REST : full + (i + 1) * REST] for i in range(3)]
        gate_grad, up_grad, down_grad = [
            jnp.concatenate(first_cuts[i::3] + second_cuts[i::3], axis=1) for i in range(3)
        ]
    else:
        down_sum = lax.psum_scatter(
            dot_tn(normed_low, latent_cot), ("fsdp", "tp"), scatter_dimension=0, tiled=True
        )
        gains = jnp.concatenate(
            [
                values.reshape(fsdp_count * tp_count, -1)
                for values in (attn_gain_grad, mlp_gain_grad, query_gain_grad, latent_gain_grad)
            ],
            axis=1,
        )
        gain_sum = lax.psum_scatter(gains, ("fsdp", "tp"), scatter_dimension=0, tiled=True)[0]
        attn_gain_sum, mlp_gain_sum, query_gain_sum, latent_gain_sum = jnp.split(
            gain_sum, [latent_rows, 2 * latent_rows, 2 * latent_rows + small_q]
        )
        sizes = [b - a for a, b in pieces]
        gate_grad, up_grad, down_grad = [
            jnp.concatenate([total[:, i * size : (i + 1) * size] for total, size in zip(mlp_sums, sizes)], axis=1)
            for i in range(3)
        ]
    query_up_grad = drop_heads(head_sum[:q_rows], QKD, LANE)
    latent_up_grad = drop_heads(head_sum[q_rows:], LANE, LANE)
    out_weight_grad = drop_heads(out_sum, VD, VD)

    return (
        block_output[None],
        input_grad[None],
        attn_gain_sum,
        down_sum[:, :qr],
        query_gain_sum,
        down_sum[:, qr:used],
        latent_gain_sum,
        query_up_grad,
        latent_up_grad,
        out_weight_grad,
        mlp_gain_sum,
        gate_grad,
        up_grad,
        down_grad,
    )


def solution(mesh):
    both = P(("fsdp", "tp"))
    rows = P(("fsdp", "tp"), None)
    grid = P("fsdp", "tp")
    tokens = P("fsdp", "tp", None)
    return jax.shard_map(
        per_device,
        mesh=mesh,
        in_specs=(tokens, P(), P(), tokens, both, rows, both, rows, both, grid, grid, grid, both, grid, grid, grid),
        out_specs=(tokens, tokens, both, rows, both, rows, both, grid, grid, grid, both, grid, grid, grid),
        check_vma=False,
    )
```

```python
import functools
import math

import jax
import jax.numpy as jnp
from jax import lax
from jax.experimental import pallas as pl
from jax.experimental.layout import Layout, with_layout_constraint
from jax.experimental.pallas import tpu as pltpu
from jax.sharding import PartitionSpec as P

KR = 256
NOPE = 64
ROPE = 32
VD = 64
QKD = 96
LANE = 128

EPSILON = 1e-05
RESIDUAL_SCALE = 1.4 / math.sqrt(62.0)
ROTARY_BASE = 10000.0
MASKED = -1e30
SCORE_SCALE = 1.0 / math.sqrt(QKD)

F32 = jnp.float32
LOW = jnp.bfloat16
NT = (((1,), (1,)), ((), ()))
TN = (((0,), (0,)), ((), ()))


def dot(left, right):
    return jnp.dot(left, right, preferred_element_type=F32)


def dot_nt(left, right):
    return lax.dot_general(left, right, NT, preferred_element_type=F32)


def dot_tn(left, right):
    return lax.dot_general(left, right, TN, preferred_element_type=F32)


def normalize(values, gain):
    factor = lax.rsqrt(jnp.mean(values * values, axis=-1, keepdims=True) + EPSILON)
    return (values * factor * gain, factor)


def norm_back(values, factor, gain, grad):
    weighted = grad * gain
    inner = jnp.mean(weighted * values, axis=-1, keepdims=True)
    dvalues = factor * weighted - values * (factor * factor * factor) * inner
    dgain = jnp.sum(grad * values * factor, axis=0)
    return (dvalues, dgain)


def rotary_tables(positions):
    halfway = ROPE // 2
    spacing = jnp.arange(halfway, dtype=F32) * (2.0 / ROPE)
    freqs = jnp.power(jnp.float32(ROTARY_BASE), -spacing)
    angle = positions.astype(F32)[:, None] * freqs[None, :]
    return (jnp.cos(angle), jnp.sin(angle))


def turn_half(values):
    halfway = values.shape[-1] // 2
    return jnp.concatenate([-values[..., halfway:], values[..., :halfway]], axis=-1)


def head_tables(cosine, sine):
    count = cosine.shape[0]
    one = jnp.ones((count, NOPE), F32)
    zero = jnp.zeros((count, NOPE), F32)
    half = jnp.zeros_like(sine)
    rest = jnp.zeros((count, LANE - NOPE - ROPE), F32)
    return (
        jnp.concatenate([one, cosine, cosine, rest], axis=1),
        jnp.concatenate([zero, half, sine, rest], axis=1),
        jnp.concatenate([zero, -sine, half, rest], axis=1),
    )


def attend_kernel(
    blocks, q_rows, lat_ref, w_ref, bias_ref, cos_ref, lift_ref, drop_ref, rot_ref, kv_ref, mix_ref, lse_ref
):
    size = lat_ref.shape[0] // blocks
    low = lax.broadcasted_iota(jnp.int32, (1, LANE), 1) < NOPE
    causal = lax.broadcasted_iota(jnp.int32, (size, size), 1) <= lax.broadcasted_iota(
        jnp.int32, (size, size), 0
    )
    half = ROPE // 2
    groups, rows_all, columns = w_ref.shape
    qr = groups * q_rows
    kv = lat_ref.shape[1] - LANE
    w_query = w_ref[:, :q_rows].reshape(qr, columns)
    w_pair = w_ref[:, q_rows:].reshape(groups * (rows_all - q_rows), columns)
    kv_ref[...] = dot(lat_ref[:, qr:kv], w_pair).astype(LOW)
    rope_ref = lat_ref.at[:, pl.ds(kv, LANE)]
    for i in range(blocks):
        rows = pl.ds(i * size, size)
        live = pl.ds(0, (i + 1) * size)
        outs = []
        projected = dot(lat_ref[rows, :qr], w_query).astype(LOW).astype(F32)
        for h in range(2):
            cols = pl.ds(h * LANE, LANE)
            query = projected[:, h * LANE : (h + 1) * LANE]
            query = (
                query * cos_ref[rows, :]
                + pltpu.roll(query, half, 1) * lift_ref[rows, :]
                + pltpu.roll(query, LANE - half, 1) * drop_ref[rows, :]
            ).astype(LOW)
            rot_ref[rows, cols] = query
            pair = kv_ref[live, cols]
            key = jnp.where(low, pair, rope_ref[live, :])
            value = jnp.where(low, jnp.ones_like(pair), pair)
            scores = dot_nt(query, key) * SCORE_SCALE + bias_ref[:, live]
            edge = jnp.where(causal, scores[:, i * size :], MASKED)
            scores = edge if i == 0 else jnp.concatenate([scores[:, : i * size], edge], axis=1)
            top = jnp.max(scores, axis=1, keepdims=True)
            expo = jnp.exp(scores - top)
            out = dot(expo.astype(LOW), value)
            total = out[:, 0:1]
            lse_ref[rows, pl.ds(h * NOPE, NOPE)] = jnp.broadcast_to(top + jnp.log(total), (size, NOPE))
            outs.append(out / total)
        mix_ref[rows, :] = jnp.where(low, pltpu.roll(outs[0], NOPE, 1), outs[1]).astype(LOW)


def attend(latents, weights, q_rows, bias, tables):
    count = latents.shape[0]
    groups, rows_all, columns = weights.shape
    steps = columns // (2 * LANE)
    blocks = 4

    def whole(shape):
        return pl.BlockSpec(shape, lambda i: (0, 0))

    wide = pl.BlockSpec((count, 2 * LANE), lambda i: (0, i))
    slim = pl.BlockSpec((count, LANE), lambda i: (0, i))
    table = whole((count, LANE))
    return pl.pallas_call(
        functools.partial(attend_kernel, blocks, q_rows),
        grid=(steps,),
        in_specs=[
            whole(latents.shape),
            pl.BlockSpec((groups, rows_all, 2 * LANE), lambda i: (0, 0, i)),
            whole((1, count)),
            table,
            table,
            table,
        ],
        out_specs=[wide, wide, slim, slim],
        out_shape=[
            jax.ShapeDtypeStruct((count, columns), LOW),
            jax.ShapeDtypeStruct((count, columns), LOW),
            jax.ShapeDtypeStruct((count, steps * LANE), LOW),
            jax.ShapeDtypeStruct((count, steps * LANE), F32),
        ],
        cost_estimate=pl.CostEstimate(flops=0, bytes_accessed=1 << 20, transcendentals=0),
        name="attend",
    )(latents, weights, bias, *tables)


def attend_back_kernel(
    blocks,
    q_ref,
    kv_ref,
    rope_ref,
    bias_ref,
    cos_ref,
    lift_ref,
    drop_ref,
    mix_ref,
    grad_ref,
    lse_ref,
    dq_ref,
    dkv_ref,
    drope_ref,
    dkey,
    dval,
    drope,
):
    size = q_ref.shape[0] // blocks
    low = lax.broadcasted_iota(jnp.int32, (1, LANE), 1) < NOPE
    causal = lax.broadcasted_iota(jnp.int32, (size, size), 1) <= lax.broadcasted_iota(
        jnp.int32, (size, size), 0
    )
    half = ROPE // 2

    @pl.when(pl.program_id(0) == 0)
    def _():
        drope[...] = jnp.zeros_like(drope)

    for h in range(2):
        cols = pl.ds(h * LANE, LANE)
        for i in range(blocks):
            rows = pl.ds(i * size, size)
            past = i * size
            live = pl.ds(0, past + size)
            query = q_ref[rows, cols]
            pair = kv_ref[live, cols]
            key = jnp.where(low, pair, rope_ref[live, :])
            both = grad_ref[rows, :]
            turned = pltpu.roll(both.astype(F32), NOPE, 1).astype(LOW) if h == 0 else both
            grad = jnp.where(low, jnp.zeros_like(both), turned)
            product = both.astype(F32) * mix_ref[rows, :].astype(F32)
            mine = low if h == 0 else ~low
            inner = jnp.sum(jnp.where(mine, product, 0.0), axis=1, keepdims=True)
            scores = dot_nt(query, key) * SCORE_SCALE + bias_ref[:, live]
            probs = jnp.exp(scores - lse_ref[rows, pl.ds(h * NOPE, 1)])
            edge = jnp.where(causal, probs[:, past:], 0.0)
            probs = edge if i == 0 else jnp.concatenate([probs[:, :past], edge], axis=1)
            score_cot = (probs * (dot_nt(grad, pair) - inner)).astype(LOW)
            dquery = dot(score_cot, key) * SCORE_SCALE
            dq_ref[rows, cols] = (
                dquery * cos_ref[rows, :]
                - pltpu.roll(dquery, half, 1) * lift_ref[rows, :]
                - pltpu.roll(dquery, LANE - half, 1) * drop_ref[rows, :]
            ).astype(LOW)
            dk = dot_tn(score_cot, query) * SCORE_SCALE
            dv = dot_tn(probs.astype(LOW), grad)
            if i > 0:
                dkey[pl.ds(0, past), :] += dk[:past]
                dval[pl.ds(0, past), :] += dv[:past]
            dkey[rows, :] = dk[past:]
            dval[rows, :] = dv[past:]
        dkv_ref[:, cols] = jnp.where(low, dkey[...], dval[...]).astype(LOW)
        drope[...] += dkey[...]
    drope_ref[...] = drope[...].astype(LOW)


def attend_back(query, pair, rope, bias, tables, mixed, grad, lse):
    count = query.shape[0]
    steps = query.shape[1] // (2 * LANE)
    blocks = 4

    def whole(shape):
        return pl.BlockSpec(shape, lambda i: (0, 0))

    wide = pl.BlockSpec((count, 2 * LANE), lambda i: (0, i))
    slim = pl.BlockSpec((count, LANE), lambda i: (0, i))
    table = whole((count, LANE))
    return pl.pallas_call(
        functools.partial(attend_back_kernel, blocks),
        grid=(steps,),
        in_specs=[wide, wide, table, whole((1, count)), table, table, table, slim, slim, slim],
        out_specs=[wide, wide, table],
        out_shape=[
            jax.ShapeDtypeStruct(query.shape, LOW),
            jax.ShapeDtypeStruct(query.shape, LOW),
            jax.ShapeDtypeStruct((count, LANE), LOW),
        ],
        scratch_shapes=[pltpu.VMEM((count, LANE), F32)] * 3,
        cost_estimate=pl.CostEstimate(flops=0, bytes_accessed=1 << 20, transcendentals=0),
        name="attend_back",
    )(query, pair, rope, bias, *tables, mixed, grad, lse)


LINE = 8
PLANE = 4


def special():
    return lax.axis_size("fsdp") == LINE and lax.axis_size("tp") == PLANE


def tie(*values):
    return lax.optimization_barrier(values)


def hop(values, pairs):
    moves = [(2 * a + core, 2 * b + core) for a, b in pairs for core in range(2)]
    return lax.ppermute(values, "fsdp", moves)


def swap_cores(values):
    return lax.ppermute(values, "fsdp", [(i, i ^ 1) for i in range(LINE)])


UP = [(0, 1), (1, 2), (2, 3)]
DOWN = [(1, 0), (2, 1), (3, 2)]


def line_index():
    return lax.axis_index("fsdp") // 2


def gather_one(values):
    return hop(values, UP), hop(values, DOWN)


def gather_two(above, below):
    return hop(above, UP[1:]) + hop(below, DOWN[:2])


def gather_three(far):
    return hop(far, [(1, 0), (2, 3)])


def assemble(own, above, below, far, last):
    z = line_index()
    whole = jnp.broadcast_to(own[None], (4,) + own.shape)
    put = lax.dynamic_update_index_in_dim
    whole = put(whole, far, (z + 2) % 4, 0)
    whole = put(whole, jnp.where(z == 0, last, above), (z + 3) % 4, 0)
    return put(whole, jnp.where(z == 3, last, below), (z + 1) % 4, 0)


def plus(left, right):
    return (left.astype(F32) + right.astype(F32)).astype(LOW)


def line_sum(part):
    lines = [[2 * z + core for z in range(4)] for core in range(2)]
    return lax.psum_scatter(part, "fsdp", scatter_dimension=0, axis_index_groups=lines, tiled=False)


def rowwise(values):
    return with_layout_constraint(values, Layout(major_to_minor=tuple(range(values.ndim))))


def by_core(own, other):
    first = lax.axis_index("fsdp") % 2 == 0
    return jnp.where(first, own, other), jnp.where(first, other, own)


def to_line(values):
    block = values.shape[-1] // LINE
    parts = [values[..., i * block : (i + 1) * block] for i in range(LINE)]
    return jnp.concatenate(by_core(jnp.concatenate(parts[0::2], axis=-1), jnp.concatenate(parts[1::2], axis=-1)), axis=-1)


def from_line(values):
    block = values.shape[-1] // LINE
    half = values.shape[-1] // 2
    even, odd = by_core(values[..., :half], values[..., half:])
    parts = [p[..., i * block : (i + 1) * block] for i in range(LINE // 2) for p in (even, odd)]
    return jnp.concatenate(parts, axis=-1)


def deal_plain(values, sources):
    group = lax.axis_index("fsdp")
    return lax.dynamic_index_in_dim(lax.all_gather(values, "fsdp"), jnp.take(sources, group), 0, keepdims=False)


MESH = pl.DeviceIdType.MESH


def square():
    me = lax.axis_index("tp")
    y, x = me // 2, me % 2
    beside, across = 2 * y + (1 - x), 2 * (1 - y) + x
    return me, beside, across, 3 - me


def greet(beside, across):
    barrier = pltpu.get_barrier_semaphore()
    for peer in (beside, across):
        pl.semaphore_signal(barrier, inc=1, device_id={"tp": peer}, device_id_type=MESH)
    pl.semaphore_wait(barrier, 2)


def send(source, target, sems, slot, peer):
    copy = pltpu.make_async_remote_copy(
        src_ref=source,
        dst_ref=target,
        send_sem=sems[0].at[slot],
        recv_sem=sems[1].at[slot],
        device_id={"tp": peer},
        device_id_type=MESH,
    )
    copy.start()
    return copy


def rows_of(position, size):
    return pl.ds(pl.multiple_of(position * size, size), size)


def reduce_square(parts, got, sems, prepare=lambda position: None, meanwhile=lambda: None):
    size = got[0].shape[1]
    me, beside, across, corner = square()
    peers = ((beside, across), (across, beside))
    prepare(corner)
    early = [
        send(parts[k].at[rows_of(corner, size), :], got[k].at[0], sems, 3 * k, first) for k, (first, _) in enumerate(peers)
    ]
    for k, (first, _) in enumerate(peers):
        prepare(first)
        early.append(send(parts[k].at[rows_of(first, size), :], got[k].at[1], sems, 3 * k + 1, first))
    for k, (_, second) in enumerate(peers):
        early[k].wait_recv()
        onward = rows_of(second, size)
        parts[k][onward, :] = (parts[k][onward, :].astype(F32) + got[k][0].astype(F32)).astype(LOW)
        early.append(send(parts[k].at[onward, :], got[k].at[2], sems, 3 * k + 2, second))
    prepare(me)
    meanwhile()
    for copy in early[2:]:
        copy.wait_recv()
    return early


def spread_square(full, columns, sems, base):
    me, beside, across, corner = square()
    size = full.shape[0] // PLANE
    own = rows_of(me, size)

    def piece(position, k):
        return full.at[rows_of(position, size), columns[k]]

    def pass_on(position, k, slot, peer):
        return send(piece(position, k), piece(position, k), sems, base + slot, peer)

    one = pass_on(me, 0, 0, across)
    two = pass_on(me, 1, 1, beside)
    three = pass_on(me, 0, 2, beside)
    four = pass_on(me, 1, 3, across)
    one.wait_recv()
    five = pass_on(across, 0, 4, beside)
    two.wait_recv()
    six = pass_on(beside, 1, 5, across)
    for copy in (three, four, five, six):
        copy.wait_recv()
    return [one, two, three, four, five, six]


def gather_kernel(cut, own_ref, full_ref, send_sems, recv_sems):
    me, beside, across, _ = square()
    size, width = own_ref.shape
    full_ref[rows_of(me, size), :] = own_ref[...]
    greet(beside, across)
    for copy in spread_square(full_ref, (pl.ds(0, cut), pl.ds(cut, width - cut)), (send_sems, recv_sems), 0):
        copy.wait_send()


def gather_tp(values, name, ident):
    if not special():
        return lax.all_gather(values, "tp", axis=0, tiled=True)
    rows, columns = values.shape
    cut = columns // LANE // 2 * LANE
    return pl.pallas_call(
        functools.partial(gather_kernel, cut),
        in_specs=[pl.BlockSpec(memory_space=pltpu.VMEM)],
        out_specs=pl.BlockSpec(memory_space=pltpu.VMEM),
        out_shape=jax.ShapeDtypeStruct((PLANE * rows, columns), values.dtype),
        scratch_shapes=[pltpu.SemaphoreType.DMA((6,)), pltpu.SemaphoreType.DMA((6,))],
        compiler_params=pltpu.CompilerParams(collective_id=ident, has_side_effects=True),
        cost_estimate=pl.CostEstimate(flops=0, bytes_accessed=1 << 20, transcendentals=0),
        name=name,
    )(values)


ROW_STEP = 32


def enter_kernel(
    mix_ref, w0_ref, w1_ref, x_ref, gain_ref, after_ref, low_ref, p0_ref, p1_ref, got0, got1, send_sems, recv_sems
):
    me, beside, across, _ = square()
    size = after_ref.shape[0]
    greet(beside, across)
    parts, gots = (p0_ref, p1_ref), (got0, got1)

    def prepare(position):
        here = rows_of(position, size)
        for part, weight in zip(parts, (w0_ref, w1_ref)):
            part[here, :] = dot_nt(mix_ref[here, :], weight[...]).astype(LOW)

    copies = reduce_square(parts, gots, (send_sems, recv_sems), prepare)

    def rows_step(step, carry):
        here = pl.ds(pl.multiple_of(step * ROW_STEP, ROW_STEP), ROW_STEP)
        mine = pl.ds(pl.multiple_of(me * size + step * ROW_STEP, ROW_STEP), ROW_STEP)
        total = jnp.concatenate(
            [
                part[mine, :].astype(F32) + got[1, here, :].astype(F32) + got[2, here, :].astype(F32)
                for part, got in zip(parts, gots)
            ],
            axis=1,
        )
        after = x_ref[here, :].astype(F32) + RESIDUAL_SCALE * total
        after_ref[here, :] = after
        factor = lax.rsqrt(jnp.mean(after * after, axis=-1, keepdims=True) + EPSILON)
        low_ref[here, :] = (after * factor * gain_ref[...]).astype(LOW)
        return carry

    lax.fori_loop(0, size // ROW_STEP, rows_step, 0)
    for copy in copies:
        copy.wait_send()


def leave_kernel(
    p0_ref, p1_ref, after_ref, cot_ref, gain_ref, grad_ref, dgain_ref, low_ref, got0, got1, send_sems, recv_sems
):
    me, beside, across, _ = square()
    size = after_ref.shape[0]
    greet(beside, across)
    parts, gots = (p0_ref, p1_ref), (got0, got1)
    copies = reduce_square(parts, gots, (send_sems, recv_sems))
    dgain_ref[...] = jnp.zeros_like(dgain_ref)

    def rows_step(step, carry):
        here = pl.ds(pl.multiple_of(step * ROW_STEP, ROW_STEP), ROW_STEP)
        mine = pl.ds(pl.multiple_of(me * size + step * ROW_STEP, ROW_STEP), ROW_STEP)
        grad = jnp.concatenate(
            [
                part[mine, :].astype(F32) + got[1, here, :].astype(F32) + got[2, here, :].astype(F32)
                for part, got in zip(parts, gots)
            ],
            axis=1,
        )
        after = after_ref[here, :]
        factor = lax.rsqrt(jnp.mean(after * after, axis=-1, keepdims=True) + EPSILON)
        weighted = grad * gain_ref[...]
        inner = jnp.mean(weighted * after, axis=-1, keepdims=True)
        dgain_ref[...] += jnp.sum(grad * after * factor, axis=0, keepdims=True)
        total = cot_ref[here, :].astype(F32) + factor * weighted - after * (factor * factor * factor) * inner
        grad_ref[here, :] = total
        low_ref[here, :] = (RESIDUAL_SCALE * total).astype(LOW)
        return carry

    lax.fori_loop(0, size // ROW_STEP, rows_step, 0)
    for copy in copies:
        copy.wait_send()


def square_scratch(size, half):
    return [
        pltpu.VMEM((3, size, half), LOW),
        pltpu.VMEM((3, size, half), LOW),
        pltpu.SemaphoreType.DMA((6,)),
        pltpu.SemaphoreType.DMA((6,)),
    ]


def enter_mlp(mixed, slabs, x_low, gain):
    rows, half = mixed.shape[0], x_low.shape[1] // 2
    if not special():
        piece = dot_nt(mixed, slabs[0]).astype(LOW)
        branch = lax.psum_scatter(piece, "tp", scatter_dimension=0, tiled=True).astype(F32)
        after = x_low.astype(F32) + RESIDUAL_SCALE * branch
        normed, _ = normalize(after, gain)
        return after, normed.astype(LOW)
    size = x_low.shape[0]
    vmem = pl.BlockSpec(memory_space=pltpu.VMEM)
    return pl.pallas_call(
        enter_kernel,
        in_specs=[vmem] * 5,
        out_specs=[vmem] * 2,
        out_shape=[jax.ShapeDtypeStruct((size, 2 * half), F32), jax.ShapeDtypeStruct((size, 2 * half), LOW)],
        scratch_shapes=[pltpu.VMEM((rows, half), LOW)] * 2 + square_scratch(size, half),
        compiler_params=pltpu.CompilerParams(collective_id=2, has_side_effects=True, vmem_limit_bytes=48 << 20),
        cost_estimate=pl.CostEstimate(flops=0, bytes_accessed=1 << 20, transcendentals=0),
        name="enter_mlp",
    )(mixed, *slabs, x_low, gain[None])


def leave_mlp(pieces, after, grad_out, gain):
    rows, half = pieces[0].shape[0], after.shape[1] // 2
    if not special():
        grad = lax.psum_scatter(pieces[0], "tp", scatter_dimension=0, tiled=True).astype(F32)
        factor = lax.rsqrt(jnp.mean(after * after, axis=-1, keepdims=True) + EPSILON)
        extra, dgain = norm_back(after, factor, gain, grad)
        total = grad_out + extra
        return total, dgain, (RESIDUAL_SCALE * total).astype(LOW)
    size = after.shape[0]
    vmem = pl.BlockSpec(memory_space=pltpu.VMEM)
    total, dgain, full = pl.pallas_call(
        leave_kernel,
        in_specs=[vmem] * 5,
        out_specs=[vmem] * 3,
        out_shape=[
            jax.ShapeDtypeStruct((size, 2 * half), F32),
            jax.ShapeDtypeStruct((1, 2 * half), F32),
            jax.ShapeDtypeStruct((size, 2 * half), LOW),
        ],
        scratch_shapes=square_scratch(size, half),
        compiler_params=pltpu.CompilerParams(collective_id=3, has_side_effects=True, vmem_limit_bytes=48 << 20),
        cost_estimate=pl.CostEstimate(flops=0, bytes_accessed=1 << 20, transcendentals=0),
        name="leave_mlp",
    )(*pieces, after, grad_out.astype(LOW), gain[None])
    return total, dgain[0], full


UNIT = 256
REST = 64
TOKEN_STEP = 512
FEATURE_STEP = 640


def units_kernel(unit, slabs, begun, x_ref, cot_ref, *refs):
    weights, rest = refs[:slabs], refs[slabs + begun :]
    act_ref, grads = rest[0], rest[1:]
    half = weights[0].shape[0]
    wide = 2 * unit

    def tokens(step, carry):
        rows = pl.ds(pl.multiple_of(step * TOKEN_STEP, TOKEN_STEP), TOKEN_STEP)
        both = 0.0
        grad = 0.0
        for k in range(slabs):
            part = pl.ds(k * half, half)
            both = both + dot(x_ref[rows, part], weights[k][:, 0:wide])
            grad = grad + dot(cot_ref[rows, part], weights[k][:, wide : wide + max(unit, LANE)])
        gate = both[:, : max(unit, LANE)]
        up = both[:, unit:] if unit >= LANE else pltpu.roll(both, unit, 1)
        sigma = 1.0 / (1.0 + jnp.exp(-gate))
        silu = gate * sigma
        activated = silu * up
        gate_cot = grad * up * (sigma * (1.0 + gate * (1.0 - sigma)))
        up_cot = grad * silu
        if unit >= LANE:
            act_ref[rows, 0:unit] = gate_cot.astype(LOW)
            act_ref[rows, unit:wide] = up_cot.astype(LOW)
            act_ref[rows, wide : wide + unit] = activated.astype(LOW)
        else:
            low = lax.broadcasted_iota(jnp.int32, (1, LANE), 1) < unit
            act_ref[rows, 0:LANE] = jnp.where(low, gate_cot, pltpu.roll(up_cot, unit, 1)).astype(LOW)
            act_ref[rows, LANE : 2 * LANE] = jnp.where(low, activated, 0.0).astype(LOW)
        return carry

    lax.fori_loop(0, x_ref.shape[0] // TOKEN_STEP, tokens, 0)
    columns = act_ref.shape[1]
    for k in range(slabs):

        def features(step, carry):
            rows = pl.ds(pl.multiple_of(step * FEATURE_STEP, FEATURE_STEP), FEATURE_STEP)
            part = pl.ds(pl.multiple_of(k * half + step * FEATURE_STEP, LANE), FEATURE_STEP)
            grads[k][rows, 0:wide] = dot_tn(x_ref[:, part], act_ref[:, 0:wide]).astype(LOW)
            grads[k][rows, wide:columns] = dot_tn(cot_ref[:, part], act_ref[:, wide:columns]).astype(LOW)
            return carry

        lax.fori_loop(0, half // FEATURE_STEP, features, 0)


def units_call(values, cot, slabs, unit, first, count, begun):
    rows, width = values.shape
    half, total = slabs[0].shape
    columns = 3 * unit if unit >= LANE else 2 * LANE
    whole = pl.BlockSpec((rows, width), lambda j: (0, 0), pipeline_mode=pl.Buffered(1))
    block = pl.BlockSpec((half, columns), lambda j: (0, j + first))
    shapes = [(rows, total)] + [(half, total)] * len(slabs)
    lead = 2 + len(slabs)
    return pl.pallas_call(
        functools.partial(units_kernel, unit, len(slabs), len(begun)),
        grid=(count,),
        in_specs=[whole, whole] + [block] * len(slabs) + [pl.BlockSpec(memory_space=pl.ANY)] * len(begun),
        out_specs=[pl.BlockSpec((rows, columns), lambda j: (0, j + first))] + [block] * len(slabs),
        out_shape=[jax.ShapeDtypeStruct(shape, LOW) for shape in shapes],
        input_output_aliases={lead + i: i for i in range(len(begun))},
        compiler_params=pltpu.CompilerParams(vmem_limit_bytes=60 << 20),
        cost_estimate=pl.CostEstimate(flops=0, bytes_accessed=1 << 20, transcendentals=0),
        name="units",
    )(values, cot, *slabs, *begun)


def units_tiles(values, cot, slabs):
    total = slabs[0].shape[1]
    full = total // (3 * UNIT)
    results = units_call(values, cot, slabs, UNIT, 0, full, [])
    if total % (3 * UNIT):
        results = units_call(values, cot, slabs, REST, full * 3, 1, results)
    return results[0], results[1:]


def close_kernel(counts, begun, *refs):
    acts, weights = refs[: len(counts)], refs[len(counts) : 2 * len(counts)]
    back_ref, branch_ref = refs[2 * len(counts) + begun :]

    def tokens(step, carry):
        rows = pl.ds(pl.multiple_of(step * TOKEN_STEP, TOKEN_STEP), TOKEN_STEP)
        back = 0.0
        branch = 0.0
        for (full, rest), act, weight in zip(counts, acts, weights):
            for j in range(full):
                a = 3 * UNIT * j
                b = a + 2 * UNIT
                back = back + dot_nt(act[rows, a:b], weight[:, a:b])
                branch = branch + dot_nt(act[rows, b : b + UNIT], weight[:, b : b + UNIT])
            if rest:
                a = 3 * UNIT * full
                b = a + LANE
                back = back + dot_nt(act[rows, a:b], weight[:, a:b])
                branch = branch + dot_nt(act[rows, b : b + LANE], weight[:, b : b + LANE])
        back_ref[rows, :] = back.astype(LOW)
        branch_ref[rows, :] = branch.astype(LOW)
        return carry

    lax.fori_loop(0, back_ref.shape[0] // TOKEN_STEP, tokens, 0)


def close_tiles(acts, slabs, first, begun):
    rows = acts[0].shape[0]
    half = slabs[0].shape[0]
    counts = [(act.shape[1] // (3 * UNIT), act.shape[1] % (3 * UNIT)) for act in acts]
    total = sum(act.shape[1] for act in acts)
    return pl.pallas_call(
        functools.partial(close_kernel, counts, len(begun)),
        grid=(half // UNIT,),
        in_specs=[pl.BlockSpec(act.shape, lambda j: (0, 0), pipeline_mode=pl.Buffered(1)) for act in acts]
        + [pl.BlockSpec((UNIT, slab.shape[1]), lambda j: (j, 0)) for slab in slabs]
        + [pl.BlockSpec(memory_space=pl.ANY)] * len(begun),
        out_specs=[
            pl.BlockSpec((rows, UNIT), lambda j: (0, j)),
            pl.BlockSpec((rows, UNIT), lambda j: (0, j + first)),
        ],
        out_shape=[jax.ShapeDtypeStruct((rows, half), LOW), jax.ShapeDtypeStruct((rows, 2 * half), LOW)],
        input_output_aliases={2 * len(acts): 1} if begun else {},
        compiler_params=pltpu.CompilerParams(vmem_limit_bytes=60 << 20),
        cost_estimate=pl.CostEstimate(flops=0, bytes_accessed=1 << 20, transcendentals=0),
        name="close",
    )(*acts, *slabs, *begun)


class Wires:
    def __init__(self, send_sems, recv_sems):
        self.send_sems, self.recv_sems = send_sems, recv_sems

    def _copy(self, source, target, number, peer):
        return pltpu.make_async_remote_copy(
            src_ref=source,
            dst_ref=target,
            send_sem=self.send_sems.at[number],
            recv_sem=self.recv_sems.at[number],
            device_id=peer,
            device_id_type=MESH,
        )

    def start(self, source, target, number, peer):
        self._copy(source, target, number, peer).start()

    def sent(self, source, number, peer):
        self._copy(source, source, number, peer).wait_send()

    def arrived(self, target, number, peer):
        self._copy(target, target, number, peer).wait_recv()


def line_peers():
    group = lax.axis_index("fsdp")
    z, core = group // 2, group % 2
    return z, core, {"fsdp": group + 1 - 2 * core}


def line_peer(z, core):
    return {"fsdp": 2 * z + core}


def greet_all(peers):
    barrier = pltpu.get_barrier_semaphore()
    for peer in peers:
        pl.semaphore_signal(barrier, inc=1, device_id=peer, device_id_type=MESH)
    pl.semaphore_wait(barrier, len(peers))


def gather_square(piece, sources, wires, base):
    me, beside, across, corner = square()
    beside_peer, across_peer = {"tp": beside}, {"tp": across}
    for number, (k, peer) in enumerate(((0, across_peer), (1, beside_peer), (0, beside_peer), (1, across_peer))):
        wires.start(sources[k], piece(me, k), base + number, peer)

    def relay():
        wires.arrived(piece(across, 0), base, across_peer)
        wires.start(piece(across, 0), piece(across, 0), base + 4, beside_peer)
        wires.arrived(piece(beside, 1), base + 1, beside_peer)
        wires.start(piece(beside, 1), piece(beside, 1), base + 5, across_peer)

    def neighbours():
        wires.arrived(piece(beside, 0), base + 2, beside_peer)
        wires.arrived(piece(across, 1), base + 3, across_peer)

    def finish():
        wires.arrived(piece(corner, 0), base + 4, beside_peer)
        wires.arrived(piece(corner, 1), base + 5, across_peer)

    def leave():
        for number, k in enumerate((0, 1, 0, 1, 0, 1)):
            wires.sent(piece(me, k), base + number, beside_peer)

    return relay, neighbours, finish, leave


def store_line(ref, rows, values, core):
    half = values.shape[1] // 2
    block = half // 4
    for i in range(4):
        even = values[:, 2 * i * block : (2 * i + 1) * block]
        odd = values[:, (2 * i + 1) * block : (2 * i + 2) * block]
        ref[rows, i * block : (i + 1) * block] = jnp.where(core == 0, even, odd).astype(ref.dtype)
        ref[rows, half + i * block : half + (i + 1) * block] = jnp.where(core == 0, odd, even).astype(ref.dtype)


def bring_kernel(
    sources_ref,
    length_ref,
    down_ref,
    qk_ref,
    out_ref,
    cot_ref,
    input_ref,
    spot_ref,
    cos_ref,
    lift_ref,
    drop_ref,
    part_ref,
    downs_ref,
    qks_ref,
    outs_ref,
    own_cot_ref,
    normed_ref,
    latents_ref,
    gains_ref,
    all_ref,
    cots_ref,
    above_ref,
    below_ref,
    x_ref,
    scaled,
    blocks,
    got,
    theirs,
    stage,
    send_sems,
    recv_sems,
    local_sems,
):
    z, core, sibling = line_peers()
    me, beside, across, corner = square()
    wires = Wires(send_sems, recv_sems)
    size, width = cot_ref.shape
    half = width // 2
    turns = [line_peer((z + r) % 4, core) for r in (1, 2, 3)]
    greet_all([sibling, {"tp": beside}, {"tp": across}] + turns)
    up, down = line_peer((z + 1) % 4, core), line_peer((z + 3) % 4, core)
    edge = (z == 0) | (z == 3)
    inner = (z == 1) | (z == 2)

    def when(condition, action):
        @pl.when(condition)
        def _():
            action()

    heads = ((qk_ref, lambda at, side: qks_ref.at[at, (core + side) % 2], 0), (out_ref, lambda at, side: outs_ref.at[side, at], 1))

    def head_hop(at, number, peer, own=False):
        for ref, slot, k in heads:
            wires.start(ref if own else slot(at, 0), slot(at, 0), number + k, peer)

    def head_in(at, number, peer):
        for _, slot, k in heads:
            wires.arrived(slot(at, 0), number + k, peer)

    def head_over(at, number):
        for ref, slot, k in heads:
            target = qks_ref.at[at, core] if k == 0 else outs_ref.at[1, at]
            wires.start(slot(at, 0), target, number + k, sibling)

    def head_back(at, number):
        for _, slot, k in heads:
            wires.arrived(slot(at, 1), number + k, sibling)

    blocks[pl.ds(z, 1)] = cot_ref[...][None]
    downs_ref[0, pl.ds(z, 1), pl.ds(me, 1)] = down_ref[...][None, None]
    keeps = [pltpu.make_async_copy(ref, slot(z, 0), local_sems.at[k]) for ref, slot, k in heads]
    for keep in keeps:
        keep.start()

    for r in (1, 2, 3):
        wires.start(down_ref, downs_ref.at[0, z, me], r, turns[r - 1])
    wires.start(down_ref, downs_ref.at[1, z, me], 4, sibling)
    when(z < 2, lambda: wires.start(cot_ref, blocks.at[z], 0, up))
    when(z > 1, lambda: wires.start(cot_ref, blocks.at[z], 5, down))
    when((z == 0) | (z == 2), lambda: head_hop(z, 6, up, True))
    when((z == 1) | (z == 3), lambda: head_hop(z, 8, down, True))
    when((z == 0) | (z == 2), lambda: wires.start(part_ref, above_ref, 48, up))
    when((z == 1) | (z == 3), lambda: wires.start(part_ref, below_ref, 49, down))
    for keep in keeps:
        keep.wait()
    head_over(z, 10)

    for r in (1, 2, 3):
        wires.arrived(downs_ref.at[0, (z + 4 - r) % 4, me], r, turns[r - 1])
    relay, neighbours, finish, leave_downs = gather_square(
        lambda position, k: downs_ref.at[0, pl.ds(2 * k, 2), position],
        [downs_ref.at[0, pl.ds(2 * k, 2), me] for k in range(2)],
        wires,
        12,
    )
    for r in (1, 2, 3):
        here = (z + r) % 4
        wires.start(downs_ref.at[0, here, me], downs_ref.at[1, here, me], 17 + r, sibling)

    @pl.when(inner)
    def _():
        wires.arrived(blocks.at[z - 1], 0, down)
        wires.arrived(blocks.at[z + 1], 5, up)

    @pl.when(z == 1)
    def _():
        wires.start(blocks.at[0], blocks.at[0], 21, up)
        head_hop(z, 6, up, True)
        head_in(0, 6, down)
        head_hop(0, 22, up)
        wires.start(part_ref, above_ref, 48, up)
        head_over(0, 24)

    @pl.when(z == 2)
    def _():
        wires.start(blocks.at[3], blocks.at[3], 21, down)
        head_hop(z, 8, down, True)
        head_in(3, 8, up)
        head_hop(3, 22, down)
        wires.start(part_ref, below_ref, 49, down)
        head_over(3, 24)

    relay()
    neighbours()
    wires.start(downs_ref.at[0, :, beside], downs_ref.at[1, :, beside], 26, sibling)
    wires.start(downs_ref.at[0, :, across], downs_ref.at[1, :, across], 27, sibling)
    finish()
    wires.start(downs_ref.at[0, :, corner], downs_ref.at[1, :, corner], 28, sibling)
    wires.arrived(downs_ref.at[1, z, me], 4, sibling)
    for r in (1, 2, 3):
        wires.arrived(downs_ref.at[1, (z + r) % 4, me], 17 + r, sibling)
    for number, position in ((26, beside), (27, across), (28, corner)):
        wires.arrived(downs_ref.at[1, :, position], number, sibling)

    kv = all_ref.shape[1] - LANE
    used = kv + ROPE
    tail = jnp.concatenate([downs_ref[k, :, :, :, kv:].reshape(half, LANE) for k in range(2)], axis=0).astype(F32).T
    gains_ref[...] = tail[ROPE : ROPE + 8]
    lead = tail[ROPE : ROPE + 8].astype(LOW)
    small = 0.0
    chunk = 4 * LANE
    for a in range(0, width, chunk):
        row = lax.broadcasted_iota(jnp.int32, (chunk, spot_ref.shape[1]), 0) + a
        here = jnp.where(row == spot_ref[...], 1.0, 0.0).astype(LOW)
        small = small + dot(lead[:, a : a + chunk], here)
    small = small[2:3]
    gain = tail[ROPE : ROPE + 1]

    def normed_step(step, carry):
        here = pl.ds(pl.multiple_of(step * ROW_STEP, ROW_STEP), ROW_STEP)
        store_line(x_ref, here, input_ref[here, :].astype(F32), core)
        value = x_ref[here, :].astype(F32)
        factor = lax.rsqrt(jnp.mean(value * value, axis=-1, keepdims=True) + EPSILON)
        normed_ref[here, :] = (value * factor * gain).astype(LOW)
        return carry

    lax.fori_loop(0, size // ROW_STEP, normed_step, 0)
    for a in range(0, kv + LANE, 3 * LANE):
        b = min(a + 3 * LANE, kv + LANE)
        total = 0.0
        for k in range(2):
            total = total + dot(normed_ref[:, k * half : (k + 1) * half], downs_ref[k, :, :, :, a:b].reshape(half, b - a))
        latents_ref[:, a:b] = total
    low = lax.broadcasted_iota(jnp.int32, (1, LANE), 1) < ROPE
    cuts = ((0, kv - KR), (kv - KR, kv))

    def latent_step(step, carry):
        here = pl.ds(pl.multiple_of(step * ROW_STEP, ROW_STEP), ROW_STEP)
        mine = pl.ds(pl.multiple_of(me * size + step * ROW_STEP, ROW_STEP), ROW_STEP)
        for a, b in cuts:
            value = latents_ref[here, a:b]
            factor = lax.rsqrt(jnp.mean(value * value, axis=-1, keepdims=True) + EPSILON)
            all_ref[mine, a:b] = (value * factor * small[:, a:b]).astype(LOW)
        rope = pltpu.roll(jnp.where(low, latents_ref[here, kv:], 0.0), NOPE, 1)
        rope = (
            rope * cos_ref[here, :]
            + pltpu.roll(rope, ROPE // 2, 1) * lift_ref[here, :]
            + pltpu.roll(rope, LANE - ROPE // 2, 1) * drop_ref[here, :]
        )
        all_ref[mine, kv:] = rope.astype(LOW)
        return carry

    lax.fori_loop(0, size // ROW_STEP, latent_step, 0)
    cut = (kv + LANE) // LANE // 2 * LANE
    columns = (pl.ds(0, cut), pl.ds(cut, kv + LANE - cut))
    relay, neighbours, finish, leave_latents = gather_square(
        lambda position, k: all_ref.at[rows_of(position, size), columns[k]],
        [all_ref.at[rows_of(me, size), columns[k]] for k in range(2)],
        wires,
        30,
    )

    when(z == 2, lambda: wires.arrived(blocks.at[0], 21, down))
    when(z == 1, lambda: wires.arrived(blocks.at[3], 21, up))
    end = jnp.where(z == 2, 6, 0)
    inner_want, inner_asked = sources_ref[end + core], sources_ref[end + 1 - core]
    want, asked = sources_ref[2 * z + core], sources_ref[2 * z + 1 - core]
    stage[0] = blocks[inner_asked // 2]
    wires.start(stage.at[0], theirs.at[0], 36, sibling)
    stage[1] = jnp.where(edge, cot_ref[...], blocks[asked // 2])
    wires.start(stage.at[1], theirs.at[1], 37, sibling)
    wires.arrived(theirs.at[0], 36, sibling)
    stage[2] = jnp.where(inner_want % 2 == core, blocks[inner_want // 2], theirs[0])
    when(z == 2, lambda: wires.start(stage.at[2], got, 38, up))
    when(z == 1, lambda: wires.start(stage.at[2], got, 38, down))
    relay()
    neighbours()
    finish()

    @pl.when(z == 1)
    def _():
        head_in(2, 8, up)
        head_hop(2, 40, down)
        head_over(2, 42)
        head_in(3, 22, up)
        head_hop(3, 44, down)
        head_over(3, 46)

    @pl.when(z == 2)
    def _():
        head_in(1, 6, down)
        head_hop(1, 40, up)
        head_over(1, 42)
        head_in(0, 22, down)
        head_hop(0, 44, up)
        head_over(0, 46)

    when(z == 0, lambda: wires.arrived(got, 38, up))
    when(z == 3, lambda: wires.arrived(got, 38, down))
    wires.arrived(theirs.at[1], 37, sibling)

    def rows_step(step, carry):
        here = pl.ds(pl.multiple_of(step * ROW_STEP, ROW_STEP), ROW_STEP)
        mine = jnp.where(edge, cot_ref[here, :], blocks[want // 2, here, :])
        local = jnp.where(want % 2 == core, mine, theirs[1, here, :])
        value = jnp.where(edge & (want // 2 != z), got[here, :], local).astype(F32)
        position = me * size + step * ROW_STEP + lax.broadcasted_iota(jnp.int32, (ROW_STEP, 1), 0)
        value = jnp.where(position < length_ref[0], value, 0.0)
        store_line(own_cot_ref, here, value, core)
        store_line(scaled, here, RESIDUAL_SCALE * value, core)
        return carry

    lax.fori_loop(0, size // ROW_STEP, rows_step, 0)

    keep_cot = pltpu.make_async_copy(scaled, cots_ref.at[rows_of(me, size), :], local_sems.at[2])
    keep_cot.start()
    halves = (pl.ds(0, half), pl.ds(half, half))
    relay, neighbours, finish, leave_cots = gather_square(
        lambda position, k: cots_ref.at[rows_of(position, size), halves[k]],
        [scaled.at[:, halves[k]] for k in range(2)],
        wires,
        50,
    )

    @pl.when(z == 0)
    def _():
        head_in(1, 8, up)
        head_over(1, 24)
        head_in(2, 40, up)
        head_over(2, 42)

    @pl.when(z == 3)
    def _():
        head_in(2, 6, down)
        head_over(2, 24)
        head_in(1, 40, down)
        head_over(1, 42)

    relay()

    @pl.when(z == 0)
    def _():
        head_in(3, 44, up)
        head_over(3, 46)

    @pl.when(z == 3)
    def _():
        head_in(0, 44, down)
        head_over(0, 46)


    head_back(z, 10)
    when(z == 1, lambda: [head_back(at, number) for at, number in ((0, 24), (2, 42), (3, 46))])
    when(z == 2, lambda: [head_back(at, number) for at, number in ((3, 24), (1, 42), (0, 46))])
    when(z == 0, lambda: [head_back(at, number) for at, number in ((1, 24), (2, 42), (3, 46))])
    when(z == 3, lambda: [head_back(at, number) for at, number in ((2, 24), (1, 42), (0, 46))])

    neighbours()
    finish()
    keep_cot.wait()
    when(z > 0, lambda: wires.arrived(above_ref, 48, down))
    when(z < 3, lambda: wires.arrived(below_ref, 49, up))

    leave_cots()
    when(z < 3, lambda: wires.sent(part_ref, 48, up))
    when(z > 0, lambda: wires.sent(part_ref, 49, down))
    for number in (1, 2, 3, 4, 18, 19, 20):
        wires.sent(down_ref, number, sibling)
    leave_downs()
    for number in (26, 27, 28):
        wires.sent(downs_ref.at[0, :, me], number, sibling)
    leave_latents()
    for number in (36, 37):
        wires.sent(stage.at[0], number, sibling)

    def head_sent(*numbers):
        for number in numbers:
            for ref, _, k in heads:
                wires.sent(ref, number + k, sibling)

    head_sent(10, 24, 42, 46)
    when(z < 2, lambda: wires.sent(cot_ref, 0, sibling))
    when(z > 1, lambda: wires.sent(cot_ref, 5, sibling))
    when(z < 3, lambda: head_sent(6))
    when(z > 0, lambda: head_sent(8))

    @pl.when(inner)
    def _():
        wires.sent(cot_ref, 21, sibling)
        wires.sent(cot_ref, 38, sibling)
        head_sent(22, 40, 44)


def bring(sources, length, down_pack, qk_pack, out_pack, cot, values, spot, tables, part):
    size, width = cot.shape
    columns = down_pack.shape[1]
    vmem, anywhere = pl.BlockSpec(memory_space=pltpu.VMEM), pl.BlockSpec(memory_space=pl.ANY)
    smem = pl.BlockSpec(memory_space=pltpu.SMEM)
    return pl.pallas_call(
        bring_kernel,
        in_specs=[smem, smem] + [vmem] * 9 + [anywhere],
        out_specs=[vmem, anywhere, anywhere] + [vmem] * 5 + [anywhere] * 3 + [vmem],
        out_shape=[
            jax.ShapeDtypeStruct((2, 4, PLANE) + down_pack.shape, LOW),
            jax.ShapeDtypeStruct((4, 2) + qk_pack.shape, LOW),
            jax.ShapeDtypeStruct((2, 4) + out_pack.shape, LOW),
            jax.ShapeDtypeStruct((size, width), LOW),
            jax.ShapeDtypeStruct((size, width), LOW),
            jax.ShapeDtypeStruct((size, columns), F32),
            jax.ShapeDtypeStruct((8, width), F32),
            jax.ShapeDtypeStruct((PLANE * size, columns), LOW),
            jax.ShapeDtypeStruct((PLANE * size, width), LOW),
            jax.ShapeDtypeStruct(part.shape, LOW),
            jax.ShapeDtypeStruct(part.shape, LOW),
            jax.ShapeDtypeStruct((size, width), LOW),
        ],
        scratch_shapes=[
            pltpu.VMEM((size, width), LOW),
            pltpu.VMEM((4, size, width), LOW),
            pltpu.VMEM((size, width), LOW),
            pltpu.VMEM((2, size, width), LOW),
            pltpu.VMEM((3, size, width), LOW),
            pltpu.SemaphoreType.DMA((56,)),
            pltpu.SemaphoreType.DMA((56,)),
            pltpu.SemaphoreType.DMA((3,)),
        ],
        compiler_params=pltpu.CompilerParams(collective_id=7, has_side_effects=True, vmem_limit_bytes=56 << 20),
        cost_estimate=pl.CostEstimate(flops=0, bytes_accessed=1 << 20, transcendentals=0),
        name="bring",
    )(sources, length, down_pack, qk_pack, out_pack, cot, values, spot, *tables, part)


def finish_kernel(
    sources_ref,
    qcot_ref,
    kvcot_ref,
    rope_ref,
    weight_ref,
    lat_ref,
    latents_ref,
    smalls_ref,
    cos_ref,
    lift_ref,
    drop_ref,
    x_ref,
    normed_ref,
    downs_ref,
    gain_ref,
    after_grad_ref,
    mlp_dgain_ref,
    own_ref,
    down_ref,
    head_ref,
    dealt_ref,
    input_ref,
    gains,
    query_ref,
    key_ref,
    part0,
    part1,
    got2,
    got3,
    cot_ref,
    gains_came,
    grad_block,
    keep,
    away,
    came,
    got0,
    got1,
    line,
    lines,
    head_came,
    head_part,
    head_lines,
    blocks,
    theirs,
    stage,
    send_sems,
    recv_sems,
    square_send,
    square_recv,
    local_sems,
):
    z, core, sibling = line_peers()
    me, beside, across, corner = square()
    wires = Wires(send_sems, recv_sems)
    turns = [line_peer((z + r) % 4, core) for r in (1, 2, 3)]
    greet_all([sibling, {"tp": beside}, {"tp": across}] + turns)
    up, down = line_peer((z + 1) % 4, core), line_peer((z + 3) % 4, core)
    edge = (z == 0) | (z == 3)
    half = normed_ref.shape[1] // 2
    used = cot_ref.shape[1]
    size = normed_ref.shape[0]
    groups, rows_all, columns = weight_ref.shape
    q_rows = query_ref.shape[2]
    qr = groups * q_rows
    kv = lat_ref.shape[1] - LANE
    slim = part0.shape[1]

    keep_own = pltpu.make_async_copy(own_ref, blocks.at[z], local_sems.at[0])
    keep_own.start()

    @pl.when(z < 2)
    def _():
        wires.start(own_ref, blocks.at[z], 0, up)

    @pl.when(z > 1)
    def _():
        wires.start(own_ref, blocks.at[z], 12, down)

    w_query = weight_ref[:, :q_rows].reshape(qr, columns)
    w_pair = weight_ref[:, q_rows:].reshape(groups * (rows_all - q_rows), columns)

    def prepare(position):
        here = rows_of(position, size)
        back = dot_nt(qcot_ref[here, :], w_query)
        part0[here, :] = back[:, :slim].astype(LOW)
        part1[here, 0 : qr - slim] = back[:, slim:].astype(LOW)
        part1[here, qr - slim : kv - slim] = dot_nt(kvcot_ref[here, :], w_pair).astype(LOW)
        part1[here, kv - slim :] = rope_ref[here, :]

    def head_gradients():
        for i in range(4):
            for c in range(2):
                g = 2 * i + c
                if g % 4 == 0:
                    grads = dot_tn(lat_ref[:, g * q_rows : (g + 4) * q_rows], qcot_ref[...]).astype(LOW)
                query_ref[i, c] = grads[(g % 4) * q_rows : (g % 4 + 1) * q_rows]
        pair_rows = rows_all - q_rows
        grads = dot_tn(lat_ref[:, qr:kv], kvcot_ref[...]).astype(LOW)
        for i in range(4):
            for c in range(2):
                g = 2 * i + c
                key_ref[i, c] = grads[g * pair_rows : (g + 1) * pair_rows]
        wires.start(query_ref.at[:, 1 - core], head_came.at[:, pl.ds(0, q_rows)], 1, sibling)
        wires.start(key_ref.at[:, 1 - core], head_came.at[:, pl.ds(q_rows, pair_rows)], 2, sibling)

    copies = reduce_square(
        (part0, part1),
        (got2, got3),
        (square_send.at[pl.ds(6, 6)], square_recv.at[pl.ds(6, 6)]),
        prepare,
        head_gradients,
    )
    gains[...] = jnp.zeros_like(gains)
    keep_own.wait()

    @pl.when((z == 1) | (z == 2))
    def _():
        wires.arrived(blocks.at[z - 1], 0, down)
        wires.arrived(blocks.at[z + 1], 12, up)

    @pl.when(z == 1)
    def _():
        wires.start(blocks.at[0], blocks.at[0], 19, up)

    @pl.when(z == 2)
    def _():
        wires.start(blocks.at[3], blocks.at[3], 19, down)

    end = jnp.where(z == 2, 6, 0)
    inner_want, inner_asked = sources_ref[end + core], sources_ref[end + 1 - core]
    want, asked = sources_ref[2 * z + core], sources_ref[2 * z + 1 - core]

    def last_hop():
        @pl.when(z == 2)
        def _():
            wires.arrived(blocks.at[0], 19, down)

        @pl.when(z == 1)
        def _():
            wires.arrived(blocks.at[3], 19, up)

        stage[0] = blocks[inner_asked // 2]
        wires.start(stage.at[0], theirs.at[0], 10, sibling)
        stage[1] = jnp.where(edge, blocks[z], blocks[asked // 2])
        wires.start(stage.at[1], theirs.at[1], 11, sibling)
        wires.arrived(theirs.at[0], 10, sibling)
        wires.sent(stage.at[0], 10, sibling)
        stage[0] = jnp.where(inner_want % 2 == core, blocks[inner_want // 2], theirs[0])

        @pl.when(z == 2)
        def _():
            wires.start(stage.at[0], dealt_ref, 20, up)

        @pl.when(z == 1)
        def _():
            wires.start(stage.at[0], dealt_ref, 20, down)

    def latent_step(step, carry):
        here = pl.ds(pl.multiple_of(step * ROW_STEP, ROW_STEP), ROW_STEP)
        mine = pl.ds(pl.multiple_of(me * size + step * ROW_STEP, ROW_STEP), ROW_STEP)
        total = jnp.concatenate(
            [
                part[mine, :].astype(F32) + come[1, here, :].astype(F32) + come[2, here, :].astype(F32)
                for part, come in ((part0, got2), (part1, got3))
            ],
            axis=1,
        )
        for a, b in ((0, qr), (qr, kv)):
            grad, value = total[:, a:b], latents_ref[here, a:b]
            factor = lax.rsqrt(jnp.mean(value * value, axis=-1, keepdims=True) + EPSILON)
            weighted = grad * smalls_ref[:, a:b]
            inside = jnp.mean(weighted * value, axis=-1, keepdims=True)
            gains[2:3, a:b] += jnp.sum(grad * value * factor, axis=0, keepdims=True)
            cot_ref[here, a:b] = (factor * weighted - value * (factor * factor * factor) * inside).astype(LOW)
        rope = total[:, kv:]
        rope = (
            rope * cos_ref[here, :]
            - pltpu.roll(rope, ROPE // 2, 1) * lift_ref[here, :]
            - pltpu.roll(rope, LANE - ROPE // 2, 1) * drop_ref[here, :]
        )
        cot_ref[here, kv:] = pltpu.roll(rope, NOPE, 1)[:, : used - kv].astype(LOW)
        return carry

    lax.fori_loop(0, size // ROW_STEP, latent_step, 0)
    rows = keep.shape[0] // 16
    block = half // 4

    def gradients(k, target):
        for pair in range(2):
            a = k * half + pair * 2 * block
            grads = dot_tn(normed_ref[:, a : a + 2 * block], cot_ref[...]).astype(LOW)
            for i in range(2):
                for t in range(PLANE):
                    row = (t * 4 + pair * 2 + i) * rows
                    target[row : row + rows, :] = grads[i * block + t * rows : i * block + (t + 1) * rows]

    gradients(1, away)
    wires.start(away, came, 3, sibling)
    gradients(0, keep)

    wires.arrived(head_came.at[:, pl.ds(0, q_rows)], 1, sibling)
    wires.arrived(head_came.at[:, pl.ds(q_rows, key_ref.shape[2])], 2, sibling)
    for i in range(4):
        for ref, a in ((query_ref, 0), (key_ref, q_rows)):
            b = a + ref.shape[2]
            head_part[i, a:b] = (ref[i, core].astype(F32) + head_came[i, a:b].astype(F32)).astype(LOW)
    for r in (1, 2, 3):
        wires.start(head_part.at[(z + r) % 4], head_lines.at[r - 1], 3 + r, turns[r - 1])
    wires.arrived(came, 3, sibling)

    def add_step(step, carry):
        here = pl.ds(pl.multiple_of(step * rows, 16), rows)
        keep[here, :] = (keep[here, :].astype(F32) + came[here, :].astype(F32)).astype(LOW)
        return carry

    lax.fori_loop(0, 16, add_step, 0)
    cut = got0.shape[2]
    parts = (keep.at[:, pl.ds(0, cut)], keep.at[:, pl.ds(cut, used - cut)])
    input_rows = grad_block.shape[0]

    def input_gradient():
        last_hop()

        def input_step(step, carry):
            here = pl.ds(pl.multiple_of(step * input_rows, input_rows), input_rows)
            bring_block = pltpu.make_async_copy(after_grad_ref.at[here, :], grad_block, local_sems.at[3])
            bring_block.start()
            cot = cot_ref[here, :]
            grad = jnp.concatenate([dot_nt(cot, downs_ref[k, :, :used]) for k in range(2)], axis=1)
            value = x_ref[here, :].astype(F32)
            factor = lax.rsqrt(jnp.mean(value * value, axis=-1, keepdims=True) + EPSILON)
            weighted = grad * gain_ref[...]
            inside = jnp.mean(weighted * value, axis=-1, keepdims=True)
            gains[0:1, :] += jnp.sum(grad * value * factor, axis=0, keepdims=True)
            total = factor * weighted - value * (factor * factor * factor) * inside
            bring_block.wait()
            total = total + grad_block[...]
            first, second = total[:, :half], total[:, half:]
            evens, odds = jnp.where(core == 0, first, second), jnp.where(core == 0, second, first)
            for i in range(4):
                piece = slice(i * block, (i + 1) * block)
                input_ref[here, 2 * i * block : (2 * i + 1) * block] = evens[:, piece].astype(LOW)
                input_ref[here, (2 * i + 1) * block : (2 * i + 2) * block] = odds[:, piece].astype(LOW)
            return carry

        lax.fori_loop(0, size // input_rows, input_step, 0)
        gains[1:2, :] = mlp_dgain_ref[...]
        for row in range(2):
            first, second = gains[row : row + 1, :half], gains[row : row + 1, half:]
            gains[row : row + 1, :half] = jnp.where(core == 0, first, second)
            gains[row : row + 1, half:] = jnp.where(core == 0, second, first)
        wires.start(gains, gains_came.at[0], 13, sibling)

    copies += reduce_square(
        parts,
        (got0, got1),
        (square_send.at[pl.ds(0, 6)], square_recv.at[pl.ds(0, 6)]),
        lambda position: None,
        input_gradient,
    )
    for k, (a, b) in enumerate(((0, cut), (cut, used))):
        got_k = (got0, got1)[k]
        total = keep[rows_of(me, 4 * rows), a:b].astype(F32) + got_k[1].astype(F32) + got_k[2].astype(F32)
        line[:, a:b] = total.astype(LOW)
    for r in (1, 2, 3):
        wires.start(line.at[rows_of((z + r) % 4, rows), :], lines.at[r - 1], 6 + r, turns[r - 1])

    for number, (slot, peer) in enumerate(((0, sibling), (1, {"tp": beside}), (2, {"tp": across}))):
        wires.arrived(gains_came.at[slot], 13 + number, peer)
        wires.sent(gains, 13 + number, peer)
        gains[...] += gains_came[slot]
        if number < 2:
            wires.start(gains, gains_came.at[slot + 1], 14 + number, ({"tp": beside}, {"tp": across})[number])
    for r in (1, 2, 3):
        wires.start(gains, gains_came.at[2 + r], 15 + r, turns[r - 1])
    for r in (1, 2, 3):
        wires.arrived(head_lines.at[r - 1], 3 + r, turns[r - 1])
    head_ref[...] = head_part[z].astype(F32) + (
        head_lines[0].astype(F32) + head_lines[1].astype(F32) + head_lines[2].astype(F32)
    )
    for r in (1, 2, 3):
        wires.arrived(lines.at[r - 1], 6 + r, turns[r - 1])
    down_ref[...] = line[rows_of(z, rows), :].astype(F32) + (
        lines[0].astype(F32) + lines[1].astype(F32) + lines[2].astype(F32)
    )
    for r in (1, 2, 3):
        wires.arrived(gains_came.at[2 + r], 15 + r, turns[r - 1])
    for r in (1, 2, 3):
        wires.sent(gains, 15 + r, turns[r - 1])
    gains[...] += gains_came[3] + (gains_came[4] + gains_came[5])
    wires.arrived(theirs.at[1], 11, sibling)

    @pl.when(z == 3)
    def _():
        wires.arrived(dealt_ref, 20, down)

    @pl.when(z == 0)
    def _():
        wires.arrived(dealt_ref, 20, up)

    mine = jnp.where(edge, blocks[z], blocks[want // 2])
    local = jnp.where(want % 2 == core, mine, theirs[1])
    dealt_ref[...] = jnp.where(edge & (want // 2 != z), dealt_ref[...], local)
    for copy in copies:
        copy.wait_send()
    wires.sent(query_ref.at[:, 0], 1, sibling)
    wires.sent(key_ref.at[:, 0], 2, sibling)
    wires.sent(away, 3, sibling)
    for r in (1, 2, 3):
        wires.sent(head_part.at[0], 3 + r, sibling)
        wires.sent(line.at[pl.ds(0, rows), :], 6 + r, sibling)
    wires.sent(stage.at[1], 11, sibling)

    @pl.when(z < 2)
    def _():
        wires.sent(own_ref, 0, sibling)

    @pl.when(z > 1)
    def _():
        wires.sent(own_ref, 12, sibling)

    @pl.when((z == 1) | (z == 2))
    def _():
        wires.sent(stage.at[0], 19, sibling)
        wires.sent(stage.at[0], 20, sibling)


def finish_all(sources, cots, rope, weights, q_rows, lat, latents, smalls, tables, values, normed, downs, gain, grad, dgain, own):
    size, width = normed.shape
    used = lat.shape[1] - LANE + ROPE
    rows = width // (LINE * PLANE)
    groups, head_rows, columns = weights.shape
    slim = lat.shape[1] // LANE // 2 * LANE + LANE
    cut = used // LANE // 2 * LANE
    vmem, smem = pl.BlockSpec(memory_space=pltpu.VMEM), pl.BlockSpec(memory_space=pltpu.SMEM)
    anywhere = pl.BlockSpec(memory_space=pl.ANY)
    mine, other = (4, 2, q_rows, columns), (4, 2, head_rows - q_rows, columns)
    return pl.pallas_call(
        finish_kernel,
        in_specs=[smem] + [vmem] * 14 + [anywhere, vmem, anywhere],
        out_specs=[vmem] * 5,
        out_shape=[
            jax.ShapeDtypeStruct((rows, used), F32),
            jax.ShapeDtypeStruct((head_rows, columns), F32),
            jax.ShapeDtypeStruct((size, width), LOW),
            jax.ShapeDtypeStruct((size, width), LOW),
            jax.ShapeDtypeStruct((8, width), F32),
        ],
        scratch_shapes=[
            pltpu.VMEM(mine, LOW),
            pltpu.VMEM(other, LOW),
            pltpu.VMEM((lat.shape[0], slim), LOW),
            pltpu.VMEM((lat.shape[0], lat.shape[1] - slim), LOW),
            pltpu.VMEM((3, size, slim), LOW),
            pltpu.VMEM((3, size, lat.shape[1] - slim), LOW),
            pltpu.VMEM((size, used), LOW),
            pltpu.VMEM((6, 8, width), F32),
            pltpu.VMEM((256, width), F32),
        ]
        + [pltpu.VMEM((16 * rows, used), LOW)] * 3
        + [
            pltpu.VMEM((3, 4 * rows, cut), LOW),
            pltpu.VMEM((3, 4 * rows, used - cut), LOW),
            pltpu.VMEM((4 * rows, used), LOW),
            pltpu.VMEM((3, rows, used), LOW),
            pltpu.VMEM((4, head_rows, columns), LOW),
            pltpu.VMEM((4, head_rows, columns), LOW),
            pltpu.VMEM((3, head_rows, columns), LOW),
            pltpu.VMEM((4, size, width), LOW),
            pltpu.VMEM((2, size, width), LOW),
            pltpu.VMEM((2, size, width), LOW),
            pltpu.SemaphoreType.DMA((21,)),
            pltpu.SemaphoreType.DMA((21,)),
            pltpu.SemaphoreType.DMA((12,)),
            pltpu.SemaphoreType.DMA((12,)),
            pltpu.SemaphoreType.DMA((4,)),
        ],
        compiler_params=pltpu.CompilerParams(collective_id=8, has_side_effects=True, vmem_limit_bytes=67 * 10**6),
        cost_estimate=pl.CostEstimate(flops=0, bytes_accessed=240 << 20, transcendentals=0),
        name="finish",
    )(sources, *cots, rope, weights, lat, latents, smalls, *tables, values, normed, downs, gain, grad, dgain, own)


def per_device(
    block_input,
    seq_lengths,
    dealt_order,
    out_cotangent,
    attn_gain,
    query_down,
    query_gain,
    latent_down,
    latent_gain,
    query_up,
    latent_up,
    output_matrix,
    mlp_gain,
    gate_weight,
    up_weight,
    down_matrix,
):
    line = special()
    tp_count = lax.axis_size("tp")
    fsdp_count = lax.axis_size("fsdp")
    group = lax.axis_index("fsdp")
    column = lax.axis_index("tp")
    _, local_len, width = block_input.shape
    full_len = local_len * tp_count
    own_len = jnp.take(seq_lengths, group)
    local_pos = column * local_len + jnp.arange(local_len, dtype=jnp.int32)
    valid = (local_pos < own_len).astype(F32)[:, None]
    order = to_line if line else (lambda values: values)
    unorder = from_line if line else (lambda values: values)
    bounds = [(0, width // 2), (width // 2, width)] if line else [(0, width)]

    qr = query_down.shape[1]
    latent_rows = query_down.shape[0]
    small_q, small_l = query_gain.shape[0], latent_gain.shape[0]
    used = qr + KR + ROPE
    padded = -(-(used + 3) // LANE) * LANE
    small = jnp.concatenate([query_gain, latent_gain, jnp.zeros((latent_rows,), F32)])
    if small_q + small_l <= latent_rows:
        small = small[:latent_rows]
        extra = 0
    else:
        small = small[: 2 * latent_rows]
        extra = 1
    down_pack = jnp.concatenate(
        [
            query_down.astype(LOW),
            latent_down.astype(LOW),
            attn_gain.astype(LOW)[:, None],
            mlp_gain.astype(LOW)[:, None],
            small.astype(LOW).reshape(1 + extra, latent_rows).T,
            jnp.zeros((latent_rows, padded - used - 3 - extra), LOW),
        ],
        axis=1,
    )

    heads = query_up.shape[1] // QKD
    even = heads + heads % 2
    q_rows, l_rows = query_up.shape[0], latent_up.shape[0]
    o_rows = output_matrix.shape[0] // 2
    half_width = even * VD

    def pad_heads(values, size, to):
        rows = values.shape[0]
        values = values.reshape(rows, heads, size)
        return jnp.pad(values, ((0, 0), (0, even - heads), (0, to - size))).reshape(rows, even * to)

    out_low = pad_heads(output_matrix.astype(LOW), VD, VD)
    qk_pack = jnp.concatenate([pad_heads(query_up.astype(LOW), QKD, LANE), pad_heads(latent_up.astype(LOW), LANE, LANE)], axis=0)
    units = gate_weight.shape[1]
    cut = 768 if units == 1600 else units // 2
    pieces = [(0, cut), (cut, units)]
    if line:
        tiles = []
        for a in range(0, units, UNIT):
            b = min(a + UNIT, units)
            tiles.append([weight[:, a:b].astype(LOW) for weight in (gate_weight, up_weight, down_matrix)])
        tiles[-1].append(jnp.zeros((gate_weight.shape[0], -3 * (units % UNIT) % LANE), LOW))
        mlp_packs = [jnp.concatenate(sum(part, []), axis=1) for part in (tiles[:3], tiles[3:])]
    else:
        mlp_packs = [
            jnp.concatenate(
                [gate_weight[:, a:b].astype(LOW), up_weight[:, a:b].astype(LOW), down_matrix[:, a:b].astype(LOW)], axis=1
            )
            for a, b in pieces
        ]
    places = jnp.arange(fsdp_count, dtype=jnp.int32)
    cot_source = jnp.sum(jnp.where(dealt_order[None, :] == places[:, None], places[None, :], 0), axis=1, dtype=jnp.int32)
    if line:
        owners = jnp.arange(fsdp_count * tp_count, dtype=jnp.int32)[:, None]
        spot = jnp.concatenate(
            [
                (owners * latent_rows + jnp.arange(small_q, dtype=jnp.int32)).reshape(-1),
                (owners * latent_rows + small_q + jnp.arange(small_l, dtype=jnp.int32)).reshape(-1),
            ]
        )
        block = width // LINE
        index = spot // block
        spot = ((index % 2) != group % 2) * (width // 2) + index // 2 * block + spot % block
        own_tables = head_tables(*rotary_tables(local_pos))
        downs, natural, out_slabs, own_cot, normed_low, latents, gain_rows, latent_all, mlp_cot, above, below, block_low = bring(
            cot_source,
            own_len[None],
            down_pack,
            qk_pack,
            out_low,
            out_cotangent[0],
            block_input[0],
            spot[None],
            own_tables,
            mlp_packs[0],
        )
        first_steps = [above, below, gather_two(above, below)]
        down_all = downs.reshape(width, padded)
        grad_out = own_cot
        out_slabs = [slab.reshape(width // 2, half_width) for slab in out_slabs]
        first_low = mlp_packs[0]
        gain_attn, gain_mlp = gain_rows[0], gain_rows[1]
        smalls = gain_rows[2].reshape(2, 4, -1)
        smalls = jnp.stack(by_core(smalls[0], smalls[1]), axis=1).reshape(-1, latent_rows)
        natural = natural.reshape(fsdp_count, q_rows + l_rows, -1)
    else:
        down_all = lax.all_gather(down_pack, ("fsdp", "tp"), axis=0, tiled=True)
        natural = lax.all_gather(qk_pack, "fsdp")
        out_slabs = [lax.all_gather(out_low, "fsdp", axis=0, tiled=True)]
        mlp_slabs = [[lax.all_gather(pack, "fsdp", axis=0, tiled=True)] for pack in mlp_packs]
        grad_out = valid * deal_plain(out_cotangent[0], cot_source).astype(F32)
        mlp_cot = lax.all_gather((RESIDUAL_SCALE * grad_out).astype(LOW), "tp", axis=0, tiled=True)
        gain_attn = down_all[:, used].astype(F32)
        gain_mlp = down_all[:, used + 1].astype(F32)
        smalls = down_all[:, used + 2 : used + 3 + extra].astype(F32).reshape(-1, latent_rows, 1 + extra)
        smalls = jnp.swapaxes(smalls, 1, 2).reshape(-1, latent_rows * (1 + extra))
        block_low = block_input[0]
    w_qup = natural[:, :q_rows].reshape(-1, even * LANE)
    w_kvup = natural[:, q_rows:].reshape(-1, even * LANE)
    w_down = down_all[:, :used]
    gain_query = smalls[:, :small_q].reshape(-1)
    gain_latent = smalls[:, small_q : small_q + small_l].reshape(-1)

    block_vals = block_low.astype(F32)
    cos_local, sin_local = rotary_tables(local_pos)
    cos_local = jnp.concatenate([cos_local, cos_local], axis=1)
    sin_local = jnp.concatenate([sin_local, sin_local], axis=1)
    if not line:
        normed_low = normalize(block_vals, gain_attn)[0].astype(LOW)
        latents = dot(normed_low, w_down)
        rope_raw = latents[:, qr + KR :]
        rotary_key = rope_raw * cos_local + turn_half(rope_raw) * sin_local
        rotary_key = jnp.pad(rotary_key, ((0, 0), (NOPE, LANE - NOPE - ROPE)))
        parts = [
            normalize(latents[:, :qr], gain_query)[0],
            normalize(latents[:, qr : qr + KR], gain_latent)[0],
            rotary_key,
        ]
        latent_all = lax.all_gather(jnp.concatenate(parts, axis=1).astype(LOW), "tp", axis=0, tiled=True)
    query_latent, kv_latent = latents[:, :qr], latents[:, qr : qr + KR]

    def factor_of(values):
        return lax.rsqrt(jnp.mean(values * values, axis=-1, keepdims=True) + EPSILON)

    query_all = latent_all[:, :qr]
    comp_all = latent_all[:, qr : qr + KR]
    rope_all = latent_all[:, qr + KR :]

    tables = head_tables(*rotary_tables(jnp.arange(full_len, dtype=jnp.int32)))
    bias = jnp.where(jnp.arange(full_len, dtype=jnp.int32) < own_len, 0.0, MASKED).astype(F32)[None, :]
    queries, key_value, mixed, lse = attend(latent_all, natural, q_rows, bias, tables)
    if line:
        mixed, first_steps[2], second_low = tie(mixed, first_steps[2], mlp_packs[1])
        second_steps = list(gather_one(second_low))
        first_steps.append(gather_three(first_steps[2]))
    after_attn, mlp_in = enter_mlp(mixed, out_slabs, block_low, gain_mlp)
    if line:
        mlp_in, *second_steps = tie(mlp_in, *second_steps)
        second_steps.append(gather_two(*second_steps))
    mlp_in = gather_tp(mlp_in, "gather_normed", 4)
    if line:
        mlp_in, first_steps[3], second_steps[2] = tie(mlp_in, first_steps[3], second_steps[2])
        second_steps.append(gather_three(second_steps[2]))
        own = assemble(first_low, *first_steps)
        mlp_slabs = [[own.reshape(width // 2, -1), swap_cores(own).reshape(width // 2, -1)]]

    def split(values):
        return values.reshape(4, -1, values.shape[-1])

    def branch_sum(parts):
        return jnp.concatenate(
            [lax.psum_scatter(piece, "tp", scatter_dimension=0, tiled=True).astype(F32) for piece in parts], axis=1
        )

    def finish(branch):
        return unorder((valid * (after_attn + RESIDUAL_SCALE * branch)).astype(LOW))

    if line:
        first_acts, first_grads = units_tiles(mlp_in, mlp_cot, mlp_slabs[0])
        own, other, second_steps[3] = tie(*first_grads, second_steps[3])
        slab = assemble(second_low, *second_steps)
        mlp_slabs.append([slab.reshape(width // 2, -1), swap_cores(slab).reshape(width // 2, -1)])
        first_total = line_sum(split(plus(own, swap_cores(other))))
        second_acts, second_grads = units_tiles(mlp_in, mlp_cot, mlp_slabs[1])
        second_acts, own, other = tie(second_acts, *second_grads)
        swapped = swap_cores(other)
        back_low, ff_low = [], []
        for k, pair in enumerate(zip(*mlp_slabs)):
            back, *ff_low = close_tiles([first_acts, second_acts], list(pair), k * (width // 2 // UNIT), ff_low)
            back_low.append(back)
        second_part = split(plus(own, swapped))
        *back_low, first_total, second_part = tie(*back_low, first_total, second_part)
        second_total = line_sum(second_part)
    else:
        mlp_grads = []
        back, branch = 0.0, 0.0
        for (a, b), (slab,) in zip(pieces, mlp_slabs):
            size = b - a
            gate, up = dot(mlp_in, slab[:, :size]), dot(mlp_in, slab[:, size : 2 * size])
            sigma = jax.nn.sigmoid(gate)
            activated = (gate * sigma * up).astype(LOW)
            grad_act = dot(mlp_cot, slab[:, 2 * size :])
            gate_cot = (grad_act * up * sigma * (1.0 + gate * (1.0 - sigma))).astype(LOW)
            up_cot = (grad_act * gate * sigma).astype(LOW)
            back += dot_nt(gate_cot, slab[:, :size]) + dot_nt(up_cot, slab[:, size : 2 * size])
            branch += dot_nt(activated, slab[:, 2 * size :])
            grads = [dot_tn(mlp_in, gate_cot), dot_tn(mlp_in, up_cot), dot_tn(mlp_cot, activated)]
            mlp_grads.append(jnp.concatenate([grad.astype(LOW) for grad in grads], axis=1))
        back_low = [back.astype(LOW)]
        ff_low = [branch.astype(LOW)]
    grad_after, mlp_gain_grad, attn_cot = leave_mlp(back_low, after_attn, grad_out, gain_mlp)
    attn_cot = gather_tp(attn_cot, "gather_cot", 5)
    if line:
        attn_cot, first_total, second_total, *ff_low = tie(attn_cot, first_total.astype(F32), second_total, *ff_low)
        ff_sum = branch_sum(ff_low)
    else:
        mlp_sums = [lax.psum_scatter(grads, "fsdp", scatter_dimension=0, tiled=True).astype(F32) for grads in mlp_grads]
        block_output = deal_plain(finish(branch_sum(ff_low)), dealt_order)

    grad_mixed = 0.0
    for (a, b), slab in zip(bounds, out_slabs):
        grad_mixed += dot(attn_cot[:, a:b], slab)
    out_grads = [rowwise(dot_tn(attn_cot[:, a:b], mixed).astype(LOW)) for a, b in bounds]
    if line:
        out_part = split(plus(out_grads[0], swap_cores(out_grads[1])))
    query_cot, kv_cot, grad_rope_all = attend_back(
        queries, key_value, rope_all, bias, tables, mixed, grad_mixed.astype(LOW), lse
    )
    if line:
        query_cot, kv_cot, out_part, second_total, ff_sum = tie(
            query_cot, kv_cot, out_part, second_total.astype(F32), ff_sum
        )
        out_sum = line_sum(out_part)
        own_output = finish(ff_sum)
        down_sum, head_sum, block_output, input_grad, gain_sums = finish_all(
            dealt_order,
            (query_cot, kv_cot),
            grad_rope_all,
            natural,
            q_rows,
            latent_all,
            latents,
            jnp.concatenate([gain_query, gain_latent])[None],
            own_tables,
            block_low,
            normed_low,
            downs.reshape(2, width // 2, padded),
            gain_attn[None],
            grad_after,
            mlp_gain_grad[None],
            own_output,
        )
        out_sum, gain_sums = tie(out_sum, gain_sums)
        out_sum = out_sum.astype(F32)
        owner = group * tp_count + column
        spots = ((0, group % 2 * (width // 2) + (group // 2 * tp_count + column) * latent_rows, latent_rows),)
        spots += ((1, spots[0][1], latent_rows), (2, owner * small_q, small_q), (2, qr + owner * small_l, small_l))
        attn_gain_sum, mlp_gain_sum, query_gain_sum, latent_gain_sum = [
            lax.dynamic_slice(gain_sums, (row, at), (1, count))[0] for row, at, count in spots
        ]
    else:
        back_latents = jnp.concatenate(
            [dot_nt(query_cot, w_qup), dot_nt(kv_cot, w_kvup), grad_rope_all], axis=1
        ).astype(LOW)
        grad_latents = lax.psum_scatter(back_latents, "tp", scatter_dimension=0, tiled=True).astype(F32)
        qup_grad = dot_tn(query_all, query_cot).astype(LOW).reshape(fsdp_count, q_rows, even * LANE)
        kvup_grad = dot_tn(comp_all, kv_cot).astype(LOW).reshape(fsdp_count, l_rows, even * LANE)
        head_grads = jnp.concatenate([qup_grad, kvup_grad], axis=1)
        head_sum = lax.psum_scatter(head_grads, "fsdp", scatter_dimension=0, tiled=False).astype(F32)
        out_sum = lax.psum_scatter(out_grads[0], "fsdp", scatter_dimension=0, tiled=True).astype(F32)

    def drop_heads(values, size, to):
        return values.reshape(values.shape[0], even, to)[:, :heads, :size].reshape(values.shape[0], heads * size)

    if not line:
        grad_query_latent, query_gain_grad = norm_back(
            query_latent, factor_of(query_latent), gain_query, grad_latents[:, :qr]
        )
        grad_kv_latent, latent_gain_grad = norm_back(
            kv_latent, factor_of(kv_latent), gain_latent, grad_latents[:, qr : qr + KR]
        )
        grad_rope = grad_latents[:, qr + KR + NOPE : qr + KR + NOPE + ROPE]
        grad_rope = grad_rope * cos_local - turn_half(grad_rope) * sin_local
        latent_cot = jnp.concatenate([grad_query_latent, grad_kv_latent, grad_rope], axis=1).astype(LOW)
        grad_normed = dot_nt(latent_cot, w_down)
        extra_input, attn_gain_grad = norm_back(block_vals, factor_of(block_vals), gain_attn, grad_normed)
        input_grad = (grad_after + extra_input).astype(LOW)

    if line:
        first_cuts = [first_total[:, a : a + UNIT] for a in range(0, first_total.shape[1], UNIT)]
        full = second_total.shape[1] // (3 * UNIT) * 3 * UNIT
        second_cuts = [second_total[:, a : a + UNIT] for a in range(0, full, UNIT)]
        second_cuts += [second_total[:, full + i * REST : full + (i + 1) * REST] for i in range(3)]
        gate_grad, up_grad, down_grad = [
            jnp.concatenate(first_cuts[i::3] + second_cuts[i::3], axis=1) for i in range(3)
        ]
    else:
        down_sum = lax.psum_scatter(
            dot_tn(normed_low, latent_cot), ("fsdp", "tp"), scatter_dimension=0, tiled=True
        )
        gains = jnp.concatenate(
            [
                values.reshape(fsdp_count * tp_count, -1)
                for values in (attn_gain_grad, mlp_gain_grad, query_gain_grad, latent_gain_grad)
            ],
            axis=1,
        )
        gain_sum = lax.psum_scatter(gains, ("fsdp", "tp"), scatter_dimension=0, tiled=True)[0]
        attn_gain_sum, mlp_gain_sum, query_gain_sum, latent_gain_sum = jnp.split(
            gain_sum, [latent_rows, 2 * latent_rows, 2 * latent_rows + small_q]
        )
        sizes = [b - a for a, b in pieces]
        gate_grad, up_grad, down_grad = [
            jnp.concatenate([total[:, i * size : (i + 1) * size] for total, size in zip(mlp_sums, sizes)], axis=1)
            for i in range(3)
        ]
    query_up_grad = drop_heads(head_sum[:q_rows], QKD, LANE)
    latent_up_grad = drop_heads(head_sum[q_rows:], LANE, LANE)
    out_weight_grad = drop_heads(out_sum, VD, VD)

    return (
        block_output[None],
        input_grad[None],
        attn_gain_sum,
        down_sum[:, :qr],
        query_gain_sum,
        down_sum[:, qr:used],
        latent_gain_sum,
        query_up_grad,
        latent_up_grad,
        out_weight_grad,
        mlp_gain_sum,
        gate_grad,
        up_grad,
        down_grad,
    )


def solution(mesh):
    both = P(("fsdp", "tp"))
    rows = P(("fsdp", "tp"), None)
    grid = P("fsdp", "tp")
    tokens = P("fsdp", "tp", None)
    return jax.shard_map(
        per_device,
        mesh=mesh,
        in_specs=(tokens, P(), P(), tokens, both, rows, both, rows, both, grid, grid, grid, both, grid, grid, grid),
        out_specs=(tokens, tokens, both, rows, both, rows, both, grid, grid, grid, both, grid, grid, grid),
        check_vma=False,
    )
```
